256 devices in a mesh: alpha: 16 (over y_hi, x, core), beta: 16 (over y_lo, z).
Axes of the slice: x: 4, y: 4 (y_hi: 2, y_lo: 2; y = y_hi * 2 + y_lo), z: 8, core: 2. Of those that a mesh axis runs over, the one named last changes fastest.
Arguments:
- coeffs: float32 [8192, 8192], P('alpha', 'beta'), may hold values from -6 to 6
- diag_alpha: float32 [8192], P('alpha'), may hold values from 0.5 to 2
- diag_beta: float32 [8192], P('beta'), may hold values from 0.5 to 2
- alpha_tiles: float32 [32, 8, 256, 256], P('alpha'), may hold values from -0.375 to 0.375
- beta_hamiltonian_tiles: float32 [32, 8, 256, 256], P('beta'), may hold values from -0.375 to 0.375
- alpha_source: int32 [32, 8], replicated, may hold values from 0 to 31, as said below
- alpha_live: int32 [32, 8], replicated, may hold values from 0 to 1, as said below
- beta_source_block: int32 [32, 8], replicated, may hold values from 0 to 31, as said below
- beta_live: int32 [32, 8], replicated, may hold values from 0 to 1, as said below
Outputs:
- sigma: float32 [8192, 8192], P('alpha', 'beta')
The draws below stay inside these ranges and needn't reach their ends.
Inputs may be any that keep to these rules, and one draw needn't show every extreme that they name: `beta_source_block`: target blocks are grouped by device: the 32 / 16 consecutive target blocks of one beta index ask, over all their slots, exactly (32 // 16 * 8) // 16 source blocks (counted with repetition) of every beta index, where beta index k holds blocks k * (32 // 16) onward. `alpha_source`: likewise for alpha: the 2 consecutive target blocks of one alpha index ask, over all their slots, exactly 2 * 8 // 16 source blocks of every alpha index. `beta_live`: in each target block the live slots come first, and slot 0 is live. `alpha_live`: in each target block the live slots come first, and slot 0 is live.
All inputs are finite; a program needn't handle non-finite values.
Results may differ from the reference program's by a relative error of at most 0.0003.
Values sent between devices are 32-bit elements; how exact they have to be, the bound alone decides.
No kernel may reach another device: no remote copies, remote signals or barrier semaphores. Data moves between devices by JAX's collectives and lax.ppermute only.
A program may use at most 128 MiB of HBM per device.

```python
import jax
import jax.numpy as jnp
from jax import lax

BS = 256
NCPL = 8
NB = 8192
NA = 8192
NAB = 32
NBB = 32
N_ALPHA = 16
N_BETA = 16


def coupling_table(key, block_total, devices):
    blocks_dev = block_total // devices
    requests = blocks_dev * NCPL
    processor_random_keys = jax.random.split(key, devices)

    def per_device(device_key):
        perm_key, inner_key = jax.random.split(device_key)
        owners = jax.random.permutation(perm_key, requests) % devices
        inner_identifiers = jax.random.randint(inner_key, (requests,), 0, blocks_dev)
        return owners * blocks_dev + inner_identifiers
    coupled = jax.vmap(per_device)(processor_random_keys)
    return coupled.reshape(block_total, NCPL).astype(jnp.int32)


def live_table(key, block_total):
    counts_live = jax.random.randint(key, (block_total,), 1, NCPL + 1)
    slot_ids = jnp.arange(NCPL)
    return (slot_ids[None, :] < counts_live[:, None]).astype(jnp.int32)


def draw_alpha_source(key, part):
    return coupling_table(jax.random.fold_in(key, 11), NA // BS, N_ALPHA)


def draw_beta_source_block(key, part):
    return coupling_table(jax.random.fold_in(key, 23), NB // BS, N_BETA)


def draw_alpha_live(key, part):
    return live_table(jax.random.fold_in(key, 37), NA // BS)


def draw_beta_live(key, part):
    return live_table(jax.random.fold_in(key, 41), NB // BS)


def levels(stream_key, dims, shards, low, top_value):
    loudness = 1.0
    for axis_at, shards_of in shards:
        steps = jax.random.uniform(jax.random.fold_in(jax.random.fold_in(stream_key, 6), axis_at), (shards_of,), jnp.float32, low / len(shards), top_value / len(shards))
        loudness = loudness * jnp.repeat(jnp.exp(steps), dims[axis_at] // shards_of).reshape((-1,) + (1,) * (len(dims) - 1 - axis_at))
    return loudness


def normal_values(stream_key, dims, spread, most, cuts=(), dtype=jnp.bfloat16):
    array = jax.random.normal(stream_key, dims, jnp.float32) * spread
    if len(cuts) > 0:
        array = levels(stream_key, dims, cuts, -0.22, 0.18) * array
    return jnp.clip(array, min=-most, max=most).astype(dtype)


def setup_inputs(seed: int = 0) -> dict:
    key_of = jax.random.split(jax.random.key(seed), 10)
    return {
        "coeffs": normal_values(key_of[0], (NA, NB), 1.0, 6.0, ((0, 16), (1, 16)), jnp.float32),
        "diag_alpha": jnp.clip(0.5 + 1.5 * jax.random.uniform(key_of[1], (NA,), jnp.float32) ** levels(key_of[1], (NA,), ((0, 16),), -0.2, 0.2), 0.5, 2.0),
        "diag_beta": jnp.clip(0.5 + 1.5 * jax.random.uniform(key_of[2], (NB,), jnp.float32) ** levels(key_of[2], (NB,), ((0, 16),), -0.2, 0.2), 0.5, 2.0),
        "alpha_tiles": normal_values(key_of[3], (NAB, NCPL, BS, BS), BS ** -0.5, 0.375, ((0, 16),), jnp.float32),
        "beta_hamiltonian_tiles": normal_values(key_of[4], (NBB, NCPL, BS, BS), BS ** -0.5, 0.375, ((0, 16),), jnp.float32),
        "alpha_source": draw_alpha_source(jax.random.fold_in(key_of[9], 71), 0),
        "alpha_live": draw_alpha_live(jax.random.fold_in(key_of[9], 71), 0),
        "beta_source_block": draw_beta_source_block(jax.random.fold_in(key_of[9], 71), 0),
        "beta_live": draw_beta_live(jax.random.fold_in(key_of[9], 71), 0),
    }


def beta_pass(coeffs, beta_hamiltonian_tiles, beta_source_block, beta_live):
    rows_all = coeffs.shape[0]
    block_size = beta_hamiltonian_tiles.shape[2]
    block_total = beta_hamiltonian_tiles.shape[0]
    blocks = coeffs.reshape(rows_all, block_total, block_size)

    def one_target(packed):
        tile_set, sources, flags = packed
        picked = jnp.take(blocks, sources.astype(jnp.int32), axis=1)
        masked = tile_set * flags.astype(jnp.float32)[:, None, None]
        return jnp.einsum("acb,cbd->ad", picked, masked, precision=lax.Precision.HIGHEST)

    sigma_output = lax.map(one_target, (beta_hamiltonian_tiles, beta_source_block, beta_live))
    return jnp.transpose(sigma_output, (1, 0, 2)).reshape(rows_all, block_total * block_size)


def alpha_pass(coeffs, alpha_tiles, alpha_source, alpha_live):
    cols_all = coeffs.shape[1]
    block_size = alpha_tiles.shape[2]
    block_total = alpha_tiles.shape[0]
    blocks = coeffs.reshape(block_total, block_size, cols_all)

    def one_target(packed):
        tile_set, sources, flags = packed
        picked = jnp.take(blocks, sources.astype(jnp.int32), axis=0)
        masked = tile_set * flags.astype(jnp.float32)[:, None, None]
        return jnp.einsum("cab,cbd->ad", masked, picked, precision=lax.Precision.HIGHEST)

    sigma_output = lax.map(one_target, (alpha_tiles, alpha_source, alpha_live))
    return sigma_output.reshape(block_total * block_size, cols_all)


def reference(coeffs, diag_alpha, diag_beta, alpha_tiles, beta_hamiltonian_tiles, alpha_source, alpha_live, beta_source_block, beta_live):
    beta_term = beta_pass(coeffs, beta_hamiltonian_tiles, beta_source_block, beta_live)
    alpha_term = alpha_pass(coeffs, alpha_tiles, alpha_source, alpha_live)
    diagonal = diag_alpha[:, None] + diag_beta[None, :]
    return diagonal * coeffs + beta_term + alpha_term
```

```python
import functools

import jax
import jax.numpy as jnp
from jax import lax
from jax.experimental import pallas as pl
from jax.experimental.pallas import tpu as pltpu
from jax.sharding import Mesh
from jax.sharding import PartitionSpec as P

AXES = ("yhi", "x", "core", "ylo", "z")
SIZES = (2, 4, 2, 2, 8)
ALPHA = ("yhi", "x", "core")
BETA = ("ylo", "z")
BS = 256


def shift(value, axis, step):
    n = lax.axis_size(axis)
    return lax.ppermute(value, axis, [(i, (i + step) % n) for i in range(n)])


def dot3(a, b):
    a_hi = a.astype(jnp.bfloat16)
    b_hi = b.astype(jnp.bfloat16)
    a_lo = (a - a_hi.astype(jnp.float32)).astype(jnp.bfloat16)
    b_lo = (b - b_hi.astype(jnp.float32)).astype(jnp.bfloat16)
    dot = functools.partial(jnp.dot, preferred_element_type=jnp.float32)
    return dot(a_hi, b_hi) + (dot(a_hi, b_lo) + dot(a_lo, b_hi))


def alpha_kernel(
    where, source, live, u0, uf, ub, u2a, u2b, v0, vf, vb, v2a, v2b, own, sib, out, data, tiles, sem
):
    copies = []
    for y, (a, f, b, la, lb) in enumerate(((u0, uf, ub, u2a, u2b), (v0, vf, vb, v2a, v2b))):
        copies += [
            (a, data.at[y, 0]),
            (f, data.at[y, 3]),
            (b, data.at[y, 1]),
            (la, data.at[y, 2, 0]),
            (lb, data.at[y, 2, 1]),
        ]
    copies += [(own, tiles.at[0]), (sib, tiles.at[1])]
    copies = [pltpu.make_async_copy(s, d, sem.at[i]) for i, (s, d) in enumerate(copies)]
    for copy in copies:
        copy.start()
    out[...] = jnp.zeros_like(out)
    me = where[0]
    for copy in copies:
        copy.wait()
    for target in range(2):
        for block in range(2):

            def slot(c, _, target=target, block=block):
                row = 2 * (me ^ target) + block

                @pl.when(live[row, c] > 0)
                def _():
                    src = source[row, c]
                    owner = src >> 1
                    y = (owner >> 3) ^ (me >> 3)
                    x = ((owner >> 1) - (me >> 1)) & 3
                    core = (owner & 1) ^ (me & 1)
                    first = pl.multiple_of((src & 1) * BS, BS)
                    rows = data[y, x, core, pl.ds(first, BS), :]
                    out[target, block * BS : (block + 1) * BS, :] += dot3(
                        tiles[target, block, c], rows
                    )

                return 0

            lax.fori_loop(0, 8, slot, 0)


def beta_kernel(
    where, source, live, ring, p0, f1, b1, f2, b2, f3, b3, f4, b4, own, par, out, data, tiles, sem
):
    me = where[1]
    z = me & 7
    half = p0.shape[0] // 2
    copies = [(ring, data.at[0]), (p0, data.at[1, z])]
    for k, (f, b) in enumerate(((f1, b1), (f2, b2), (f3, b3)), 1):
        copies += [(f, data.at[1, (z - k) & 7]), (b, data.at[1, (z + k) & 7])]
    copies += [
        (f4, data.at[1, (z + 4) & 7, pl.ds(0, half)]),
        (b4, data.at[1, (z + 4) & 7, pl.ds(half, half)]),
        (own, tiles.at[0]),
        (par, tiles.at[1]),
    ]
    copies = [pltpu.make_async_copy(s, d, sem.at[i]) for i, (s, d) in enumerate(copies)]
    for copy in copies:
        copy.start()
    out[...] = jnp.zeros_like(out)
    for copy in copies:
        copy.wait()
    for target in range(2):
        for block in range(2):

            def slot(c, _, target=target, block=block):
                row = 2 * (me ^ (8 * target)) + block

                @pl.when(live[row, c] > 0)
                def _():
                    src = source[row, c]
                    owner = src >> 1
                    y = (owner >> 3) ^ (me >> 3)
                    first = pl.multiple_of((src & 1) * BS, BS)
                    columns = data[y, owner & 7, :, pl.ds(first, BS)]
                    out[target, :, block * BS : (block + 1) * BS] += dot3(
                        columns, tiles[target, block, c]
                    )

                return 0

            lax.fori_loop(0, 8, slot, 0)


def last_kernel(where, x, da, db, alpha, alpha_other, beta, beta_other, out):
    core = where[0] & 1
    ylo = where[1] >> 3
    out[...] = (da[...] + db[...]) * x[...]

    def columns(first, part):
        out[:, first : first + BS] += part[...]

    def rows(first, part):
        out[first : first + BS, :] += part[...]

    for side in range(2):

        @pl.when(core == side)
        def _(side=side):
            columns(side * BS, alpha)
            columns((1 - side) * BS, alpha_other)

        @pl.when(ylo == side)
        def _(side=side):
            rows(side * BS, beta)
            rows((1 - side) * BS, beta_other)


SMEM = pl.BlockSpec(memory_space=pltpu.SMEM)
ANY = pl.BlockSpec(memory_space=pl.ANY)
VMEM = pl.BlockSpec(memory_space=pltpu.VMEM)
MIB = 1 << 20


def per_device(
    coeffs,
    diag_alpha,
    diag_beta,
    alpha_tiles,
    beta_tiles,
    alpha_source,
    alpha_live,
    beta_source,
    beta_live,
):
    n = coeffs.shape[0]
    core = lax.axis_index("core")
    ylo = lax.axis_index("ylo")
    where = jnp.stack([lax.axis_index(ALPHA), lax.axis_index(BETA)]).astype(jnp.int32)

    keep = lax.dynamic_slice_in_dim(coeffs, ylo * BS, BS, 0)
    give = lax.dynamic_slice_in_dim(coeffs, (1 - ylo) * BS, BS, 0)
    ring = lax.all_gather(keep, "z")
    p0 = shift(give, "ylo", 1)
    f1, b1 = shift(p0, "z", 1), shift(p0, "z", -1)
    f2, b2 = shift(f1, "z", 1), shift(b1, "z", -1)
    f3, b3 = shift(f2, "z", 1), shift(b2, "z", -1)
    f4, b4 = shift(f3[: BS // 2], "z", 1), shift(b3[BS // 2 :], "z", -1)
    mine = lax.dynamic_index_in_dim(beta_tiles, core, 0, keepdims=False)
    got = shift(mine, "ylo", 1)
    other = shift(got, "core", 1)
    par_tiles = jnp.stack([jnp.where(core == 0, got, other), jnp.where(core == 0, other, got)])

    left = lax.dynamic_slice_in_dim(coeffs, core * BS, BS, 1)
    right = lax.dynamic_slice_in_dim(coeffs, (1 - core) * BS, BS, 1)
    u0 = jnp.stack([left, shift(right, "core", 1)])
    v0 = shift(u0, "yhi", 1)
    gathered = []
    for first in (u0, v0):
        f, b = shift(first, "x", 1), shift(first, "x", -1)
        gathered += [first, f, b, shift(f[0], "x", 1), shift(b[1], "x", -1)]
    sib_tiles = shift(alpha_tiles, "core", 1)

    flops = 2 * 32 * BS**3 * 3
    alpha = pl.pallas_call(
        alpha_kernel,
        out_shape=jax.ShapeDtypeStruct((2, n, BS), jnp.float32),
        in_specs=[SMEM] * 3 + [ANY] * 12,
        out_specs=VMEM,
        scratch_shapes=[
            pltpu.VMEM((2, 4, 2, n, BS), jnp.float32),
            pltpu.VMEM((2, 2, 8, BS, BS), jnp.float32),
            pltpu.SemaphoreType.DMA((12,)),
        ],
        compiler_params=pltpu.CompilerParams(vmem_limit_bytes=32 * MIB),
        cost_estimate=pl.CostEstimate(flops=flops, bytes_accessed=17 * MIB, transcendentals=0),
        name="alpha",
    )(where, alpha_source, alpha_live, *gathered, alpha_tiles, sib_tiles)
    alpha_other = shift(alpha[1], "core", 1)

    beta = pl.pallas_call(
        beta_kernel,
        out_shape=jax.ShapeDtypeStruct((2, BS, n), jnp.float32),
        in_specs=[SMEM] * 3 + [ANY] * 12,
        out_specs=VMEM,
        scratch_shapes=[
            pltpu.VMEM((2, 8, BS, n), jnp.float32),
            pltpu.VMEM((2, 2, 8, BS, BS), jnp.float32),
            pltpu.SemaphoreType.DMA((12,)),
        ],
        compiler_params=pltpu.CompilerParams(vmem_limit_bytes=32 * MIB),
        cost_estimate=pl.CostEstimate(flops=flops, bytes_accessed=17 * MIB, transcendentals=0),
        name="beta",
    )(where, beta_source, beta_live, ring, p0, f1, b1, f2, b2, f3, b3, f4, b4, beta_tiles, par_tiles)
    beta_other = shift(beta[1], "ylo", 1)

    return pl.pallas_call(
        last_kernel,
        out_shape=jax.ShapeDtypeStruct((n, n), jnp.float32),
        in_specs=[SMEM] + [VMEM] * 7,
        out_specs=VMEM,
        cost_estimate=pl.CostEstimate(flops=4 * n * n, bytes_accessed=5 * MIB, transcendentals=0),
        name="last",
    )(where, coeffs, diag_alpha[:, None], diag_beta[None, :], alpha[0], alpha_other, beta[0], beta_other)


def solution(mesh):
    parts = Mesh(mesh.devices.reshape(SIZES), AXES)
    return jax.shard_map(
        per_device,
        mesh=parts,
        in_specs=(
            P(ALPHA, BETA),
            P(ALPHA),
            P(BETA),
            P(ALPHA, None, None, None),
            P(BETA, None, None, None),
            P(),
            P(),
            P(),
            P(),
        ),
        out_specs=P(ALPHA, BETA),
        check_vma=False,
    )
```

```python
import functools

import jax
import jax.numpy as jnp
from jax import lax
from jax.experimental import pallas as pl
from jax.experimental.pallas import tpu as pltpu
from jax.sharding import Mesh
from jax.sharding import PartitionSpec as P

AXES = ("yhi", "x", "core", "ylo", "z")
SIZES = (2, 4, 2, 2, 8)
ALPHA = ("yhi", "x", "core")
BETA = ("ylo", "z")
BS = 256
SLOTS = 8
MIB = 1 << 20

SMEM = pl.BlockSpec(memory_space=pltpu.SMEM)
HBM = pl.BlockSpec(memory_space=pltpu.HBM)
VMEM = pl.BlockSpec(memory_space=pltpu.VMEM)


def swap(value, axis):
    return lax.ppermute(value, axis, [(0, 1), (1, 0)])


def step(value, axis):
    n = lax.axis_size(axis)
    if axis == "z":
        pairs = [(i, (i + 1) % n) for i in range(n)]
        pairs += [(n + i, n + (i - 1) % n) for i in range(n)]
        return lax.ppermute(value, ("core", axis), pairs)
    pairs = [(2 * i, 2 * ((i + 1) % n)) for i in range(n)]
    pairs += [(2 * i + 1, 2 * ((i - 1) % n) + 1) for i in range(n)]
    return lax.ppermute(value, (axis, "core"), pairs)


def after(value, *earlier):
    return lax.optimization_barrier((value, *earlier))[0]


def dot3(a, b):
    a_hi = a.astype(jnp.bfloat16)
    b_hi = b.astype(jnp.bfloat16)
    a_lo = (a - a_hi.astype(jnp.float32)).astype(jnp.bfloat16)
    b_lo = (b - b_hi.astype(jnp.float32)).astype(jnp.bfloat16)
    dot = functools.partial(jnp.dot, preferred_element_type=jnp.float32)
    return dot(a_hi, b_hi) + (dot(a_hi, b_lo) + dot(a_lo, b_hi))


def each_slot(body):
    for target in range(2):
        for block in range(2):
            lax.fori_loop(
                0, SLOTS, lambda c, _, t=target, b=block: (body(t, b, c), 0)[1], 0
            )


def alpha_kernel(side, where, source, live, *refs):
    arrived, (own, sib), refs = refs[:4], refs[4:6], refs[6:]
    before, refs = (refs[:2], refs[2:]) if side else ((), refs)
    outs, (data, tiles, data_sem, tile_sem, out_sem) = refs[:2], refs[2:]
    me = where[0]

    def copy_of(d):
        return pltpu.make_async_copy(arrived[d], data.at[d], data_sem.at[d])

    def tile_of(target, block, c):
        index = (target * 2 + block) * SLOTS + c
        return pltpu.make_async_copy(
            (own, sib)[target].at[block, c], tiles.at[index], tile_sem.at[index]
        )

    def when_mine(target, block, c, body):
        row = 2 * (me ^ target) + block
        src = source[row, c]
        owner = src >> 1
        mine = (live[row, c] > 0) & (((owner >> 3) ^ (me >> 3)) == side)
        pl.when(mine)(lambda: body(src))

    for d in range(4):
        copy_of(d).start()
    each_slot(
        lambda t, b, c: when_mine(t, b, c, lambda src: tile_of(t, b, c).start())
    )
    for i, out in enumerate(outs):
        if side:
            pltpu.make_async_copy(before[i], out, out_sem.at[i]).start()
        else:
            out[...] = jnp.zeros_like(out)
    for i, out in enumerate(outs):
        if side:
            pltpu.make_async_copy(before[i], out, out_sem.at[i]).wait()
    for d in range(4):
        copy_of(d).wait()

    def product(target, block, c):
        def body(src):
            owner = src >> 1
            ahead = (me >> 1) - (owner >> 1)
            d = jnp.where((me & 1) == 0, ahead, -ahead) & 3
            core = (owner & 1) ^ (me & 1)
            first = pl.multiple_of((src & 1) * BS, BS)
            tile_of(target, block, c).wait()
            rows = data[d, core, pl.ds(first, BS), :]
            tile = tiles[(target * 2 + block) * SLOTS + c]
            outs[target][block * BS : (block + 1) * BS, :] += dot3(tile, rows)

        when_mine(target, block, c, body)

    each_slot(product)


def alpha_call(side, where, source, live, arrived, own, sib, before=()):
    n = own.shape[0] * BS
    return pl.pallas_call(
        functools.partial(alpha_kernel, side),
        out_shape=[jax.ShapeDtypeStruct((n, BS), jnp.float32)] * 2,
        in_specs=[SMEM] * 3 + [HBM] * (6 + len(before)),
        out_specs=[VMEM] * 2,
        scratch_shapes=[
            pltpu.VMEM((4, 2, n, BS), jnp.float32),
            pltpu.VMEM((4 * SLOTS, BS, BS), jnp.float32),
            pltpu.SemaphoreType.DMA((4,)),
            pltpu.SemaphoreType.DMA((4 * SLOTS,)),
            pltpu.SemaphoreType.DMA((2,)),
        ],
        compiler_params=pltpu.CompilerParams(vmem_limit_bytes=20 * MIB),
        cost_estimate=pl.CostEstimate(
            flops=16 * 6 * BS**3, bytes_accessed=8 * MIB, transcendentals=0
        ),
        name=f"alpha{side}",
    )(where, source, live, *arrived, own, sib, *before)


def beta_kernel(steps, done, late, where, source, live, *refs):
    count = steps[0] + steps[1] + 2
    arrived, refs = refs[:count], refs[count:]
    arrived = (arrived[: steps[0] + 1], arrived[steps[0] + 1 :])
    own, refs = refs[0], refs[1:]
    par, refs = refs[: 4 if late else 2], refs[4 if late else 2 :]
    before, refs = (refs[:2], refs[2:]) if done else ((), refs)
    outs, (data, tiles, need, data_sem, tile_sem, out_sem) = refs[:2], refs[2:]
    me, core = where[1], where[0] & 1

    def origin(src):
        owner = src >> 1
        y = (owner >> 3) ^ (me >> 3)
        ahead = me - owner
        return y, jnp.where(core == 0, ahead, -ahead) & 7

    def here(hops, has_late, y, d, target, c):
        if hops is None:
            return False
        ready = jnp.where(y == 0, d <= hops[0], d <= hops[1])
        if target == 1 and not has_late:
            ready = ready & (c < SLOTS // 2)
        return ready

    def when_mine(target, block, c, body):
        row = 2 * (me ^ (8 * target)) + block
        src = source[row, c]
        y, d = origin(src)
        mine = (live[row, c] > 0) & here(steps, late, y, d, target, c)
        if done:
            mine = mine & jnp.logical_not(here(done, False, y, d, target, c))
        pl.when(mine)(lambda: body(src, y, d))

    def copy_of(y, d):
        return pltpu.make_async_copy(arrived[y][d], data.at[y * 8 + d], data_sem.at[y * 8 + d])

    def tile_at(ref, index):
        return pltpu.make_async_copy(ref, tiles.at[index], tile_sem.at[index])

    for i, out in enumerate(outs):
        if done:
            pltpu.make_async_copy(before[i], out, out_sem.at[i]).start()
    for i in range(16):
        need[i] = 0

    def fetch(target, block, c):
        index = (target * 2 + block) * SLOTS + c

        def body(src, y, d):
            need[y * 8 + d] = 1
            if target == 0:
                tile_at(own.at[block, c], index).start()
                return
            for half in range(len(par) // 2):
                for held in range(2):
                    ok = ((core ^ block) == held) & ((c >> 2) == half)

                    @pl.when(ok)
                    def _(half=half, held=held):
                        tile_at(par[2 * half + held].at[c & 3], index).start()

        when_mine(target, block, c, body)

    each_slot(fetch)
    for y in range(2):
        for d in range(steps[y] + 1):
            pl.when(need[y * 8 + d] == 1)(lambda y=y, d=d: copy_of(y, d).start())
    for i, out in enumerate(outs):
        if done:
            pltpu.make_async_copy(before[i], out, out_sem.at[i]).wait()
        else:
            out[...] = jnp.zeros_like(out)

    def product(target, block, c):
        index = (target * 2 + block) * SLOTS + c

        def body(src, y, d):
            place = y * 8 + d

            @pl.when(need[place] == 1)
            def _():
                pltpu.make_async_copy(arrived[0][0], data.at[place], data_sem.at[place]).wait()
                need[place] = 2

            tile_at(own.at[0, 0], index).wait()
            first = pl.multiple_of((src & 1) * BS, BS)
            columns = data[place, :, pl.ds(first, BS)]
            outs[target][:, block * BS : (block + 1) * BS] += dot3(columns, tiles[index])

        when_mine(target, block, c, body)

    each_slot(product)


def beta_call(steps, done, late, where, source, live, chains, own, par, before=()):
    rows, n = chains[0][0].shape
    arrived = chains[0][: steps[0] + 1] + chains[1][: steps[1] + 1]
    return pl.pallas_call(
        functools.partial(beta_kernel, steps, done, late),
        out_shape=[jax.ShapeDtypeStruct((rows, n), jnp.float32)] * 2,
        in_specs=[SMEM] * 3 + [HBM] * (len(arrived) + 1 + len(par) + len(before)),
        out_specs=[VMEM] * 2,
        scratch_shapes=[
            pltpu.VMEM((16, rows, n), jnp.float32),
            pltpu.VMEM((4 * SLOTS, BS, BS), jnp.float32),
            pltpu.SMEM((16,), jnp.int32),
            pltpu.SemaphoreType.DMA((16,)),
            pltpu.SemaphoreType.DMA((4 * SLOTS,)),
            pltpu.SemaphoreType.DMA((2,)),
        ],
        compiler_params=pltpu.CompilerParams(vmem_limit_bytes=24 * MIB),
        cost_estimate=pl.CostEstimate(
            flops=16 * 6 * BS**3, bytes_accessed=8 * MIB, transcendentals=0
        ),
        name=f"beta{len(before) // 2}",
    )(where, source, live, *arrived, own, *par, *before)


def join_kernel(where, x, da, db, alpha, alpha_other, beta, out):
    core = where[0] & 1
    ylo = where[1] >> 3
    out[...] = (da[...] + db[...]) * x[...]
    for side in range(2):

        @pl.when(core == side)
        def _(side=side):
            out[:, side * BS : (side + 1) * BS] += alpha[...]
            out[:, (1 - side) * BS : (2 - side) * BS] += alpha_other[...]

        @pl.when(ylo == side)
        def _(side=side):
            out[side * BS : (side + 1) * BS, :] += beta[...]


def last_kernel(where, joined, beta_other, out, total, part, sems):
    first = pl.multiple_of((1 - (where[1] >> 3)) * BS, BS)
    rows = out.at[pl.ds(first, BS)]
    copies = [
        pltpu.make_async_copy(joined.at[pl.ds(first, BS)], total, sems.at[0]),
        pltpu.make_async_copy(beta_other, part, sems.at[1]),
    ]
    for copy in copies:
        copy.start()
    for copy in copies:
        copy.wait()
    total[...] += part[...]
    back = pltpu.make_async_copy(total, rows, sems.at[2])
    back.start()
    back.wait()


def per_device(
    coeffs,
    diag_alpha,
    diag_beta,
    alpha_tiles,
    beta_tiles,
    alpha_source,
    alpha_live,
    beta_source,
    beta_live,
):
    n = coeffs.shape[0]
    core = lax.axis_index("core")
    ylo = lax.axis_index("ylo")
    where = jnp.stack([lax.axis_index(ALPHA), lax.axis_index(BETA)]).astype(jnp.int32)

    a = [lax.dynamic_slice_in_dim(coeffs, ylo * BS, BS, 0)]
    give = lax.dynamic_slice_in_dim(coeffs, (1 - ylo) * BS, BS, 0)
    b = [swap(give, "ylo")]
    a.append(step(a[0], "z"))
    whole = after(coeffs, a[0], give)
    left = lax.dynamic_slice_in_dim(whole, core * BS, BS, 1)
    right = lax.dynamic_slice_in_dim(whole, (1 - core) * BS, BS, 1)
    u = [jnp.stack([left, swap(right, "core")])]
    v = [swap(u[0], "yhi")]
    sib_tiles = swap(after(alpha_tiles, u[0]), "core")
    mine = lax.dynamic_index_in_dim(beta_tiles, core, 0, keepdims=False)

    u.append(step(u[0], "x"))
    b.append(step(b[0], "z"))
    a.append(step(after(a[1], b[0]), "z"))
    u.append(step(after(u[1], b[0], a[1]), "x"))
    b.append(step(b[1], "z"))
    a.append(step(after(a[2], b[1], u[1], sib_tiles), "z"))
    u.append(step(after(u[2], b[1], a[2]), "x"))
    b.append(step(b[2], "z"))
    a.append(step(after(a[3], b[2], u[2], v[0]), "z"))
    got0 = swap(after(mine[: SLOTS // 2], v[0]), "ylo")
    v.append(step(after(v[0], u[3], b[2], a[3]), "x"))
    b.append(step(b[3], "z"))
    a.append(step(after(a[4], b[3], u[3]), "z"))
    alpha = alpha_call(
        0, where, alpha_source, alpha_live, [after(u[0], a[4]), *u[1:]], alpha_tiles, sib_tiles
    )
    v.append(step(v[1], "x"))
    b.append(step(b[4], "z"))
    a.append(step(after(a[5], b[4], v[1]), "z"))
    oth0 = swap(got0, "core")
    got1 = swap(after(mine[SLOTS // 2 :], got0), "ylo")
    v.append(step(v[2], "x"))
    b.append(step(b[5], "z"))
    a.append(step(after(a[6], b[5], v[2], oth0), "z"))
    own = after(beta_tiles, a[6])
    beta = beta_call(
        (5, 4), None, False, where, beta_source, beta_live, (a, b), own, [got0, oth0]
    )
    oth1 = swap(got1, "core")
    b.append(step(b[6], "z"))
    alpha = alpha_call(
        1, where, alpha_source, alpha_live, [after(v[0], a[7]), *v[1:]], alpha_tiles, sib_tiles, alpha
    )
    alpha_other = swap(alpha[1], "core")
    beta = beta_call(
        (7, 7),
        (5, 4),
        True,
        where,
        beta_source,
        beta_live,
        (a, b),
        own,
        [got0, oth0, got1, oth1],
        beta,
    )
    beta_other = swap(beta[1], "ylo")

    joined = pl.pallas_call(
        join_kernel,
        out_shape=jax.ShapeDtypeStruct((n, n), jnp.float32),
        in_specs=[SMEM] + [VMEM] * 6,
        out_specs=VMEM,
        cost_estimate=pl.CostEstimate(flops=4 * n * n, bytes_accessed=5 * MIB, transcendentals=0),
        name="join",
    )(where, coeffs, diag_alpha[:, None], diag_beta[None, :], alpha[0], alpha_other, beta[0])
    return pl.pallas_call(
        last_kernel,
        out_shape=jax.ShapeDtypeStruct((n, n), jnp.float32),
        in_specs=[SMEM, HBM, HBM],
        out_specs=HBM,
        scratch_shapes=[
            pltpu.VMEM((BS, n), jnp.float32),
            pltpu.VMEM((BS, n), jnp.float32),
            pltpu.SemaphoreType.DMA((3,)),
        ],
        input_output_aliases={1: 0},
        cost_estimate=pl.CostEstimate(flops=n * BS, bytes_accessed=2 * MIB, transcendentals=0),
        name="last",
    )(where, joined, beta_other)


def solution(mesh):
    parts = Mesh(mesh.devices.reshape(SIZES), AXES)
    return jax.shard_map(
        per_device,
        mesh=parts,
        in_specs=(
            P(ALPHA, BETA),
            P(ALPHA),
            P(BETA),
            P(ALPHA, None, None, None),
            P(BETA, None, None, None),
            P(),
            P(),
            P(),
            P(),
        ),
        out_specs=P(ALPHA, BETA),
        check_vma=False,
    )
```

```python
import functools

import jax
import jax.numpy as jnp
from jax import lax
from jax.experimental import pallas as pl
from jax.experimental.pallas import tpu as pltpu
from jax.sharding import Mesh
from jax.sharding import PartitionSpec as P

AXES = ("yhi", "x", "core", "ylo", "z")
SIZES = (2, 4, 2, 2, 8)
ALPHA = ("yhi", "x", "core")
BETA = ("ylo", "z")
BS = 256
SLOTS = 8
MIB = 1 << 20

SMEM = pl.BlockSpec(memory_space=pltpu.SMEM)
HBM = pl.BlockSpec(memory_space=pltpu.HBM)
ANY = pl.BlockSpec(memory_space=pl.ANY)
VMEM = pl.BlockSpec(memory_space=pltpu.VMEM)


def swap(value, axis):
    return lax.ppermute(value, axis, [(0, 1), (1, 0)])


def step(value, axis):
    n = lax.axis_size(axis)
    if axis == "z":
        pairs = [(i, (i + 1) % n) for i in range(n)]
        pairs += [(n + i, n + (i - 1) % n) for i in range(n)]
        return lax.ppermute(value, ("core", axis), pairs)
    pairs = [(2 * i, 2 * ((i + 1) % n)) for i in range(n)]
    pairs += [(2 * i + 1, 2 * ((i - 1) % n) + 1) for i in range(n)]
    return lax.ppermute(value, (axis, "core"), pairs)


def in_hbm(*values):
    return [pltpu.with_memory_space_constraint(value, pltpu.HBM) for value in values]


def after(value, *earlier):
    return lax.optimization_barrier((value, *earlier))[0]


def dot3(a, b):
    a_hi = a.astype(jnp.bfloat16)
    b_hi = b.astype(jnp.bfloat16)
    a_lo = (a - a_hi.astype(jnp.float32)).astype(jnp.bfloat16)
    b_lo = (b - b_hi.astype(jnp.float32)).astype(jnp.bfloat16)
    dot = functools.partial(jnp.dot, preferred_element_type=jnp.float32)
    return dot(a_hi, b_hi) + (dot(a_hi, b_lo) + dot(a_lo, b_hi))


HOPS = ((5, 4), (7, 7))


def plan_kernel(where, alpha_source, alpha_live, beta_source, beta_live, alpha_plan, beta_plan):
    me, mb = where[0], where[1]
    up = (me & 1) == 0
    for row in range(2):
        alpha_plan[row, 0] = 0
    for row in range(4):
        beta_plan[row, 0] = 0

    def put(plan, row, word):
        count = plan[row, 0] + 1
        plan[row, 0] = count
        plan[row, count] = word

    def alpha(slot, _):
        row, c = 2 * me + (slot >> 3), slot & 7

        @pl.when(alpha_live[row, c] > 0)
        def _():
            src = alpha_source[row, c]
            owner = src >> 1
            ahead = (me >> 1) - (owner >> 1)
            hops = jnp.where((owner & 1) == 0, ahead, -ahead) & 3
            piece = 2 * hops + ((owner ^ me) & 1)
            put(alpha_plan, (owner >> 3) ^ (me >> 3), piece * 64 + (src & 1) * 32 + slot)

        return 0

    def beta(target, slot, _):
        row, c = 2 * (mb ^ (8 * target)) + (slot >> 3), slot & 7

        @pl.when(beta_live[row, c] > 0)
        def _():
            src = beta_source[row, c]
            owner = src >> 1
            y = (owner >> 3) ^ (mb >> 3)
            ahead = mb - owner
            d = jnp.where(up, ahead, -ahead) & 7
            early = d <= jnp.where(y == 0, HOPS[0][0], HOPS[0][1])
            if target:
                early = early & (c < SLOTS // 2)
            call = jnp.where(early, 0, 1)
            put(beta_plan, 2 * call + target, (y * 8 + d) * 64 + (src & 1) * 32 + slot)

        return 0

    lax.fori_loop(0, 2 * SLOTS, alpha, 0)
    for target in range(2):
        lax.fori_loop(0, 2 * SLOTS, functools.partial(beta, target), 0)


def start_one_of(pieces, piece, make):
    for i, ref in enumerate(pieces):
        pl.when(piece == i)(lambda ref=ref: make(ref).start())


def alpha_kernel(side, plan, *refs):
    pieces, own, refs = refs[:8], refs[8], refs[9:]
    before, refs = (refs[:1], refs[1:]) if side else ((), refs)
    out, data, tiles, data_sem, tile_sem, out_sem = refs
    count = plan[side, 0]
    if side:
        first = pltpu.make_async_copy(before[0], out, out_sem)
        first.start()

    def tile_of(k, slot):
        return pltpu.make_async_copy(own.at[slot >> 3, slot & 7], tiles.at[k], tile_sem.at[k])

    def rows_of(k, ref, block):
        first = pl.multiple_of(block * BS, BS)
        return pltpu.make_async_copy(ref.at[pl.ds(first, BS)], data.at[k], data_sem.at[k])

    def fetch(k, _):
        word = plan[side, k + 1]
        tile_of(k, word & 31).start()
        start_one_of(pieces, word >> 6, lambda ref: rows_of(k, ref, (word >> 5) & 1))
        return 0

    lax.fori_loop(0, count, fetch, 0)
    if side:
        first.wait()
    else:
        out[...] = jnp.zeros_like(out)

    def product(k, _):
        slot = plan[side, k + 1] & 31
        tile_of(k, slot).wait()
        rows_of(k, pieces[0], 0).wait()
        rows = pl.multiple_of((slot >> 3) * BS, BS)
        out[pl.ds(rows, BS), :] += dot3(tiles[k], data[k])
        return 0

    lax.fori_loop(0, count, product, 0)


def alpha_call(side, plan, pieces, own, before=()):
    n = own.shape[0] * BS
    return pl.pallas_call(
        functools.partial(alpha_kernel, side),
        out_shape=jax.ShapeDtypeStruct((n, n), jnp.float32),
        in_specs=[SMEM] + [HBM] * 9 + [ANY] * len(before),
        out_specs=VMEM,
        scratch_shapes=[
            pltpu.VMEM((SLOTS, BS, n), jnp.float32),
            pltpu.VMEM((SLOTS, BS, BS), jnp.float32),
            pltpu.SemaphoreType.DMA((SLOTS,)),
            pltpu.SemaphoreType.DMA((SLOTS,)),
            pltpu.SemaphoreType.DMA,
        ],
        compiler_params=pltpu.CompilerParams(vmem_limit_bytes=16 * MIB),
        cost_estimate=pl.CostEstimate(
            flops=8 * 12 * BS**3, bytes_accessed=8 * MIB, transcendentals=0
        ),
        name=f"alpha{side}",
    )(plan, *in_hbm(*pieces, own), *before)


def beta_kernel(call, targets, where, plan, *refs):
    hops = HOPS[call]
    numbers = [d for d in range(hops[0] + 1)] + [8 + d for d in range(hops[1] + 1)]
    pieces, refs = dict(zip(numbers, refs)), refs[len(numbers) :]
    own, refs = refs[0], refs[1:]
    par, refs = refs[: 2 * call + 2], refs[2 * call + 2 :]
    before, refs = (refs[: len(targets)], refs[len(targets) :]) if call else ((), refs)
    outs, (data, tiles, data_sem, tile_sem, out_sem) = refs[: len(targets)], refs[len(targets) :]
    core = where[0] & 1
    firsts = [
        pltpu.make_async_copy(b, out, out_sem.at[i]) for i, (b, out) in enumerate(zip(before, outs))
    ]
    for first in firsts:
        first.start()

    def columns_of(k, ref, block):
        first = pl.multiple_of(block * BS, BS)
        return pltpu.make_async_copy(ref.at[:, pl.ds(first, BS)], data.at[k], data_sem.at[k])

    def tile_from(k, ref):
        return pltpu.make_async_copy(ref, tiles.at[k], tile_sem.at[k])

    base = 0
    for target in targets:
        row = 2 * call + target

        def fetch(j, _, target=target, row=row, base=base):
            word = plan[row, j + 1]
            k = base + j
            slot = word & 31
            for number, ref in pieces.items():
                pl.when((word >> 6) == number)(
                    lambda ref=ref: columns_of(k, ref, (word >> 5) & 1).start()
                )
            if target == 0:
                tile_from(k, own.at[slot >> 3, slot & 7]).start()
            else:
                which = (core ^ (slot >> 3)) + 2 * ((slot >> 2) & 1)
                start_one_of(par, which, lambda ref: tile_from(k, ref.at[slot & 3]))
            return 0

        lax.fori_loop(0, plan[row, 0], fetch, 0)
        base = base + plan[row, 0]
    for out in outs:
        if not call:
            out[...] = jnp.zeros_like(out)
    for first in firsts:
        first.wait()
    base = 0
    for target, out in zip(targets, outs):
        row = 2 * call + target

        def product(j, _, out=out, row=row, base=base):
            k = base + j
            slot = plan[row, j + 1] & 31
            columns_of(k, pieces[0], 0).wait()
            tile_from(k, own.at[0, 0]).wait()
            columns = pl.multiple_of((slot >> 3) * BS, BS)
            out[:, pl.ds(columns, BS)] += dot3(data[k], tiles[k])
            return 0

        lax.fori_loop(0, plan[row, 0], product, 0)
        base = base + plan[row, 0]


def beta_call(call, targets, where, plan, chains, own, par, before=()):
    rows, n = chains[0][0].shape
    pieces = chains[0][: HOPS[call][0] + 1] + chains[1][: HOPS[call][1] + 1]
    most = 2 * SLOTS * len(targets)
    return pl.pallas_call(
        functools.partial(beta_kernel, call, targets),
        out_shape=[jax.ShapeDtypeStruct((rows, n), jnp.float32)] * len(targets),
        in_specs=[SMEM] * 2 + [HBM] * (len(pieces) + 1 + len(par)) + [ANY] * len(before),
        out_specs=[VMEM] * len(targets),
        scratch_shapes=[
            pltpu.VMEM((most, rows, BS), jnp.float32),
            pltpu.VMEM((most, BS, BS), jnp.float32),
            pltpu.SemaphoreType.DMA((most,)),
            pltpu.SemaphoreType.DMA((most,)),
            pltpu.SemaphoreType.DMA((2,)),
        ],
        compiler_params=pltpu.CompilerParams(vmem_limit_bytes=24 * MIB),
        cost_estimate=pl.CostEstimate(
            flops=8 * 6 * BS**3 * len(targets), bytes_accessed=6 * MIB, transcendentals=0
        ),
        name=f"beta{call}{len(targets)}",
    )(where, plan, *in_hbm(*pieces, own, *par), *before)


def join_kernel(where, x, da, db, alpha, beta, out):
    ylo = where[1] >> 3
    out[...] = (da[...] + db[...]) * x[...] + alpha[...]
    rows = pl.ds(pl.multiple_of(ylo * BS, BS), BS)
    out[rows, :] += beta[...]


def last_kernel(where, joined, beta_other, out, total, part, sems):
    first = pl.multiple_of((1 - (where[1] >> 3)) * BS, BS)
    rows = out.at[pl.ds(first, BS)]
    copies = [
        pltpu.make_async_copy(joined.at[pl.ds(first, BS)], total, sems.at[0]),
        pltpu.make_async_copy(beta_other, part, sems.at[1]),
    ]
    for copy in copies:
        copy.start()
    for copy in copies:
        copy.wait()
    total[...] += part[...]
    back = pltpu.make_async_copy(total, rows, sems.at[2])
    back.start()
    back.wait()


def per_device(
    coeffs,
    diag_alpha,
    diag_beta,
    alpha_tiles,
    beta_tiles,
    alpha_source,
    alpha_live,
    beta_source,
    beta_live,
):
    n = coeffs.shape[0]
    core = lax.axis_index("core")
    ylo = lax.axis_index("ylo")
    where = jnp.stack([lax.axis_index(ALPHA), lax.axis_index(BETA)]).astype(jnp.int32)
    alpha_plan, beta_plan = pl.pallas_call(
        plan_kernel,
        out_shape=[
            jax.ShapeDtypeStruct((2, 16), jnp.int32),
            jax.ShapeDtypeStruct((4, 32), jnp.int32),
        ],
        in_specs=[SMEM] * 5,
        out_specs=[SMEM] * 2,
        name="plan",
    )(where, alpha_source, alpha_live, beta_source, beta_live)

    a = [lax.dynamic_slice_in_dim(coeffs, ylo * BS, BS, 0)]
    give = lax.dynamic_slice_in_dim(coeffs, (1 - ylo) * BS, BS, 0)
    b = [swap(give, "ylo")]
    a.append(step(a[0], "z"))
    u = [coeffs, step(coeffs, "x")]
    v = [swap(after(coeffs, b[0]), "yhi")]
    us = [swap(coeffs, "core")]
    mine = lax.dynamic_index_in_dim(beta_tiles, core, 0, keepdims=False)

    b.append(step(b[0], "z"))
    a.append(step(after(a[1], b[0], us[0], alpha_plan), "z"))
    u.append(step(after(u[1], b[0], a[1]), "x"))
    us.append(swap(u[1], "core"))
    b.append(step(b[1], "z"))
    a.append(step(after(a[2], b[1], u[1]), "z"))
    u.append(step(after(u[2], b[1], a[2], us[1]), "x"))
    us.append(swap(u[2], "core"))
    b.append(step(b[2], "z"))
    a.append(step(after(a[3], b[2], u[2], us[1]), "z"))
    got0 = swap(after(mine[: SLOTS // 2], v[0]), "ylo")
    v.append(step(after(v[0], u[3], b[2], a[3], us[2]), "x"))
    us.append(swap(u[3], "core"))
    b.append(step(b[3], "z"))
    a.append(step(after(a[4], b[3], u[3], v[0], us[2]), "z"))
    alpha = alpha_call(
        0,
        alpha_plan,
        [p for pair in zip([after(u[0], a[4]), *u[1:]], us) for p in pair],
        alpha_tiles,
    )
    vs = [swap(v[0], "core")]
    v.append(step(v[1], "x"))
    vs.append(swap(v[1], "core"))
    b.append(step(b[4], "z"))
    a.append(step(after(a[5], b[4], v[1], alpha, vs[0]), "z"))
    oth0 = swap(got0, "core")
    got1 = swap(after(mine[SLOTS // 2 :], got0), "ylo")
    v.append(step(v[2], "x"))
    vs.append(swap(v[2], "core"))
    b.append(step(b[5], "z"))
    a.append(step(after(a[6], b[5], v[2], oth0, vs[1]), "z"))
    beta_own, beta_par = beta_call(
        0, (0, 1), where, beta_plan, (a, b), after(beta_tiles, b[5]), [got0, oth0]
    )
    oth1 = swap(got1, "core")
    vs.append(swap(v[3], "core"))
    b.append(step(after(b[6], beta_own, vs[2]), "z"))
    alpha = alpha_call(
        1, alpha_plan, [p for pair in zip(v, vs) for p in pair], alpha_tiles, [alpha]
    )
    par = [got0, oth0, got1, oth1]
    (beta_par,) = beta_call(
        1, (1,), where, beta_plan, (a, b), after(beta_tiles, alpha), par, [beta_par]
    )
    beta_other = swap(beta_par, "ylo")
    (beta_own,) = beta_call(
        1, (0,), where, beta_plan, (a, b), after(beta_tiles, beta_par), par, [beta_own]
    )

    joined = pl.pallas_call(
        join_kernel,
        out_shape=jax.ShapeDtypeStruct((n, n), jnp.float32),
        in_specs=[SMEM] + [VMEM] * 5,
        out_specs=VMEM,
        cost_estimate=pl.CostEstimate(flops=4 * n * n, bytes_accessed=5 * MIB, transcendentals=0),
        name="join",
    )(where, coeffs, diag_alpha[:, None], diag_beta[None, :], alpha, beta_own)
    return pl.pallas_call(
        last_kernel,
        out_shape=jax.ShapeDtypeStruct((n, n), jnp.float32),
        in_specs=[SMEM, ANY, ANY],
        out_specs=ANY,
        scratch_shapes=[
            pltpu.VMEM((BS, n), jnp.float32),
            pltpu.VMEM((BS, n), jnp.float32),
            pltpu.SemaphoreType.DMA((3,)),
        ],
        input_output_aliases={1: 0},
        cost_estimate=pl.CostEstimate(flops=n * BS, bytes_accessed=2 * MIB, transcendentals=0),
        name="last",
    )(where, joined, beta_other)


def solution(mesh):
    parts = Mesh(mesh.devices.reshape(SIZES), AXES)
    return jax.shard_map(
        per_device,
        mesh=parts,
        in_specs=(
            P(ALPHA, BETA),
            P(ALPHA),
            P(BETA),
            P(ALPHA, None, None, None),
            P(BETA, None, None, None),
            P(),
            P(),
            P(),
            P(),
        ),
        out_specs=P(ALPHA, BETA),
        check_vma=False,
    )
```

```python
import functools

import jax
import jax.numpy as jnp
from jax import lax
from jax.experimental import pallas as pl
from jax.experimental.pallas import tpu as pltpu
from jax.sharding import Mesh
from jax.sharding import PartitionSpec as P

AXES = ("yhi", "x", "core", "ylo", "z")
SIZES = (2, 4, 2, 2, 8)
ALPHA = ("yhi", "x", "core")
BETA = ("ylo", "z")
BS = 256
SLOTS = 8
MIB = 1 << 20

SMEM = pl.BlockSpec(memory_space=pltpu.SMEM)
HBM = pl.BlockSpec(memory_space=pltpu.HBM)
ANY = pl.BlockSpec(memory_space=pl.ANY)
VMEM = pl.BlockSpec(memory_space=pltpu.VMEM)


def swap(value, axis):
    return lax.ppermute(value, axis, [(0, 1), (1, 0)])


def step(value, axis, way=1):
    n = lax.axis_size(axis)
    if axis == "z":
        pairs = [(i, (i + way) % n) for i in range(n)]
        pairs += [(n + i, n + (i - way) % n) for i in range(n)]
        return lax.ppermute(value, ("core", axis), pairs)
    pairs = [(2 * i, 2 * ((i + way) % n)) for i in range(n)]
    pairs += [(2 * i + 1, 2 * ((i - way) % n) + 1) for i in range(n)]
    return lax.ppermute(value, (axis, "core"), pairs)


def in_hbm(*values):
    return [pltpu.with_memory_space_constraint(value, pltpu.HBM) for value in values]


def after(value, *earlier):
    return lax.optimization_barrier((value, *earlier))[0]


def dot3(a, b):
    a_hi = a.astype(jnp.bfloat16)
    b_hi = b.astype(jnp.bfloat16)
    a_lo = (a - a_hi.astype(jnp.float32)).astype(jnp.bfloat16)
    b_lo = (b - b_hi.astype(jnp.float32)).astype(jnp.bfloat16)
    dot = functools.partial(jnp.dot, preferred_element_type=jnp.float32)
    return dot(a_hi, b_hi) + (dot(a_hi, b_lo) + dot(a_lo, b_hi))


EARLY = (0, 1, 2, 6, 7)


def plan_kernel(where, alpha_source, alpha_live, beta_source, beta_live, alpha_plan, beta_plan, picks):
    me, mb = where[0], where[1]
    up = (me & 1) == 0
    for row in range(2):
        alpha_plan[row, 0] = 0
    for row in range(4):
        beta_plan[row, 0] = 0

    def put(plan, row, word):
        count = plan[row, 0] + 1
        plan[row, 0] = count
        plan[row, count] = word

    def alpha(slot, _):
        row, c = 2 * me + (slot >> 3), slot & 7

        @pl.when(alpha_live[row, c] > 0)
        def _():
            src = alpha_source[row, c]
            owner = src >> 1
            ahead = (me >> 1) - (owner >> 1)
            hops = jnp.where((owner & 1) == 0, ahead, -ahead) & 3
            piece = hops + 4 * ((owner ^ me) & 1)
            put(alpha_plan, (owner >> 3) ^ (me >> 3), piece * 64 + (src & 1) * 32 + slot)

        src = alpha_source[2 * (me ^ 1) + (slot >> 3), c]
        owner = src >> 1

        @pl.when(((owner ^ me) & 1) == 0)
        def _():
            ahead = (me >> 1) - (owner >> 1)
            picks[(owner >> 3) ^ (me >> 3), jnp.where(up, ahead, -ahead) & 3] = src & 1

        return 0

    def beta(target, slot, _):
        row, c = 2 * (mb ^ (8 * target)) + (slot >> 3), slot & 7

        @pl.when(beta_live[row, c] > 0)
        def _():
            src = beta_source[row, c]
            owner = src >> 1
            y = (owner >> 3) ^ (mb >> 3)
            ahead = mb - owner
            d = jnp.where(up, ahead, -ahead) & 7
            early = (y == 0) | (d <= 2) | (d >= 6)
            if target:
                early = early & (c < SLOTS // 2)
            call = jnp.where(early, 0, 1)
            piece = jnp.where(y == 0, owner & 7, 8 + d)
            put(beta_plan, 2 * call + target, piece * 64 + (src & 1) * 32 + slot)

        return 0

    lax.fori_loop(0, 2 * SLOTS, alpha, 0)
    for target in range(2):
        lax.fori_loop(0, 2 * SLOTS, functools.partial(beta, target), 0)


def start_one_of(pieces, piece, make):
    for i, ref in enumerate(pieces):
        pl.when(piece == i)(lambda ref=ref: make(ref).start())


def pick_kernel(side, picks, *refs):
    pieces, (out, sem) = refs[:4], refs[4:]
    copies = [
        pltpu.make_async_copy(
            piece.at[pl.ds(pl.multiple_of(picks[side, d] * BS, BS), BS)], out.at[d], sem.at[d]
        )
        for d, piece in enumerate(pieces)
    ]
    for copy in copies:
        copy.start()
    for copy in copies:
        copy.wait()


def pick_call(side, picks, pieces):
    n = pieces[0].shape[1]
    return pl.pallas_call(
        functools.partial(pick_kernel, side),
        out_shape=jax.ShapeDtypeStruct((4, BS, n), jnp.float32),
        in_specs=[SMEM] + [ANY] * 4,
        out_specs=ANY,
        scratch_shapes=[pltpu.SemaphoreType.DMA((4,))],
        cost_estimate=pl.CostEstimate(flops=0, bytes_accessed=4 * MIB, transcendentals=0),
        name=f"pick{side}",
    )(picks, *pieces)


def alpha_kernel(side, plan, *refs):
    pieces, picked, own, refs = refs[:4], refs[4], refs[5], refs[6:]
    before, refs = (refs[:1], refs[1:]) if side else ((), refs)
    out, data, tiles, data_sem, tile_sem, out_sem = refs
    count = plan[side, 0]
    if side:
        first = pltpu.make_async_copy(before[0], out, out_sem)
        first.start()

    def tile_of(k, slot):
        return pltpu.make_async_copy(own.at[slot >> 3, slot & 7], tiles.at[k], tile_sem.at[k])

    def rows_of(k, ref):
        return pltpu.make_async_copy(ref, data.at[k], data_sem.at[k])

    def fetch(k, _):
        word = plan[side, k + 1]
        piece = word >> 6
        tile_of(k, word & 31).start()
        rows = pl.ds(pl.multiple_of(((word >> 5) & 1) * BS, BS), BS)
        start_one_of(pieces, piece, lambda ref: rows_of(k, ref.at[rows]))
        pl.when(piece >= 4)(lambda: rows_of(k, picked.at[piece & 3]).start())
        return 0

    lax.fori_loop(0, count, fetch, 0)
    if side:
        first.wait()
    else:
        out[...] = jnp.zeros_like(out)

    def product(k, _):
        slot = plan[side, k + 1] & 31
        tile_of(k, slot).wait()
        rows_of(k, picked.at[0]).wait()
        rows = pl.multiple_of((slot >> 3) * BS, BS)
        out[pl.ds(rows, BS), :] += dot3(tiles[k], data[k])
        return 0

    lax.fori_loop(0, count, product, 0)


def alpha_call(side, plan, pieces, picked, own, before=()):
    n = own.shape[0] * BS
    return pl.pallas_call(
        functools.partial(alpha_kernel, side),
        out_shape=jax.ShapeDtypeStruct((n, n), jnp.float32),
        in_specs=[SMEM] + [HBM] * 6 + [ANY] * len(before),
        out_specs=VMEM,
        scratch_shapes=[
            pltpu.VMEM((SLOTS, BS, n), jnp.float32),
            pltpu.VMEM((SLOTS, BS, BS), jnp.float32),
            pltpu.SemaphoreType.DMA((SLOTS,)),
            pltpu.SemaphoreType.DMA((SLOTS,)),
            pltpu.SemaphoreType.DMA,
        ],
        compiler_params=pltpu.CompilerParams(vmem_limit_bytes=16 * MIB),
        cost_estimate=pl.CostEstimate(
            flops=8 * 12 * BS**3, bytes_accessed=8 * MIB, transcendentals=0
        ),
        name=f"alpha{side}",
    )(plan, *in_hbm(*pieces, picked, own), *before)


def which_pieces(call, targets):
    if not call:
        return True, EARLY
    if 1 in targets:
        return True, tuple(range(8))
    return False, (3, 4, 5)


def beta_kernel(call, targets, where, plan, *refs):
    has_ring, numbers = which_pieces(call, targets)
    ring, refs = (refs[0], refs[1:]) if has_ring else (None, refs)
    pieces, refs = dict(zip(numbers, refs)), refs[len(numbers) :]
    own, refs = refs[0], refs[1:]
    par, refs = refs[: 2 * call + 2], refs[2 * call + 2 :]
    before, refs = (refs[: len(targets)], refs[len(targets) :]) if call else ((), refs)
    outs, (data, tiles, data_sem, tile_sem, out_sem) = refs[: len(targets)], refs[len(targets) :]
    core = where[0] & 1
    firsts = [
        pltpu.make_async_copy(b, out, out_sem.at[i]) for i, (b, out) in enumerate(zip(before, outs))
    ]
    for first in firsts:
        first.start()

    def columns_of(k, ref, block):
        first = pl.multiple_of(block * BS, BS)
        return pltpu.make_async_copy(ref.at[:, pl.ds(first, BS)], data.at[k], data_sem.at[k])

    def tile_from(k, ref):
        return pltpu.make_async_copy(ref, tiles.at[k], tile_sem.at[k])

    base = 0
    for target in targets:
        row = 2 * call + target

        def fetch(j, _, target=target, row=row, base=base):
            word = plan[row, j + 1]
            k = base + j
            slot = word & 31
            piece = word >> 6
            if has_ring:
                pl.when(piece < 8)(
                    lambda: columns_of(k, ring.at[piece & 7], (word >> 5) & 1).start()
                )
            for number, ref in pieces.items():
                pl.when(piece == 8 + number)(
                    lambda ref=ref: columns_of(k, ref, (word >> 5) & 1).start()
                )
            if target == 0:
                tile_from(k, own.at[slot >> 3, slot & 7]).start()
            else:
                which = (core ^ (slot >> 3)) + 2 * ((slot >> 2) & 1)
                start_one_of(par, which, lambda ref: tile_from(k, ref.at[slot & 3]))
            return 0

        lax.fori_loop(0, plan[row, 0], fetch, 0)
        base = base + plan[row, 0]
    for out in outs:
        if not call:
            out[...] = jnp.zeros_like(out)
    for first in firsts:
        first.wait()
    base = 0
    for target, out in zip(targets, outs):
        row = 2 * call + target

        def product(j, _, out=out, row=row, base=base):
            k = base + j
            slot = plan[row, j + 1] & 31
            columns_of(k, pieces[3 if call else 0], 0).wait()
            tile_from(k, own.at[0, 0]).wait()
            columns = pl.multiple_of((slot >> 3) * BS, BS)
            out[:, pl.ds(columns, BS)] += dot3(data[k], tiles[k])
            return 0

        lax.fori_loop(0, plan[row, 0], product, 0)
        base = base + plan[row, 0]


def beta_call(call, targets, where, plan, ring, held, own, par, before=()):
    rows, n = held[0].shape
    has_ring, numbers = which_pieces(call, targets)
    pieces = [ring] * has_ring + [held[i] for i in numbers]
    most = 2 * SLOTS * len(targets)
    return pl.pallas_call(
        functools.partial(beta_kernel, call, targets),
        out_shape=[jax.ShapeDtypeStruct((rows, n), jnp.float32)] * len(targets),
        in_specs=[SMEM] * 2 + [HBM] * (len(pieces) + 1 + len(par)) + [ANY] * len(before),
        out_specs=[VMEM] * len(targets),
        scratch_shapes=[
            pltpu.VMEM((most, rows, BS), jnp.float32),
            pltpu.VMEM((most, BS, BS), jnp.float32),
            pltpu.SemaphoreType.DMA((most,)),
            pltpu.SemaphoreType.DMA((most,)),
            pltpu.SemaphoreType.DMA((2,)),
        ],
        compiler_params=pltpu.CompilerParams(vmem_limit_bytes=24 * MIB),
        cost_estimate=pl.CostEstimate(
            flops=8 * 6 * BS**3 * len(targets), bytes_accessed=6 * MIB, transcendentals=0
        ),
        name=f"beta{call}{len(targets)}",
    )(where, plan, *in_hbm(*pieces, own, *par), *before)


def join_kernel(where, x, da, db, alpha, beta, out):
    ylo = where[1] >> 3
    out[...] = (da[...] + db[...]) * x[...] + alpha[...]
    rows = pl.ds(pl.multiple_of(ylo * BS, BS), BS)
    out[rows, :] += beta[...]


def last_kernel(where, joined, beta_other, out, total, part, sems):
    first = pl.multiple_of((1 - (where[1] >> 3)) * BS, BS)
    rows = out.at[pl.ds(first, BS)]
    copies = [
        pltpu.make_async_copy(joined.at[pl.ds(first, BS)], total, sems.at[0]),
        pltpu.make_async_copy(beta_other, part, sems.at[1]),
    ]
    for copy in copies:
        copy.start()
    for copy in copies:
        copy.wait()
    total[...] += part[...]
    back = pltpu.make_async_copy(total, rows, sems.at[2])
    back.start()
    back.wait()


def per_device(
    coeffs,
    diag_alpha,
    diag_beta,
    alpha_tiles,
    beta_tiles,
    alpha_source,
    alpha_live,
    beta_source,
    beta_live,
):
    n = coeffs.shape[0]
    core = lax.axis_index("core")
    ylo = lax.axis_index("ylo")
    where = jnp.stack([lax.axis_index(ALPHA), lax.axis_index(BETA)]).astype(jnp.int32)
    alpha_plan, beta_plan, picks = pl.pallas_call(
        plan_kernel,
        out_shape=[
            jax.ShapeDtypeStruct((2, 16), jnp.int32),
            jax.ShapeDtypeStruct((4, 32), jnp.int32),
            jax.ShapeDtypeStruct((2, 4), jnp.int32),
        ],
        in_specs=[SMEM] * 5,
        out_specs=[SMEM] * 3,
        name="plan",
    )(where, alpha_source, alpha_live, beta_source, beta_live)

    keep = lax.dynamic_slice_in_dim(coeffs, ylo * BS, BS, 0)
    give = lax.dynamic_slice_in_dim(coeffs, (1 - ylo) * BS, BS, 0)
    ring = lax.all_gather(keep, "z")
    p = swap(give, "ylo")
    mine = lax.dynamic_index_in_dim(beta_tiles, core, 0, keepdims=False)
    uf, ub = step(coeffs, "x"), step(coeffs, "x", -1)
    f1, b1 = step(p, "z"), step(p, "z", -1)
    v = swap(after(coeffs, p), "yhi")
    f1, b1, uf, ub, v, picks = lax.optimization_barrier((f1, b1, uf, ub, v, picks))
    f2, b2 = step(f1, "z"), step(b1, "z", -1)
    u2 = step(uf, "x")
    got0 = swap(after(mine[: SLOTS // 2], v), "ylo")
    f2, b2, u2, got0 = lax.optimization_barrier((f2, b2, u2, got0))
    f3, b3 = step(f2, "z"), step(b2, "z", -1)
    vf, vb = step(after(v, f2), "x"), step(after(v, f2), "x", -1)
    u_picked = swap(pick_call(0, picks, [coeffs, uf, u2, ub]), "core")
    alpha = alpha_call(0, alpha_plan, [coeffs, uf, u2, ub], u_picked, alpha_tiles)
    got1 = swap(after(mine[SLOTS // 2 :], got0, u_picked), "ylo")
    f3, b3, vf, vb, alpha, got1, ring = lax.optimization_barrier(
        (f3, b3, vf, vb, alpha, got1, ring)
    )
    f4 = step(f3, "z")
    v2 = step(vf, "x")
    oth0 = swap(got0, "core")
    held = [p, f1, f2, f3, f4, b3, b2, b1]
    beta_own, beta_par = beta_call(
        0, (0, 1), where, beta_plan, ring, held, after(beta_tiles, f3), [got0, oth0]
    )
    v_picked = swap(pick_call(1, picks, [v, vf, after(v2, f4), vb]), "core")
    oth1 = swap(got1, "core")
    alpha = alpha_call(1, alpha_plan, [v, vf, v2, vb], v_picked, alpha_tiles, [alpha])
    par = [got0, oth0, got1, oth1]
    (beta_par,) = beta_call(
        1, (1,), where, beta_plan, ring, held, after(beta_tiles, alpha), par, [beta_par]
    )
    beta_other = swap(beta_par, "ylo")
    (beta_own,) = beta_call(
        1, (0,), where, beta_plan, ring, held, after(beta_tiles, beta_par), par, [beta_own]
    )

    joined = pl.pallas_call(
        join_kernel,
        out_shape=jax.ShapeDtypeStruct((n, n), jnp.float32),
        in_specs=[SMEM] + [VMEM] * 5,
        out_specs=VMEM,
        cost_estimate=pl.CostEstimate(flops=4 * n * n, bytes_accessed=5 * MIB, transcendentals=0),
        name="join",
    )(where, coeffs, diag_alpha[:, None], diag_beta[None, :], alpha, beta_own)
    return pl.pallas_call(
        last_kernel,
        out_shape=jax.ShapeDtypeStruct((n, n), jnp.float32),
        in_specs=[SMEM, ANY, ANY],
        out_specs=ANY,
        scratch_shapes=[
            pltpu.VMEM((BS, n), jnp.float32),
            pltpu.VMEM((BS, n), jnp.float32),
            pltpu.SemaphoreType.DMA((3,)),
        ],
        input_output_aliases={1: 0},
        cost_estimate=pl.CostEstimate(flops=n * BS, bytes_accessed=2 * MIB, transcendentals=0),
        name="last",
    )(where, joined, beta_other)


def solution(mesh):
    parts = Mesh(mesh.devices.reshape(SIZES), AXES)
    return jax.shard_map(
        per_device,
        mesh=parts,
        in_specs=(
            P(ALPHA, BETA),
            P(ALPHA),
            P(BETA),
            P(ALPHA, None, None, None),
            P(BETA, None, None, None),
            P(),
            P(),
            P(),
            P(),
        ),
        out_specs=P(ALPHA, BETA),
        check_vma=False,
    )
```

```python
import functools

import jax
import jax.numpy as jnp
from jax import lax
from jax.experimental import pallas as pl
from jax.experimental.pallas import tpu as pltpu
from jax.sharding import Mesh
from jax.sharding import PartitionSpec as P

AXES = ("yhi", "x", "core", "ylo", "z")
SIZES = (2, 4, 2, 2, 8)
ALPHA = ("yhi", "x", "core")
BETA = ("ylo", "z")
BS = 256
SLOTS = 8
MIB = 1 << 20

SMEM = pl.BlockSpec(memory_space=pltpu.SMEM)
HBM = pl.BlockSpec(memory_space=pltpu.HBM)
ANY = pl.BlockSpec(memory_space=pl.ANY)
VMEM = pl.BlockSpec(memory_space=pltpu.VMEM)


def swap(value, axis):
    return lax.ppermute(value, axis, [(0, 1), (1, 0)])


def step(value, axis, way=1):
    n = lax.axis_size(axis)
    if axis == "z":
        pairs = [(i, (i + way) % n) for i in range(n)]
        pairs += [(n + i, n + (i - way) % n) for i in range(n)]
        return lax.ppermute(value, ("core", axis), pairs)
    pairs = [(2 * i, 2 * ((i + way) % n)) for i in range(n)]
    pairs += [(2 * i + 1, 2 * ((i - way) % n) + 1) for i in range(n)]
    return lax.ppermute(value, (axis, "core"), pairs)


def in_hbm(*values):
    return [pltpu.with_memory_space_constraint(value, pltpu.HBM) for value in values]


def after(value, *earlier):
    return lax.optimization_barrier((value, *earlier))[0]


def dot3(a, b):
    a_hi = a.astype(jnp.bfloat16)
    b_hi = b.astype(jnp.bfloat16)
    a_lo = (a - a_hi.astype(jnp.float32)).astype(jnp.bfloat16)
    b_lo = (b - b_hi.astype(jnp.float32)).astype(jnp.bfloat16)
    dot = functools.partial(jnp.dot, preferred_element_type=jnp.float32)
    return dot(a_hi, b_hi) + (dot(a_hi, b_lo) + dot(a_lo, b_hi))


def plan_kernel(where, alpha_source, alpha_live, beta_source, beta_live, alpha_plan, beta_plan, picks):
    me, mb = where[0], where[1]
    up = (me & 1) == 0
    for row in range(2):
        alpha_plan[row, 0] = 0
    for row in range(4):
        beta_plan[row, 0] = 0

    def put(plan, row, word):
        count = plan[row, 0] + 1
        plan[row, 0] = count
        plan[row, count] = word

    def alpha(slot, _):
        row, c = 2 * me + (slot >> 3), slot & 7

        @pl.when(alpha_live[row, c] > 0)
        def _():
            src = alpha_source[row, c]
            owner = src >> 1
            ahead = (me >> 1) - (owner >> 1)
            hops = jnp.where((owner & 1) == 0, ahead, -ahead) & 3
            piece = hops + 4 * ((owner ^ me) & 1)
            put(alpha_plan, (owner >> 3) ^ (me >> 3), piece * 64 + (src & 1) * 32 + slot)

        src = alpha_source[2 * (me ^ 1) + (slot >> 3), c]
        owner = src >> 1

        @pl.when(((owner ^ me) & 1) == 0)
        def _():
            ahead = (me >> 1) - (owner >> 1)
            picks[(owner >> 3) ^ (me >> 3), jnp.where(up, ahead, -ahead) & 3] = src & 1

        return 0

    def beta(target, slot, _):
        row, c = 2 * (mb ^ (8 * target)) + (slot >> 3), slot & 7

        @pl.when(beta_live[row, c] > 0)
        def _():
            src = beta_source[row, c]
            owner = src >> 1
            side = (owner >> 3) ^ (mb >> 3)
            piece = owner & 7
            put(beta_plan, 2 * side + target, piece * 64 + (src & 1) * 32 + slot)

        return 0

    lax.fori_loop(0, 2 * SLOTS, alpha, 0)
    for target in range(2):
        lax.fori_loop(0, 2 * SLOTS, functools.partial(beta, target), 0)


def start_one_of(pieces, piece, make):
    for i, ref in enumerate(pieces):
        pl.when(piece == i)(lambda ref=ref: make(ref).start())


def pick_kernel(side, picks, *refs):
    pieces, (out, sem) = refs[:4], refs[4:]
    copies = [
        pltpu.make_async_copy(
            piece.at[pl.ds(pl.multiple_of(picks[side, d] * BS, BS), BS)], out.at[d], sem.at[d]
        )
        for d, piece in enumerate(pieces)
    ]
    for copy in copies:
        copy.start()
    for copy in copies:
        copy.wait()


def pick_call(side, picks, pieces):
    n = pieces[0].shape[1]
    return pl.pallas_call(
        functools.partial(pick_kernel, side),
        out_shape=jax.ShapeDtypeStruct((4, BS, n), jnp.float32),
        in_specs=[SMEM] + [ANY] * 4,
        out_specs=VMEM,
        scratch_shapes=[pltpu.SemaphoreType.DMA((4,))],
        cost_estimate=pl.CostEstimate(flops=0, bytes_accessed=4 * MIB, transcendentals=0),
        name=f"pick{side}",
    )(picks, *pieces)


def alpha_kernel(side, plan, *refs):
    pieces, picked, own, refs = refs[:4], refs[4], refs[5], refs[6:]
    before, refs = (refs[:1], refs[1:]) if side else ((), refs)
    out, data, tiles, data_sem, tile_sem, out_sem = refs
    count = plan[side, 0]
    if side:
        first = pltpu.make_async_copy(before[0], out, out_sem)
        first.start()

    def tile_of(k, slot):
        return pltpu.make_async_copy(own.at[slot >> 3, slot & 7], tiles.at[k], tile_sem.at[k])

    def rows_of(k, ref):
        return pltpu.make_async_copy(ref, data.at[k], data_sem.at[k])

    def fetch(k, _):
        word = plan[side, k + 1]
        piece = word >> 6
        tile_of(k, word & 31).start()
        rows = pl.ds(pl.multiple_of(((word >> 5) & 1) * BS, BS), BS)
        start_one_of(pieces, piece, lambda ref: rows_of(k, ref.at[rows]))
        pl.when(piece >= 4)(lambda: rows_of(k, picked.at[piece & 3]).start())
        return 0

    lax.fori_loop(0, count, fetch, 0)
    if side:
        first.wait()
    else:
        out[...] = jnp.zeros_like(out)

    def product(k, _):
        slot = plan[side, k + 1] & 31
        tile_of(k, slot).wait()
        rows_of(k, picked.at[0]).wait()
        rows = pl.multiple_of((slot >> 3) * BS, BS)
        out[pl.ds(rows, BS), :] += dot3(tiles[k], data[k])
        return 0

    lax.fori_loop(0, count, product, 0)


def alpha_call(side, plan, pieces, picked, own, before=()):
    n = own.shape[0] * BS
    return pl.pallas_call(
        functools.partial(alpha_kernel, side),
        out_shape=jax.ShapeDtypeStruct((n, n), jnp.float32),
        in_specs=[SMEM] + [HBM] * 6 + [ANY] * len(before),
        out_specs=VMEM,
        scratch_shapes=[
            pltpu.VMEM((SLOTS, BS, n), jnp.float32),
            pltpu.VMEM((SLOTS, BS, BS), jnp.float32),
            pltpu.SemaphoreType.DMA((SLOTS,)),
            pltpu.SemaphoreType.DMA((SLOTS,)),
            pltpu.SemaphoreType.DMA,
        ],
        compiler_params=pltpu.CompilerParams(vmem_limit_bytes=16 * MIB),
        cost_estimate=pl.CostEstimate(
            flops=8 * 12 * BS**3, bytes_accessed=8 * MIB, transcendentals=0
        ),
        name=f"alpha{side}",
    )(plan, *in_hbm(*pieces, picked, own), *before)


def beta_kernel(call, targets, where, plan, *refs):
    ring, refs = refs[0], refs[1:]
    own, refs = refs[0], refs[1:]
    par, refs = refs[:2], refs[2:]
    before, refs = (refs[: len(targets)], refs[len(targets) :]) if call else ((), refs)
    outs, (data, tiles, data_sem, tile_sem, out_sem) = refs[: len(targets)], refs[len(targets) :]
    core = where[0] & 1
    firsts = [
        pltpu.make_async_copy(b, out, out_sem.at[i]) for i, (b, out) in enumerate(zip(before, outs))
    ]
    for first in firsts:
        first.start()

    def columns_of(k, ref, block):
        first = pl.multiple_of(block * BS, BS)
        return pltpu.make_async_copy(ref.at[:, pl.ds(first, BS)], data.at[k], data_sem.at[k])

    def tile_from(k, ref):
        return pltpu.make_async_copy(ref, tiles.at[k], tile_sem.at[k])

    base = 0
    for target in targets:
        row = 2 * call + target

        def fetch(j, _, target=target, row=row, base=base):
            word = plan[row, j + 1]
            k = base + j
            slot = word & 31
            columns_of(k, ring.at[word >> 6], (word >> 5) & 1).start()
            if target == 0:
                tile_from(k, own.at[slot >> 3, slot & 7]).start()
            else:
                start_one_of(par, core ^ (slot >> 3), lambda ref: tile_from(k, ref.at[slot & 7]))
            return 0

        lax.fori_loop(0, plan[row, 0], fetch, 0)
        base = base + plan[row, 0]
    for out in outs:
        if not call:
            out[...] = jnp.zeros_like(out)
    for first in firsts:
        first.wait()
    base = 0
    for target, out in zip(targets, outs):
        row = 2 * call + target

        def product(j, _, out=out, row=row, base=base):
            k = base + j
            slot = plan[row, j + 1] & 31
            columns_of(k, ring.at[0], 0).wait()
            tile_from(k, own.at[0, 0]).wait()
            columns = pl.multiple_of((slot >> 3) * BS, BS)
            out[:, pl.ds(columns, BS)] += dot3(data[k], tiles[k])
            return 0

        lax.fori_loop(0, plan[row, 0], product, 0)
        base = base + plan[row, 0]


def beta_call(call, targets, where, plan, ring, own, par, before=()):
    _, rows, n = ring.shape
    most = 2 * SLOTS * len(targets)
    return pl.pallas_call(
        functools.partial(beta_kernel, call, targets),
        out_shape=[jax.ShapeDtypeStruct((rows, n), jnp.float32)] * len(targets),
        in_specs=[SMEM] * 2 + [HBM] * (2 + len(par)) + [ANY] * len(before),
        out_specs=[VMEM] * len(targets),
        scratch_shapes=[
            pltpu.VMEM((most, rows, BS), jnp.float32),
            pltpu.VMEM((most, BS, BS), jnp.float32),
            pltpu.SemaphoreType.DMA((most,)),
            pltpu.SemaphoreType.DMA((most,)),
            pltpu.SemaphoreType.DMA((2,)),
        ],
        compiler_params=pltpu.CompilerParams(vmem_limit_bytes=24 * MIB),
        cost_estimate=pl.CostEstimate(
            flops=8 * 6 * BS**3 * len(targets), bytes_accessed=6 * MIB, transcendentals=0
        ),
        name=f"beta{call}{len(targets)}",
    )(where, plan, *in_hbm(ring, own, *par), *before)


def join_kernel(where, x, da, db, alpha, beta, out):
    ylo = where[1] >> 3
    out[...] = (da[...] + db[...]) * x[...] + alpha[...]
    rows = pl.ds(pl.multiple_of(ylo * BS, BS), BS)
    out[rows, :] += beta[...]


def last_kernel(where, joined, beta_other, out, total, part, sems):
    first = pl.multiple_of((1 - (where[1] >> 3)) * BS, BS)
    rows = out.at[pl.ds(first, BS)]
    copies = [
        pltpu.make_async_copy(joined.at[pl.ds(first, BS)], total, sems.at[0]),
        pltpu.make_async_copy(beta_other, part, sems.at[1]),
    ]
    for copy in copies:
        copy.start()
    for copy in copies:
        copy.wait()
    total[...] += part[...]
    back = pltpu.make_async_copy(total, rows, sems.at[2])
    back.start()
    back.wait()


def per_device(
    coeffs,
    diag_alpha,
    diag_beta,
    alpha_tiles,
    beta_tiles,
    alpha_source,
    alpha_live,
    beta_source,
    beta_live,
):
    n = coeffs.shape[0]
    core = lax.axis_index("core")
    ylo = lax.axis_index("ylo")
    where = jnp.stack([lax.axis_index(ALPHA), lax.axis_index(BETA)]).astype(jnp.int32)
    keep = lax.dynamic_slice_in_dim(coeffs, ylo * BS, BS, 0)
    give = lax.dynamic_slice_in_dim(coeffs, (1 - ylo) * BS, BS, 0)
    near = lax.all_gather(keep, "z")
    p = swap(give, "ylo")
    far = lax.all_gather(p, "z")
    mine = lax.dynamic_index_in_dim(beta_tiles, core, 0, keepdims=False)
    uf, ub = step(coeffs, "x"), step(coeffs, "x", -1)
    v = swap(after(coeffs, p), "yhi")
    alpha_plan, beta_plan, picks = pl.pallas_call(
        plan_kernel,
        out_shape=[
            jax.ShapeDtypeStruct((2, 16), jnp.int32),
            jax.ShapeDtypeStruct((4, 32), jnp.int32),
            jax.ShapeDtypeStruct((2, 4), jnp.int32),
        ],
        in_specs=[SMEM] * 5,
        out_specs=[SMEM] * 3,
        name="plan",
    )(after(where, uf), alpha_source, alpha_live, beta_source, beta_live)
    uf, ub = lax.optimization_barrier((uf, ub))
    u2 = step(uf, "x")
    got = swap(after(mine, uf), "ylo")
    u2, v, picks = lax.optimization_barrier((u2, v, picks))
    vf, vb = step(v, "x"), step(v, "x", -1)
    u_picked = swap(pick_call(0, picks, [coeffs, uf, u2, ub]), "core")
    alpha = alpha_call(0, alpha_plan, [coeffs, uf, u2, ub], u_picked, alpha_tiles)
    vf, vb, alpha, near = lax.optimization_barrier((vf, vb, alpha, near))
    v2 = step(vf, "x")
    other = swap(after(got, vf), "core")
    beta = beta_call(0, (0, 1), where, beta_plan, near, beta_tiles, [got, other])
    v2, beta_own, beta_par = lax.optimization_barrier((v2, *beta))
    v_picked = swap(pick_call(1, picks, [v, vf, v2, vb]), "core")
    alpha = alpha_call(1, alpha_plan, [v, vf, v2, vb], v_picked, alpha_tiles, [alpha])
    far = after(far, alpha)
    (beta_par,) = beta_call(
        1, (1,), where, beta_plan, far, beta_tiles, [got, other], [beta_par]
    )
    beta_other = swap(beta_par, "ylo")
    (beta_own,) = beta_call(
        1, (0,), where, beta_plan, far, after(beta_tiles, beta_par), [got, other], [beta_own]
    )

    joined = pl.pallas_call(
        join_kernel,
        out_shape=jax.ShapeDtypeStruct((n, n), jnp.float32),
        in_specs=[SMEM] + [VMEM] * 5,
        out_specs=VMEM,
        cost_estimate=pl.CostEstimate(flops=4 * n * n, bytes_accessed=5 * MIB, transcendentals=0),
        name="join",
    )(where, coeffs, diag_alpha[:, None], diag_beta[None, :], alpha, beta_own)
    return pl.pallas_call(
        last_kernel,
        out_shape=jax.ShapeDtypeStruct((n, n), jnp.float32),
        in_specs=[SMEM, ANY, ANY],
        out_specs=ANY,
        scratch_shapes=[
            pltpu.VMEM((BS, n), jnp.float32),
            pltpu.VMEM((BS, n), jnp.float32),
            pltpu.SemaphoreType.DMA((3,)),
        ],
        input_output_aliases={1: 0},
        cost_estimate=pl.CostEstimate(flops=n * BS, bytes_accessed=2 * MIB, transcendentals=0),
        name="last",
    )(where, joined, beta_other)


def solution(mesh):
    parts = Mesh(mesh.devices.reshape(SIZES), AXES)
    return jax.shard_map(
        per_device,
        mesh=parts,
        in_specs=(
            P(ALPHA, BETA),
            P(ALPHA),
            P(BETA),
            P(ALPHA, None, None, None),
            P(BETA, None, None, None),
            P(),
            P(),
            P(),
            P(),
        ),
        out_specs=P(ALPHA, BETA),
        check_vma=False,
    )
```

```python
import functools

import jax
import jax.numpy as jnp
from jax import lax
from jax.experimental import pallas as pl
from jax.experimental.pallas import tpu as pltpu
from jax.sharding import Mesh
from jax.sharding import PartitionSpec as P

AXES = ("yhi", "x", "core", "ylo", "z")
SIZES = (2, 4, 2, 2, 8)
ALPHA = ("yhi", "x", "core")
BETA = ("ylo", "z")
BS = 256
SLOTS = 8
MIB = 1 << 20
SMALL = pl.CostEstimate(flops=1 << 20, bytes_accessed=1 << 18, transcendentals=0)

SMEM = pl.BlockSpec(memory_space=pltpu.SMEM)
HBM = pl.BlockSpec(memory_space=pltpu.HBM)
ANY = pl.BlockSpec(memory_space=pl.ANY)
VMEM = pl.BlockSpec(memory_space=pltpu.VMEM)


def swap(value, axis):
    return lax.ppermute(value, axis, [(0, 1), (1, 0)])


def step(value, axis, way=1):
    n = lax.axis_size(axis)
    if axis == "z":
        pairs = [(i, (i + way) % n) for i in range(n)]
        pairs += [(n + i, n + (i - way) % n) for i in range(n)]
        return lax.ppermute(value, ("core", axis), pairs)
    pairs = [(2 * i, 2 * ((i + way) % n)) for i in range(n)]
    pairs += [(2 * i + 1, 2 * ((i - way) % n) + 1) for i in range(n)]
    return lax.ppermute(value, (axis, "core"), pairs)


def in_hbm(*values):
    return [pltpu.with_memory_space_constraint(value, pltpu.HBM) for value in values]


def after(value, *earlier):
    return lax.optimization_barrier((value, *earlier))[0]


def dot3(a, b):
    a_hi = a.astype(jnp.bfloat16)
    b_hi = b.astype(jnp.bfloat16)
    a_lo = (a - a_hi.astype(jnp.float32)).astype(jnp.bfloat16)
    b_lo = (b - b_hi.astype(jnp.float32)).astype(jnp.bfloat16)
    dot = functools.partial(jnp.dot, preferred_element_type=jnp.float32)
    return dot(a_hi, b_hi) + (dot(a_hi, b_lo) + dot(a_lo, b_hi))


def plan_kernel(
    where, alpha_source, alpha_live, beta_source, beta_live, alpha_plan, beta_plan, picks, sends
):
    me, mb = where[0], where[1]
    up = (me & 1) == 0
    for row in range(2):
        alpha_plan[row, 0] = 0
    for row in range(4):
        beta_plan[row, 0] = 0

    def put(plan, row, word):
        count = plan[row, 0] + 1
        plan[row, 0] = count
        plan[row, count] = word

    def alpha(slot, _):
        row, c = 2 * me + (slot >> 3), slot & 7

        @pl.when(alpha_live[row, c] > 0)
        def _():
            src = alpha_source[row, c]
            owner = src >> 1
            ahead = (me >> 1) - (owner >> 1)
            hops = jnp.where((owner & 1) == 0, ahead, -ahead) & 3
            piece = hops + 4 * ((owner ^ me) & 1)
            put(alpha_plan, (owner >> 3) ^ (me >> 3), piece * 64 + (src & 1) * 32 + slot)

        src = alpha_source[2 * (me ^ 1) + (slot >> 3), c]
        owner = src >> 1

        @pl.when(((owner ^ me) & 1) == 0)
        def _():
            ahead = (me >> 1) - (owner >> 1)
            picks[(owner >> 3) ^ (me >> 3), jnp.where(up, ahead, -ahead) & 3] = src & 1

        return 0

    def beta(target, slot, _):
        row, c = 2 * (mb ^ (8 * target)) + (slot >> 3), slot & 7
        src = beta_source[row, c]
        owner = src >> 1
        near = (owner >> 3) == (mb >> 3)
        place = owner & 7

        @pl.when(near & (beta_live[row, c] > 0))
        def _():
            ahead = mb - owner
            d = jnp.where(up, ahead, -ahead) & 7
            call = jnp.where((d <= 2) | (d >= 6), 0, 1)
            tile = place if target else c
            word = d * 64 + (src & 1) * 32 + (slot >> 3) * 16 + tile
            put(beta_plan, 2 * call + target, word)

        if not target:

            @pl.when(jnp.logical_not(near))
            def _():
                sends[place] = slot

        return 0

    lax.fori_loop(0, 2 * SLOTS, alpha, 0)
    for target in range(2):
        lax.fori_loop(0, 2 * SLOTS, functools.partial(beta, target), 0)


def start_one_of(pieces, piece, make):
    for i, ref in enumerate(pieces):
        pl.when(piece == i)(lambda ref=ref: make(ref).start())


def pick_kernel(side, picks, *refs):
    pieces, (out, sem) = refs[:4], refs[4:]
    copies = [
        pltpu.make_async_copy(
            piece.at[pl.ds(pl.multiple_of(picks[side, d] * BS, BS), BS)], out.at[d], sem.at[d]
        )
        for d, piece in enumerate(pieces)
    ]
    for copy in copies:
        copy.start()
    for copy in copies:
        copy.wait()


def pick_call(side, picks, pieces):
    n = pieces[0].shape[1]
    return pl.pallas_call(
        functools.partial(pick_kernel, side),
        out_shape=jax.ShapeDtypeStruct((4, BS, n), jnp.float32),
        in_specs=[SMEM] + [ANY] * 4,
        out_specs=VMEM,
        scratch_shapes=[pltpu.SemaphoreType.DMA((4,))],
        cost_estimate=SMALL,
        name=f"pick{side}",
    )(picks, *pieces)


def alpha_kernel(side, plan, *refs):
    pieces, picked, own, refs = refs[:4], refs[4], refs[5], refs[6:]
    before, refs = (refs[:1], refs[1:]) if side else ((), refs)
    out, data, tiles, data_sem, tile_sem, out_sem = refs
    count = plan[side, 0]
    if side:
        first = pltpu.make_async_copy(before[0], out, out_sem)
        first.start()

    def tile_of(k, slot):
        return pltpu.make_async_copy(own.at[slot >> 3, slot & 7], tiles.at[k], tile_sem.at[k])

    def rows_of(k, ref):
        return pltpu.make_async_copy(ref, data.at[k], data_sem.at[k])

    def fetch(k, _):
        word = plan[side, k + 1]
        piece = word >> 6
        tile_of(k, word & 31).start()
        rows = pl.ds(pl.multiple_of(((word >> 5) & 1) * BS, BS), BS)
        start_one_of(pieces, piece, lambda ref: rows_of(k, ref.at[rows]))
        pl.when(piece >= 4)(lambda: rows_of(k, picked.at[piece & 3]).start())
        return 0

    lax.fori_loop(0, count, fetch, 0)
    if side:
        first.wait()
    else:
        out[...] = jnp.zeros_like(out)

    def product(k, _):
        slot = plan[side, k + 1] & 31
        tile_of(k, slot).wait()
        rows_of(k, picked.at[0]).wait()
        rows = pl.multiple_of((slot >> 3) * BS, BS)
        out[pl.ds(rows, BS), :] += dot3(tiles[k], data[k])
        return 0

    lax.fori_loop(0, count, product, 0)


def alpha_call(side, plan, pieces, picked, own, before=()):
    n = own.shape[0] * BS
    return pl.pallas_call(
        functools.partial(alpha_kernel, side),
        out_shape=jax.ShapeDtypeStruct((n, n), jnp.float32),
        in_specs=[SMEM] + [HBM] * 6 + [ANY] * len(before),
        out_specs=VMEM,
        scratch_shapes=[
            pltpu.VMEM((SLOTS, BS, n), jnp.float32),
            pltpu.VMEM((SLOTS, BS, BS), jnp.float32),
            pltpu.SemaphoreType.DMA((SLOTS,)),
            pltpu.SemaphoreType.DMA((SLOTS,)),
            pltpu.SemaphoreType.DMA,
        ],
        compiler_params=pltpu.CompilerParams(vmem_limit_bytes=16 * MIB),
        cost_estimate=SMALL,
        name=f"alpha{side}",
    )(plan, *in_hbm(*pieces, picked, own), *before)


def send_kernel(where, sends, own, out, sem):
    copies = []
    for i in range(SLOTS // 2):
        slot = sends[(where[0] & 1) * (SLOTS // 2) + i]
        copies.append(
            pltpu.make_async_copy(own.at[slot >> 3, slot & 7], out.at[i], sem.at[i])
        )
    for copy in copies:
        copy.start()
    for copy in copies:
        copy.wait()


def send_call(where, sends, own):
    return pl.pallas_call(
        send_kernel,
        out_shape=jax.ShapeDtypeStruct((SLOTS // 2, BS, BS), jnp.float32),
        in_specs=[SMEM] * 2 + [HBM],
        out_specs=VMEM,
        scratch_shapes=[pltpu.SemaphoreType.DMA((SLOTS // 2,))],
        cost_estimate=SMALL,
        name="send",
    )(where, sends, *in_hbm(own))


HOPS = ((0, 1, 2, 6, 7), (3, 4, 5))


def beta_kernel(call, targets, where, plan, *refs):
    numbers = HOPS[call]
    pieces, refs = refs[: len(numbers)], refs[len(numbers) :]
    own, got, other, refs = refs[0], refs[1], refs[2], refs[3:]
    before, refs = (refs[: len(targets)], refs[len(targets) :]) if call else ((), refs)
    outs, (data, tiles, data_sem, tile_sem, out_sem) = refs[: len(targets)], refs[len(targets) :]
    core = where[0] & 1
    firsts = [
        pltpu.make_async_copy(b, out, out_sem.at[i]) for i, (b, out) in enumerate(zip(before, outs))
    ]
    for first in firsts:
        first.start()

    def columns_of(k, ref, block):
        first = pl.multiple_of(block * BS, BS)
        return pltpu.make_async_copy(ref.at[:, pl.ds(first, BS)], data.at[k], data_sem.at[k])

    def tile_from(k, ref):
        return pltpu.make_async_copy(ref, tiles.at[k], tile_sem.at[k])

    base = 0
    for target in targets:
        row = 2 * call + target

        def fetch(j, _, target=target, row=row, base=base):
            word = plan[row, j + 1]
            k = base + j
            tile = word & 15
            for number, ref in zip(numbers, pieces):
                pl.when((word >> 6) == number)(
                    lambda ref=ref: columns_of(k, ref, (word >> 5) & 1).start()
                )
            if target == 0:
                tile_from(k, own.at[(word >> 4) & 1, tile]).start()
            else:
                start_one_of(
                    (got, other), core ^ (tile >> 2), lambda ref: tile_from(k, ref.at[tile & 3])
                )
            return 0

        lax.fori_loop(0, plan[row, 0], fetch, 0)
        base = base + plan[row, 0]
    for out in outs:
        if not call:
            out[...] = jnp.zeros_like(out)
    for first in firsts:
        first.wait()
    base = 0
    for target, out in zip(targets, outs):
        row = 2 * call + target

        def product(j, _, out=out, row=row, base=base):
            k = base + j
            block = (plan[row, j + 1] >> 4) & 1
            columns_of(k, pieces[0], 0).wait()
            tile_from(k, own.at[0, 0]).wait()
            columns = pl.multiple_of(block * BS, BS)
            out[:, pl.ds(columns, BS)] += dot3(data[k], tiles[k])
            return 0

        lax.fori_loop(0, plan[row, 0], product, 0)
        base = base + plan[row, 0]


def beta_call(call, targets, where, plan, held, own, got, other, before=()):
    n = held[0].shape[0]
    pieces = [held[d] for d in HOPS[call]]
    most = len(HOPS[call]) * len(targets)
    return pl.pallas_call(
        functools.partial(beta_kernel, call, targets),
        out_shape=[jax.ShapeDtypeStruct((n, n), jnp.float32)] * len(targets),
        in_specs=[SMEM] * 2 + [HBM] * (len(pieces) + 3) + [ANY] * len(before),
        out_specs=[VMEM] * len(targets),
        scratch_shapes=[
            pltpu.VMEM((most, n, BS), jnp.float32),
            pltpu.VMEM((most, BS, BS), jnp.float32),
            pltpu.SemaphoreType.DMA((most,)),
            pltpu.SemaphoreType.DMA((most,)),
            pltpu.SemaphoreType.DMA((2,)),
        ],
        compiler_params=pltpu.CompilerParams(vmem_limit_bytes=16 * MIB),
        cost_estimate=SMALL,
        name=f"beta{call}{len(targets)}",
    )(where, plan, *in_hbm(*pieces, own, got, other), *before)


def per_device(
    coeffs,
    diag_alpha,
    diag_beta,
    alpha_tiles,
    beta_tiles,
    alpha_source,
    alpha_live,
    beta_source,
    beta_live,
):
    where = jnp.stack([lax.axis_index(ALPHA), lax.axis_index(BETA)]).astype(jnp.int32)
    f1, b1 = step(coeffs, "z"), step(coeffs, "z", -1)
    uf, ub = step(coeffs, "x"), step(coeffs, "x", -1)
    v = swap(coeffs, "yhi")
    alpha_plan, beta_plan, picks, sends = pl.pallas_call(
        plan_kernel,
        out_shape=[
            jax.ShapeDtypeStruct((2, 16), jnp.int32),
            jax.ShapeDtypeStruct((4, 32), jnp.int32),
            jax.ShapeDtypeStruct((2, 4), jnp.int32),
            jax.ShapeDtypeStruct((SLOTS,), jnp.int32),
        ],
        in_specs=[SMEM] * 5,
        out_specs=[SMEM] * 4,
        name="plan",
    )(where, alpha_source, alpha_live, beta_source, beta_live)
    tiles = send_call(where, sends, beta_tiles)
    f1, b1, uf, ub, v, tiles, picks = lax.optimization_barrier((f1, b1, uf, ub, v, tiles, picks))
    f2, b2 = step(f1, "z"), step(b1, "z", -1)
    u2 = step(uf, "x")
    got = swap(tiles, "ylo")
    f2, b2, u2, got = lax.optimization_barrier((f2, b2, u2, got))
    f3, b3 = step(f2, "z"), step(b2, "z", -1)
    vf, vb = step(v, "x"), step(v, "x", -1)
    other = swap(got, "core")
    picked = pick_call(0, after(picks, other), [coeffs, uf, u2, ub])
    held = [coeffs, f1, f2, None, None, None, b2, b1]
    beta_own, beta_par = beta_call(0, (0, 1), where, beta_plan, held, beta_tiles, got, other)
    f3, b3, vf, vb, picked, beta_own, beta_par = lax.optimization_barrier(
        (f3, b3, vf, vb, picked, beta_own, beta_par)
    )
    held[3], held[4], held[5] = f3, step(f3, "z"), b3
    v2 = step(vf, "x")
    u_picked = swap(picked, "core")
    alpha = alpha_call(0, alpha_plan, [coeffs, uf, u2, ub], u_picked, alpha_tiles)
    alpha, beta_par = lax.optimization_barrier((alpha, beta_par))
    (beta_par,) = beta_call(
        1, (1,), where, beta_plan, held, beta_tiles, got, other, [beta_par]
    )
    beta_other = swap(beta_par, "ylo")
    (beta_own,) = beta_call(
        1, (0,), where, beta_plan, held, after(beta_tiles, beta_par), got, other, [beta_own]
    )
    v_picked = swap(pick_call(1, after(picks, beta_own), [v, vf, v2, vb]), "core")
    alpha = alpha_call(1, alpha_plan, [v, vf, v2, vb], v_picked, alpha_tiles, [alpha])
    joined = (diag_alpha[:, None] + diag_beta[None, :]) * coeffs + alpha + beta_own
    return lax.optimization_barrier(joined) + beta_other


def solution(mesh):
    parts = Mesh(mesh.devices.reshape(SIZES), AXES)
    return jax.shard_map(
        per_device,
        mesh=parts,
        in_specs=(
            P(ALPHA, BETA),
            P(ALPHA),
            P(BETA),
            P(ALPHA, None, None, None),
            P(BETA, None, None, None),
            P(),
            P(),
            P(),
            P(),
        ),
        out_specs=P(ALPHA, BETA),
        check_vma=False,
    )
```

```python
import functools

import jax
import jax.numpy as jnp
from jax import lax
from jax.experimental import pallas as pl
from jax.experimental.pallas import tpu as pltpu
from jax.sharding import Mesh
from jax.sharding import PartitionSpec as P

AXES = ("yhi", "x", "core", "ylo", "z")
SIZES = (2, 4, 2, 2, 8)
ALPHA = ("yhi", "x", "core")
BETA = ("ylo", "z")
BS = 256
SLOTS = 8
MIB = 1 << 20
SMALL = pl.CostEstimate(flops=1 << 20, bytes_accessed=1 << 18, transcendentals=0)

SMEM = pl.BlockSpec(memory_space=pltpu.SMEM)
HBM = pl.BlockSpec(memory_space=pltpu.HBM)
ANY = pl.BlockSpec(memory_space=pl.ANY)
VMEM = pl.BlockSpec(memory_space=pltpu.VMEM)


def swap(value, axis):
    return lax.ppermute(value, axis, [(0, 1), (1, 0)])


def step(value, axis, way=1):
    n = lax.axis_size(axis)
    if axis == "z":
        pairs = [(i, (i + way) % n) for i in range(n)]
        pairs += [(n + i, n + (i - way) % n) for i in range(n)]
        return lax.ppermute(value, ("core", axis), pairs)
    pairs = [(2 * i, 2 * ((i + way) % n)) for i in range(n)]
    pairs += [(2 * i + 1, 2 * ((i - way) % n) + 1) for i in range(n)]
    return lax.ppermute(value, (axis, "core"), pairs)


def in_hbm(*values):
    return [pltpu.with_memory_space_constraint(value, pltpu.HBM) for value in values]


def after(value, *earlier):
    return lax.optimization_barrier((value, *earlier))[0]


def dot3(a, b):
    a_hi = a.astype(jnp.bfloat16)
    b_hi = b.astype(jnp.bfloat16)
    a_lo = (a - a_hi.astype(jnp.float32)).astype(jnp.bfloat16)
    b_lo = (b - b_hi.astype(jnp.float32)).astype(jnp.bfloat16)
    dot = functools.partial(jnp.dot, preferred_element_type=jnp.float32)
    return dot(a_hi, b_hi) + (dot(a_hi, b_lo) + dot(a_lo, b_hi))


def plan_kernel(
    where, alpha_source, alpha_live, beta_source, beta_live, alpha_plan, beta_plan, picks, sends
):
    me, mb = where[0], where[1]
    up = (me & 1) == 0
    alpha_plan[0, 0] = 0
    for row in range(6):
        beta_plan[row, 0] = 0

    def put(plan, row, word):
        count = plan[row, 0] + 1
        plan[row, 0] = count
        plan[row, count] = word

    def alpha(slot, _):
        row, c = 2 * me + (slot >> 3), slot & 7

        @pl.when(alpha_live[row, c] > 0)
        def _():
            src = alpha_source[row, c]
            owner = src >> 1
            ahead = (me >> 1) - (owner >> 1)
            hops = jnp.where((owner & 1) == 0, ahead, -ahead) & 3
            piece = hops + 4 * ((owner >> 3) ^ (me >> 3)) + 8 * ((owner ^ me) & 1)
            put(alpha_plan, 0, piece * 64 + (src & 1) * 32 + slot)

        src = alpha_source[2 * (me ^ 1) + (slot >> 3), c]
        owner = src >> 1

        @pl.when(((owner ^ me) & 1) == 0)
        def _():
            ahead = (me >> 1) - (owner >> 1)
            picks[4 * ((owner >> 3) ^ (me >> 3)) + (jnp.where(up, ahead, -ahead) & 3)] = src & 1

        return 0

    def beta(target, slot, _):
        row, c = 2 * (mb ^ (8 * target)) + (slot >> 3), slot & 7
        src = beta_source[row, c]
        owner = src >> 1
        near = (owner >> 3) == (mb >> 3)
        place = owner & 7

        @pl.when(near & (beta_live[row, c] > 0))
        def _():
            ahead = mb - owner
            d = jnp.where(up, ahead, -ahead) & 7
            call = jnp.where((d <= 2) | (d >= 6), 0, 1)
            if target:
                call = jnp.where(d == 4, 2, call)
            tile = place if target else c
            word = d * 64 + (src & 1) * 32 + (slot >> 3) * 16 + tile
            put(beta_plan, 2 * call + target, word)

        if not target:

            @pl.when(jnp.logical_not(near))
            def _():
                sends[place] = slot

        return 0

    lax.fori_loop(0, 2 * SLOTS, alpha, 0)
    for target in range(2):
        lax.fori_loop(0, 2 * SLOTS, functools.partial(beta, target), 0)


def start_one_of(pieces, piece, make):
    for i, ref in enumerate(pieces):
        pl.when(piece == i)(lambda ref=ref: make(ref).start())


def pick_kernel(picks, *refs):
    pieces, (out, sem) = refs[:8], refs[8:]
    copies = [
        pltpu.make_async_copy(
            piece.at[pl.ds(pl.multiple_of(picks[d] * BS, BS), BS)], out.at[d], sem.at[d]
        )
        for d, piece in enumerate(pieces)
    ]
    for copy in copies:
        copy.start()
    for copy in copies:
        copy.wait()


def pick_call(picks, pieces):
    n = pieces[0].shape[1]
    return pl.pallas_call(
        pick_kernel,
        out_shape=jax.ShapeDtypeStruct((8, BS, n), jnp.float32),
        in_specs=[SMEM] + [ANY] * 8,
        out_specs=VMEM,
        scratch_shapes=[pltpu.SemaphoreType.DMA((8,))],
        compiler_params=pltpu.CompilerParams(vmem_limit_bytes=12 * MIB),
        cost_estimate=SMALL,
        name="pick",
    )(picks, *pieces)


def alpha_kernel(plan, *refs):
    pieces, picked, own, refs = refs[:8], refs[8], refs[9], refs[10:]
    out, data, tiles, data_sem, tile_sem = refs
    count = plan[0, 0]

    def tile_of(k, slot):
        return pltpu.make_async_copy(own.at[slot >> 3, slot & 7], tiles.at[k], tile_sem.at[k])

    def rows_of(k, ref):
        return pltpu.make_async_copy(ref, data.at[k], data_sem.at[k])

    def fetch(k, _):
        word = plan[0, k + 1]
        piece = word >> 6
        tile_of(k, word & 31).start()
        rows = pl.ds(pl.multiple_of(((word >> 5) & 1) * BS, BS), BS)
        start_one_of(pieces, piece, lambda ref: rows_of(k, ref.at[rows]))
        pl.when(piece >= 8)(lambda: rows_of(k, picked.at[piece & 7]).start())
        return 0

    lax.fori_loop(0, count, fetch, 0)
    out[...] = jnp.zeros_like(out)

    def product(k, _):
        slot = plan[0, k + 1] & 31
        tile_of(k, slot).wait()
        rows_of(k, picked.at[0]).wait()
        rows = pl.multiple_of((slot >> 3) * BS, BS)
        out[pl.ds(rows, BS), :] += dot3(tiles[k], data[k])
        return 0

    lax.fori_loop(0, count, product, 0)


def alpha_call(plan, pieces, picked, own):
    n = own.shape[0] * BS
    return pl.pallas_call(
        alpha_kernel,
        out_shape=jax.ShapeDtypeStruct((n, n), jnp.float32),
        in_specs=[SMEM] + [HBM] * 10,
        out_specs=VMEM,
        scratch_shapes=[
            pltpu.VMEM((2 * SLOTS, BS, n), jnp.float32),
            pltpu.VMEM((2 * SLOTS, BS, BS), jnp.float32),
            pltpu.SemaphoreType.DMA((2 * SLOTS,)),
            pltpu.SemaphoreType.DMA((2 * SLOTS,)),
        ],
        compiler_params=pltpu.CompilerParams(vmem_limit_bytes=18 * MIB),
        cost_estimate=SMALL,
        name="alpha",
    )(plan, *in_hbm(*pieces, picked, own))


def send_kernel(where, sends, own, out, sem):
    copies = []
    for i in range(SLOTS // 2):
        slot = sends[(where[0] & 1) * (SLOTS // 2) + i]
        copies.append(
            pltpu.make_async_copy(own.at[slot >> 3, slot & 7], out.at[i], sem.at[i])
        )
    for copy in copies:
        copy.start()
    for copy in copies:
        copy.wait()


def send_call(where, sends, own):
    return pl.pallas_call(
        send_kernel,
        out_shape=jax.ShapeDtypeStruct((SLOTS // 2, BS, BS), jnp.float32),
        in_specs=[SMEM] * 2 + [HBM],
        out_specs=VMEM,
        scratch_shapes=[pltpu.SemaphoreType.DMA((SLOTS // 2,))],
        cost_estimate=SMALL,
        name="send",
    )(where, sends, *in_hbm(own))


HOPS = {(0, 0): (0, 1, 2, 6, 7), (0, 1): (0, 1, 2, 6, 7), (1, 0): (3, 4, 5), (1, 1): (3, 5), (2, 1): (4,)}


def beta_kernel(call, targets, where, plan, *refs):
    numbers = HOPS[call, targets[0]]
    pieces, refs = refs[: len(numbers)], refs[len(numbers) :]
    own, got, other, refs = refs[0], refs[1], refs[2], refs[3:]
    before, refs = (refs[: len(targets)], refs[len(targets) :]) if call == 1 else ((), refs)
    outs, (data, tiles, data_sem, tile_sem, out_sem) = refs[: len(targets)], refs[len(targets) :]
    core = where[0] & 1
    firsts = [
        pltpu.make_async_copy(b, out, out_sem.at[i]) for i, (b, out) in enumerate(zip(before, outs))
    ]
    for first in firsts:
        first.start()

    def columns_of(k, ref, block):
        first = pl.multiple_of(block * BS, BS)
        return pltpu.make_async_copy(ref.at[:, pl.ds(first, BS)], data.at[k], data_sem.at[k])

    def tile_from(k, ref):
        return pltpu.make_async_copy(ref, tiles.at[k], tile_sem.at[k])

    base = 0
    for target in targets:
        row = 2 * call + target

        def fetch(j, _, target=target, row=row, base=base):
            word = plan[row, j + 1]
            k = base + j
            tile = word & 15
            for number, ref in zip(numbers, pieces):
                pl.when((word >> 6) == number)(
                    lambda ref=ref: columns_of(k, ref, (word >> 5) & 1).start()
                )
            if target == 0:
                tile_from(k, own.at[(word >> 4) & 1, tile]).start()
            else:
                start_one_of(
                    (got, other), core ^ (tile >> 2), lambda ref: tile_from(k, ref.at[tile & 3])
                )
            return 0

        lax.fori_loop(0, plan[row, 0], fetch, 0)
        base = base + plan[row, 0]
    for out in outs:
        if call != 1:
            out[...] = jnp.zeros_like(out)
    for first in firsts:
        first.wait()
    base = 0
    for target, out in zip(targets, outs):
        row = 2 * call + target

        def product(j, _, out=out, row=row, base=base):
            k = base + j
            block = (plan[row, j + 1] >> 4) & 1
            columns_of(k, pieces[0], 0).wait()
            tile_from(k, own.at[0, 0]).wait()
            columns = 0 if call == 2 else pl.multiple_of(block * BS, BS)
            out[:, pl.ds(columns, BS)] += dot3(data[k], tiles[k])
            return 0

        lax.fori_loop(0, plan[row, 0], product, 0)
        base = base + plan[row, 0]


def beta_call(call, targets, where, plan, held, own, got, other, before=()):
    n = held[0].shape[0]
    pieces = [held[d] for d in HOPS[call, targets[0]]]
    most = len(pieces) * len(targets)
    width = BS if call == 2 else n
    return pl.pallas_call(
        functools.partial(beta_kernel, call, targets),
        out_shape=[jax.ShapeDtypeStruct((n, width), jnp.float32)] * len(targets),
        in_specs=[SMEM] * 2 + [HBM] * (len(pieces) + 3) + [ANY] * len(before),
        out_specs=[VMEM] * len(targets),
        scratch_shapes=[
            pltpu.VMEM((most, n, BS), jnp.float32),
            pltpu.VMEM((most, BS, BS), jnp.float32),
            pltpu.SemaphoreType.DMA((most,)),
            pltpu.SemaphoreType.DMA((most,)),
            pltpu.SemaphoreType.DMA((2,)),
        ],
        compiler_params=pltpu.CompilerParams(vmem_limit_bytes=16 * MIB),
        cost_estimate=(pl.CostEstimate(flops=1 << 34, bytes_accessed=1 << 25, transcendentals=0) if call else SMALL),
        name=f"beta{call}{len(targets)}",
    )(where, plan, *in_hbm(*pieces, own, got, other), *before)


def per_device(
    coeffs,
    diag_alpha,
    diag_beta,
    alpha_tiles,
    beta_tiles,
    alpha_source,
    alpha_live,
    beta_source,
    beta_live,
):
    where = jnp.stack([lax.axis_index(ALPHA), lax.axis_index(BETA)]).astype(jnp.int32)
    f1, b1 = step(coeffs, "z"), step(coeffs, "z", -1)
    uf, ub = step(coeffs, "x"), step(coeffs, "x", -1)
    v = swap(coeffs, "yhi")
    alpha_plan, beta_plan, picks, sends = pl.pallas_call(
        plan_kernel,
        out_shape=[
            jax.ShapeDtypeStruct((1, 32), jnp.int32),
            jax.ShapeDtypeStruct((6, 32), jnp.int32),
            jax.ShapeDtypeStruct((8,), jnp.int32),
            jax.ShapeDtypeStruct((SLOTS,), jnp.int32),
        ],
        in_specs=[SMEM] * 5,
        out_specs=[SMEM] * 4,
        name="plan",
    )(where, alpha_source, alpha_live, beta_source, beta_live)
    tiles = send_call(where, sends, beta_tiles)
    f1, b1, tiles = lax.optimization_barrier((f1, b1, tiles))
    f2, b2 = step(f1, "z"), step(b1, "z", -1)
    uf, ub, v = lax.optimization_barrier((uf, ub, v, f1))[:3]
    vf, vb = step(v, "x"), step(v, "x", -1)
    got = swap(after(tiles, v), "ylo")
    f2, b2 = lax.optimization_barrier((f2, b2))
    f3, b3 = step(f2, "z"), step(b2, "z", -1)
    vf, vb, got, uf = lax.optimization_barrier((vf, vb, got, uf, f2))[:4]
    u2, v2 = step(uf, "x"), step(vf, "x")
    other = swap(got, "core")
    held = [coeffs, f1, f2, None, None, None, b2, b1]
    beta_own, beta_par = beta_call(0, (0, 1), where, beta_plan, held, beta_tiles, got, other)
    f3, b3, beta_own, beta_par = lax.optimization_barrier((f3, b3, beta_own, beta_par))
    held[3], held[4], held[5] = f3, step(f3, "z"), b3
    (beta_par,) = beta_call(
        1, (1,), where, beta_plan, held, beta_tiles, got, other, [beta_par]
    )
    beta_other = swap(beta_par, "ylo")
    pieces = [coeffs, uf, u2, ub, v, vf, v2, vb]
    picked = swap(pick_call(after(picks, beta_par), pieces), "core")
    (far,) = beta_call(2, (1,), where, beta_plan, held, beta_tiles, got, other)
    far_other = swap(far, "ylo")
    alpha = alpha_call(alpha_plan, pieces, picked, after(alpha_tiles, far))
    (beta_own,) = beta_call(
        1, (0,), where, beta_plan, held, after(beta_tiles, far), got, other, [beta_own]
    )
    joined = (diag_alpha[:, None] + diag_beta[None, :]) * coeffs + alpha + beta_own
    joined, place = lax.optimization_barrier((joined, (where[1] + 4) & 7))
    joined = lax.optimization_barrier(joined + beta_other)
    block = lax.dynamic_index_in_dim(sends, place, 0, keepdims=False) >> 3
    zero = jnp.zeros_like(far_other)
    low = jnp.where(block == 0, far_other, zero)
    high = jnp.where(block == 0, zero, far_other)
    return joined + jnp.concatenate([low, high], axis=1)


def solution(mesh):
    parts = Mesh(mesh.devices.reshape(SIZES), AXES)
    return jax.shard_map(
        per_device,
        mesh=parts,
        in_specs=(
            P(ALPHA, BETA),
            P(ALPHA),
            P(BETA),
            P(ALPHA, None, None, None),
            P(BETA, None, None, None),
            P(),
            P(),
            P(),
            P(),
        ),
        out_specs=P(ALPHA, BETA),
        check_vma=False,
    )
```

```python
import functools

import jax
import jax.numpy as jnp
from jax import lax
from jax.experimental import pallas as pl
from jax.experimental.pallas import tpu as pltpu
from jax.sharding import Mesh
from jax.sharding import PartitionSpec as P

AXES = ("yhi", "x", "core", "ylo", "z")
SIZES = (2, 4, 2, 2, 8)
ALPHA = ("yhi", "x", "core")
BETA = ("ylo", "z")
BS = 256
SLOTS = 8
MIB = 1 << 20
LARGE = pl.CostEstimate(flops=1 << 34, bytes_accessed=1 << 25, transcendentals=0)
SMALL = pl.CostEstimate(flops=1 << 20, bytes_accessed=1 << 18, transcendentals=0)

SMEM = pl.BlockSpec(memory_space=pltpu.SMEM)
HBM = pl.BlockSpec(memory_space=pltpu.HBM)
ANY = pl.BlockSpec(memory_space=pl.ANY)
VMEM = pl.BlockSpec(memory_space=pltpu.VMEM)


def swap(value, axis):
    return lax.ppermute(value, axis, [(0, 1), (1, 0)])


def step(value, axis, way=1):
    n = lax.axis_size(axis)
    if axis == "z":
        pairs = [(i, (i + way) % n) for i in range(n)]
        pairs += [(n + i, n + (i - way) % n) for i in range(n)]
        return lax.ppermute(value, ("core", axis), pairs)
    pairs = [(2 * i, 2 * ((i + way) % n)) for i in range(n)]
    pairs += [(2 * i + 1, 2 * ((i - way) % n) + 1) for i in range(n)]
    return lax.ppermute(value, (axis, "core"), pairs)


def in_hbm(*values):
    return [pltpu.with_memory_space_constraint(value, pltpu.HBM) for value in values]


def after(value, *earlier):
    return lax.optimization_barrier((value, *earlier))[0]


def dot3(a, b):
    a_hi = a.astype(jnp.bfloat16)
    b_hi = b.astype(jnp.bfloat16)
    a_lo = (a - a_hi.astype(jnp.float32)).astype(jnp.bfloat16)
    b_lo = (b - b_hi.astype(jnp.float32)).astype(jnp.bfloat16)
    dot = functools.partial(jnp.dot, preferred_element_type=jnp.float32)
    return dot(a_hi, b_hi) + (dot(a_hi, b_lo) + dot(a_lo, b_hi))


def plan_kernel(
    where, alpha_source, alpha_live, beta_source, beta_live, alpha_plan, beta_plan, picks, sends
):
    me, mb = where[0], where[1]
    up = (me & 1) == 0
    alpha_plan[0, 0] = 0
    for row in range(3):
        beta_plan[row, 0] = 0

    def put(plan, row, word):
        count = plan[row, 0] + 1
        plan[row, 0] = count
        plan[row, count] = word

    def alpha(slot, _):
        row, c = 2 * me + (slot >> 3), slot & 7

        @pl.when(alpha_live[row, c] > 0)
        def _():
            src = alpha_source[row, c]
            owner = src >> 1
            ahead = (me >> 1) - (owner >> 1)
            hops = jnp.where((owner & 1) == 0, ahead, -ahead) & 3
            piece = hops + 4 * ((owner >> 3) ^ (me >> 3)) + 8 * ((owner ^ me) & 1)
            put(alpha_plan, 0, piece * 64 + (src & 1) * 32 + slot)

        src = alpha_source[2 * (me ^ 1) + (slot >> 3), c]
        owner = src >> 1

        @pl.when(((owner ^ me) & 1) == 0)
        def _():
            ahead = (me >> 1) - (owner >> 1)
            picks[4 * ((owner >> 3) ^ (me >> 3)) + (jnp.where(up, ahead, -ahead) & 3)] = src & 1

        return 0

    def beta(target, slot, _):
        row, c = 2 * (mb ^ (8 * target)) + (slot >> 3), slot & 7
        src = beta_source[row, c]
        owner = src >> 1
        near = (owner >> 3) == (mb >> 3)
        place = owner & 7

        @pl.when(near & (beta_live[row, c] > 0))
        def _():
            ahead = mb - owner
            d = jnp.where(up, ahead, -ahead) & 7
            call = jnp.where(d == 4, 2, 1) if target else 0
            tile = place if target else c
            word = d * 64 + (src & 1) * 32 + (slot >> 3) * 16 + tile
            put(beta_plan, call, word)

        if not target:

            @pl.when(jnp.logical_not(near))
            def _():
                sends[place] = slot

        return 0

    lax.fori_loop(0, 2 * SLOTS, alpha, 0)
    for target in range(2):
        lax.fori_loop(0, 2 * SLOTS, functools.partial(beta, target), 0)


def start_one_of(pieces, piece, make):
    for i, ref in enumerate(pieces):
        pl.when(piece == i)(lambda ref=ref: make(ref).start())


SOON = (0, 1, 3, 4, 5, 7)


def pick_kernel(picks, *refs):
    pieces, (out, sem) = refs[:6], refs[6:]
    copies = [
        pltpu.make_async_copy(
            piece.at[pl.ds(pl.multiple_of(picks[d] * BS, BS), BS)], out.at[i], sem.at[i]
        )
        for i, (d, piece) in enumerate(zip(SOON, pieces))
    ]
    for copy in copies:
        copy.start()
    for copy in copies:
        copy.wait()


def pick_call(picks, pieces):
    n = pieces[0].shape[1]
    return pl.pallas_call(
        pick_kernel,
        out_shape=jax.ShapeDtypeStruct((6, BS, n), jnp.float32),
        in_specs=[SMEM] + [ANY] * 6,
        out_specs=VMEM,
        scratch_shapes=[pltpu.SemaphoreType.DMA((6,))],
        compiler_params=pltpu.CompilerParams(vmem_limit_bytes=12 * MIB),
        cost_estimate=SMALL,
        name="pick",
    )(picks, *pieces)


def alpha_kernel(plan, *refs):
    pieces, (us2, vs2, picked, own), refs = refs[:8], refs[8:12], refs[12:]
    out, data, tiles, data_sem, tile_sem = refs
    count = plan[0, 0]

    def tile_of(k, slot):
        return pltpu.make_async_copy(own.at[slot >> 3, slot & 7], tiles.at[k], tile_sem.at[k])

    def rows_of(k, ref):
        return pltpu.make_async_copy(ref, data.at[k], data_sem.at[k])

    def fetch(k, _):
        word = plan[0, k + 1]
        piece = word >> 6
        tile_of(k, word & 31).start()
        rows = pl.ds(pl.multiple_of(((word >> 5) & 1) * BS, BS), BS)
        start_one_of(pieces, piece, lambda ref: rows_of(k, ref.at[rows]))
        pl.when(piece == 10)(lambda: rows_of(k, us2.at[rows]).start())
        pl.when(piece == 14)(lambda: rows_of(k, vs2.at[rows]).start())
        place = (piece & 7) - (piece > 10).astype(jnp.int32) - (piece > 14).astype(jnp.int32)
        pl.when((piece >= 8) & (piece != 10) & (piece != 14))(
            lambda: rows_of(k, picked.at[place]).start()
        )
        return 0

    lax.fori_loop(0, count, fetch, 0)
    out[...] = jnp.zeros_like(out)

    def product(k, _):
        slot = plan[0, k + 1] & 31
        tile_of(k, slot).wait()
        rows_of(k, picked.at[0]).wait()
        rows = pl.multiple_of((slot >> 3) * BS, BS)
        out[pl.ds(rows, BS), :] += dot3(tiles[k], data[k])
        return 0

    lax.fori_loop(0, count, product, 0)


def alpha_call(plan, pieces, us2, vs2, picked, own):
    n = own.shape[0] * BS
    return pl.pallas_call(
        alpha_kernel,
        out_shape=jax.ShapeDtypeStruct((n, n), jnp.float32),
        in_specs=[SMEM] + [HBM] * 12,
        out_specs=VMEM,
        scratch_shapes=[
            pltpu.VMEM((2 * SLOTS, BS, n), jnp.float32),
            pltpu.VMEM((2 * SLOTS, BS, BS), jnp.float32),
            pltpu.SemaphoreType.DMA((2 * SLOTS,)),
            pltpu.SemaphoreType.DMA((2 * SLOTS,)),
        ],
        compiler_params=pltpu.CompilerParams(vmem_limit_bytes=18 * MIB),
        cost_estimate=SMALL,
        name="alpha",
    )(plan, *in_hbm(*pieces, us2, vs2, picked, own))


def send_kernel(where, sends, own, out, sem):
    copies = []
    for i in range(SLOTS // 2):
        slot = sends[(where[0] & 1) * (SLOTS // 2) + i]
        copies.append(
            pltpu.make_async_copy(own.at[slot >> 3, slot & 7], out.at[i], sem.at[i])
        )
    for copy in copies:
        copy.start()
    for copy in copies:
        copy.wait()


def send_call(where, sends, own):
    return pl.pallas_call(
        send_kernel,
        out_shape=jax.ShapeDtypeStruct((SLOTS // 2, BS, BS), jnp.float32),
        in_specs=[SMEM] * 2 + [HBM],
        out_specs=VMEM,
        scratch_shapes=[pltpu.SemaphoreType.DMA((SLOTS // 2,))],
        cost_estimate=SMALL,
        name="send",
    )(where, sends, *in_hbm(own))


HOPS = (tuple(range(8)), (0, 1, 2, 3, 5, 6, 7), (4,))


def beta_kernel(call, where, plan, *refs):
    numbers = HOPS[call]
    pieces, refs = refs[: len(numbers)], refs[len(numbers) :]
    own, got, other, out, data, tiles, data_sem, tile_sem = refs
    core = where[0] & 1
    count = plan[call, 0]

    def columns_of(k, ref, block):
        first = pl.multiple_of(block * BS, BS)
        return pltpu.make_async_copy(ref.at[:, pl.ds(first, BS)], data.at[k], data_sem.at[k])

    def tile_from(k, ref):
        return pltpu.make_async_copy(ref, tiles.at[k], tile_sem.at[k])

    def fetch(k, _):
        word = plan[call, k + 1]
        tile = word & 15
        for number, ref in zip(numbers, pieces):
            pl.when((word >> 6) == number)(
                lambda ref=ref: columns_of(k, ref, (word >> 5) & 1).start()
            )
        if call == 0:
            tile_from(k, own.at[(word >> 4) & 1, tile]).start()
        else:
            start_one_of(
                (got, other), core ^ (tile >> 2), lambda ref: tile_from(k, ref.at[tile & 3])
            )
        return 0

    lax.fori_loop(0, count, fetch, 0)
    out[...] = jnp.zeros_like(out)

    def product(k, _):
        block = (plan[call, k + 1] >> 4) & 1
        columns_of(k, pieces[0], 0).wait()
        tile_from(k, own.at[0, 0]).wait()
        columns = 0 if call == 2 else pl.multiple_of(block * BS, BS)
        out[:, pl.ds(columns, BS)] += dot3(data[k], tiles[k])
        return 0

    lax.fori_loop(0, count, product, 0)


def beta_call(call, where, plan, held, own, got, other):
    n = held[0].shape[0]
    pieces = [held[d] for d in HOPS[call]]
    return pl.pallas_call(
        functools.partial(beta_kernel, call),
        out_shape=jax.ShapeDtypeStruct((n, BS if call == 2 else n), jnp.float32),
        in_specs=[SMEM] * 2 + [HBM] * (len(pieces) + 3),
        out_specs=VMEM,
        scratch_shapes=[
            pltpu.VMEM((len(pieces), n, BS), jnp.float32),
            pltpu.VMEM((len(pieces), BS, BS), jnp.float32),
            pltpu.SemaphoreType.DMA((len(pieces),)),
            pltpu.SemaphoreType.DMA((len(pieces),)),
        ],
        compiler_params=pltpu.CompilerParams(vmem_limit_bytes=12 * MIB),
        cost_estimate=LARGE,
        name=f"beta{call}",
    )(where, plan, *in_hbm(*pieces, own, got, other))


def per_device(
    coeffs,
    diag_alpha,
    diag_beta,
    alpha_tiles,
    beta_tiles,
    alpha_source,
    alpha_live,
    beta_source,
    beta_live,
):
    where = jnp.stack([lax.axis_index(ALPHA), lax.axis_index(BETA)]).astype(jnp.int32)
    f1, b1 = step(coeffs, "z"), step(coeffs, "z", -1)
    uf, ub = step(coeffs, "x"), step(coeffs, "x", -1)
    v = swap(coeffs, "yhi")
    alpha_plan, beta_plan, picks, sends = pl.pallas_call(
        plan_kernel,
        out_shape=[
            jax.ShapeDtypeStruct((1, 32), jnp.int32),
            jax.ShapeDtypeStruct((3, 32), jnp.int32),
            jax.ShapeDtypeStruct((8,), jnp.int32),
            jax.ShapeDtypeStruct((SLOTS,), jnp.int32),
        ],
        in_specs=[SMEM] * 5,
        out_specs=[SMEM] * 4,
        name="plan",
    )(where, alpha_source, alpha_live, beta_source, beta_live)
    tiles = send_call(where, sends, beta_tiles)
    f1, b1, tiles = lax.optimization_barrier((f1, b1, tiles))
    f2, b2 = step(f1, "z"), step(b1, "z", -1)
    uf, ub, v = lax.optimization_barrier((uf, ub, v, f1))[:3]
    vf, vb = step(v, "x"), step(v, "x", -1)
    got = swap(after(tiles, v), "ylo")
    f2, b2 = lax.optimization_barrier((f2, b2))
    f3, b3 = step(f2, "z"), step(b2, "z", -1)
    vf, vb, got, uf = lax.optimization_barrier((vf, vb, got, uf, f2))[:4]
    u2, v2 = step(uf, "x"), step(vf, "x")
    other = swap(got, "core")
    picked = pick_call(picks, [coeffs, uf, ub, v, vf, vb])
    f3, b3, picked = lax.optimization_barrier((f3, b3, picked))
    picked = swap(picked, "core")
    held = [coeffs, f1, f2, f3, step(f3, "z"), b3, b2, b1]
    beta_par = beta_call(1, where, beta_plan, held, beta_tiles, got, other)
    beta_other = swap(beta_par, "ylo")
    pieces = [coeffs, uf, u2, ub, v, vf, v2, vb]
    us2, vs2 = swap(after(u2, beta_par), "core"), swap(after(v2, beta_par), "core")
    far = beta_call(2, where, beta_plan, held, beta_tiles, got, other)
    far_other = swap(far, "ylo")
    alpha = alpha_call(alpha_plan, pieces, us2, vs2, picked, after(alpha_tiles, far))
    beta_own = beta_call(0, where, beta_plan, held, after(beta_tiles, far), got, other)
    joined = (diag_alpha[:, None] + diag_beta[None, :]) * coeffs + alpha + beta_own
    joined, place = lax.optimization_barrier((joined, (where[1] + 4) & 7))
    joined = lax.optimization_barrier(joined + beta_other)
    block = lax.dynamic_index_in_dim(sends, place, 0, keepdims=False) >> 3
    zero = jnp.zeros_like(far_other)
    low = jnp.where(block == 0, far_other, zero)
    high = jnp.where(block == 0, zero, far_other)
    return joined + jnp.concatenate([low, high], axis=1)


def solution(mesh):
    parts = Mesh(mesh.devices.reshape(SIZES), AXES)
    return jax.shard_map(
        per_device,
        mesh=parts,
        in_specs=(
            P(ALPHA, BETA),
            P(ALPHA),
            P(BETA),
            P(ALPHA, None, None, None),
            P(BETA, None, None, None),
            P(),
            P(),
            P(),
            P(),
        ),
        out_specs=P(ALPHA, BETA),
        check_vma=False,
    )
```

```python
import functools

import jax
import jax.numpy as jnp
from jax import lax
from jax.experimental import pallas as pl
from jax.experimental.pallas import tpu as pltpu
from jax.sharding import Mesh
from jax.sharding import PartitionSpec as P

AXES = ("yhi", "x", "core", "ylo", "z")
SIZES = (2, 4, 2, 2, 8)
ALPHA = ("yhi", "x", "core")
BETA = ("ylo", "z")
BS = 256
SLOTS = 8
MIB = 1 << 20
LARGE = pl.CostEstimate(flops=1 << 34, bytes_accessed=1 << 25, transcendentals=0)
SMALL = pl.CostEstimate(flops=1 << 20, bytes_accessed=1 << 18, transcendentals=0)

SMEM = pl.BlockSpec(memory_space=pltpu.SMEM)
HBM = pl.BlockSpec(memory_space=pltpu.HBM)
ANY = pl.BlockSpec(memory_space=pl.ANY)
VMEM = pl.BlockSpec(memory_space=pltpu.VMEM)


def swap(value, axis):
    return lax.ppermute(value, axis, [(0, 1), (1, 0)])


def step(value, axis, way=1):
    n = lax.axis_size(axis)
    if axis == "z":
        pairs = [(i, (i + way) % n) for i in range(n)]
        pairs += [(n + i, n + (i - way) % n) for i in range(n)]
        return lax.ppermute(value, ("core", axis), pairs)
    pairs = [(2 * i, 2 * ((i + way) % n)) for i in range(n)]
    pairs += [(2 * i + 1, 2 * ((i - way) % n) + 1) for i in range(n)]
    return lax.ppermute(value, (axis, "core"), pairs)


def in_hbm(*values):
    return [pltpu.with_memory_space_constraint(value, pltpu.HBM) for value in values]


def after(value, *earlier):
    return lax.optimization_barrier((value, *earlier))[0]


def dot3(a, b):
    a_hi = a.astype(jnp.bfloat16)
    b_hi = b.astype(jnp.bfloat16)
    a_lo = (a - a_hi.astype(jnp.float32)).astype(jnp.bfloat16)
    b_lo = (b - b_hi.astype(jnp.float32)).astype(jnp.bfloat16)
    dot = functools.partial(jnp.dot, preferred_element_type=jnp.float32)
    return dot(a_hi, b_hi) + (dot(a_hi, b_lo) + dot(a_lo, b_hi))


def plan_kernel(
    where, alpha_source, alpha_live, beta_source, beta_live, alpha_plan, beta_plan, picks, sends
):
    me, mb = where[0], where[1]
    up = (me & 1) == 0
    alpha_plan[0, 0] = 0
    for row in range(3):
        beta_plan[row, 0] = 0

    def put(plan, row, word):
        count = plan[row, 0] + 1
        plan[row, 0] = count
        plan[row, count] = word

    def alpha(slot, _):
        row, c = 2 * me + (slot >> 3), slot & 7

        @pl.when(alpha_live[row, c] > 0)
        def _():
            src = alpha_source[row, c]
            owner = src >> 1
            ahead = (me >> 1) - (owner >> 1)
            hops = jnp.where((owner & 1) == 0, ahead, -ahead) & 3
            piece = hops + 4 * ((owner >> 3) ^ (me >> 3)) + 8 * ((owner ^ me) & 1)
            put(alpha_plan, 0, piece * 64 + (src & 1) * 32 + slot)

        src = alpha_source[2 * (me ^ 1) + (slot >> 3), c]
        owner = src >> 1

        @pl.when(((owner ^ me) & 1) == 0)
        def _():
            ahead = (me >> 1) - (owner >> 1)
            picks[4 * ((owner >> 3) ^ (me >> 3)) + (jnp.where(up, ahead, -ahead) & 3)] = src & 1

        return 0

    def beta(target, slot, _):
        row, c = 2 * (mb ^ (8 * target)) + (slot >> 3), slot & 7
        src = beta_source[row, c]
        owner = src >> 1
        near = (owner >> 3) == (mb >> 3)
        place = owner & 7

        @pl.when(near & (beta_live[row, c] > 0))
        def _():
            ahead = mb - owner
            d = jnp.where(up, ahead, -ahead) & 7
            call = jnp.where(d == 4, 2, 1) if target else 0
            tile = place if target else c
            word = d * 64 + (src & 1) * 32 + (slot >> 3) * 16 + tile
            put(beta_plan, call, word)

        if not target:

            @pl.when(jnp.logical_not(near))
            def _():
                sends[place] = slot

        return 0

    lax.fori_loop(0, 2 * SLOTS, alpha, 0)
    for target in range(2):
        lax.fori_loop(0, 2 * SLOTS, functools.partial(beta, target), 0)


def start_one_of(pieces, piece, make):
    for i, ref in enumerate(pieces):
        pl.when(piece == i)(lambda ref=ref: make(ref).start())


SOON = (0, 1, 3, 4, 5, 7)


def pick_kernel(picks, *refs):
    pieces, (out, sem) = refs[:6], refs[6:]
    copies = [
        pltpu.make_async_copy(
            piece.at[pl.ds(pl.multiple_of(picks[d] * BS, BS), BS)], out.at[i], sem.at[i]
        )
        for i, (d, piece) in enumerate(zip(SOON, pieces))
    ]
    for copy in copies:
        copy.start()
    for copy in copies:
        copy.wait()


def pick_call(picks, pieces):
    n = pieces[0].shape[1]
    return pl.pallas_call(
        pick_kernel,
        out_shape=jax.ShapeDtypeStruct((6, BS, n), jnp.float32),
        in_specs=[SMEM] + [ANY] * 6,
        out_specs=VMEM,
        scratch_shapes=[pltpu.SemaphoreType.DMA((6,))],
        compiler_params=pltpu.CompilerParams(vmem_limit_bytes=12 * MIB),
        cost_estimate=SMALL,
        name="pick",
    )(picks, *pieces)


def alpha_kernel(plan, *refs):
    pieces, (us2, vs2, picked, own), refs = refs[:8], refs[8:12], refs[12:]
    out, data, tiles, data_sem, tile_sem = refs
    count = plan[0, 0]

    def tile_of(k, slot):
        return pltpu.make_async_copy(own.at[slot >> 3, slot & 7], tiles.at[k], tile_sem.at[k])

    def rows_of(k, ref):
        return pltpu.make_async_copy(ref, data.at[k], data_sem.at[k])

    def fetch(k, _):
        word = plan[0, k + 1]
        piece = word >> 6
        tile_of(k, word & 31).start()
        rows = pl.ds(pl.multiple_of(((word >> 5) & 1) * BS, BS), BS)
        start_one_of(pieces, piece, lambda ref: rows_of(k, ref.at[rows]))
        pl.when(piece == 10)(lambda: rows_of(k, us2.at[rows]).start())
        pl.when(piece == 14)(lambda: rows_of(k, vs2.at[rows]).start())
        place = (piece & 7) - (piece > 10).astype(jnp.int32) - (piece > 14).astype(jnp.int32)
        pl.when((piece >= 8) & (piece != 10) & (piece != 14))(
            lambda: rows_of(k, picked.at[place]).start()
        )
        return 0

    lax.fori_loop(0, count, fetch, 0)
    out[...] = jnp.zeros_like(out)

    def product(k, _):
        slot = plan[0, k + 1] & 31
        tile_of(k, slot).wait()
        rows_of(k, picked.at[0]).wait()
        rows = pl.multiple_of((slot >> 3) * BS, BS)
        out[pl.ds(rows, BS), :] += dot3(tiles[k], data[k])
        return 0

    lax.fori_loop(0, count, product, 0)


def alpha_call(plan, pieces, us2, vs2, picked, own):
    n = own.shape[0] * BS
    return pl.pallas_call(
        alpha_kernel,
        out_shape=jax.ShapeDtypeStruct((n, n), jnp.float32),
        in_specs=[SMEM] + [HBM] * 12,
        out_specs=VMEM,
        scratch_shapes=[
            pltpu.VMEM((2 * SLOTS, BS, n), jnp.float32),
            pltpu.VMEM((2 * SLOTS, BS, BS), jnp.float32),
            pltpu.SemaphoreType.DMA((2 * SLOTS,)),
            pltpu.SemaphoreType.DMA((2 * SLOTS,)),
        ],
        compiler_params=pltpu.CompilerParams(vmem_limit_bytes=18 * MIB),
        cost_estimate=SMALL,
        name="alpha",
    )(plan, *in_hbm(*pieces, us2, vs2, picked, own))


def send_kernel(where, sends, own, out, sem):
    copies = []
    for i in range(SLOTS // 2):
        slot = sends[(where[0] & 1) * (SLOTS // 2) + i]
        copies.append(
            pltpu.make_async_copy(own.at[slot >> 3, slot & 7], out.at[i], sem.at[i])
        )
    for copy in copies:
        copy.start()
    for copy in copies:
        copy.wait()


def send_call(where, sends, own):
    return pl.pallas_call(
        send_kernel,
        out_shape=jax.ShapeDtypeStruct((SLOTS // 2, BS, BS), jnp.float32),
        in_specs=[SMEM] * 2 + [HBM],
        out_specs=VMEM,
        scratch_shapes=[pltpu.SemaphoreType.DMA((SLOTS // 2,))],
        cost_estimate=SMALL,
        name="send",
    )(where, sends, *in_hbm(own))


HOPS = (tuple(range(8)), (0, 1, 2, 3, 5, 6, 7), (4,))


def beta_kernel(call, where, plan, *refs):
    numbers = HOPS[call]
    pieces, refs = refs[: len(numbers)], refs[len(numbers) :]
    own, got, other, refs = refs[0], refs[1], refs[2], refs[3:]
    before, refs = (refs[0], refs[1:]) if call == 2 else (None, refs)
    outs, (data, tiles, data_sem, tile_sem, out_sem) = refs[:-5], refs[-5:]
    n, half = data.shape[1], data.shape[1] // 2
    if call == 2:
        first = pltpu.make_async_copy(before, outs[0].at[:, pl.ds(0, n)], out_sem)
        first.start()
    core = where[0] & 1
    count = plan[call, 0]

    def columns_of(k, ref, block):
        first = pl.multiple_of(block * BS, BS)
        return pltpu.make_async_copy(ref.at[:, pl.ds(first, BS)], data.at[k], data_sem.at[k])

    def tile_from(k, ref):
        return pltpu.make_async_copy(ref, tiles.at[k], tile_sem.at[k])

    def fetch(k, _):
        word = plan[call, k + 1]
        tile = word & 15
        for number, ref in zip(numbers, pieces):
            pl.when((word >> 6) == number)(
                lambda ref=ref: columns_of(k, ref, (word >> 5) & 1).start()
            )
        if call == 0:
            tile_from(k, own.at[(word >> 4) & 1, tile]).start()
        else:
            start_one_of(
                (got, other), core ^ (tile >> 2), lambda ref: tile_from(k, ref.at[tile & 3])
            )
        return 0

    lax.fori_loop(0, count, fetch, 0)
    if call == 2:
        outs[0][:, n:] = jnp.zeros((half, BS), jnp.float32)
        first.wait()
    else:
        for out in outs:
            out[...] = jnp.zeros_like(out)

    def product(k, _):
        block = (plan[call, k + 1] >> 4) & 1
        columns_of(k, pieces[0], 0).wait()
        tile_from(k, own.at[0, 0]).wait()
        columns = pl.ds(pl.multiple_of(block * BS, BS), BS)
        if call == 0:
            outs[0][:, columns] += dot3(data[k], tiles[k])
        elif call == 1:
            outs[0][:, columns] += dot3(data[k, :half], tiles[k])
            outs[1][:, columns] += dot3(data[k, half:], tiles[k])
        else:
            outs[0][:, n:] += dot3(data[k, :half], tiles[k])
            outs[0][:, columns] += dot3(data[k, half:], tiles[k])
        return 0

    lax.fori_loop(0, count, product, 0)


def beta_call(call, where, plan, held, own, got, other, before=()):
    n = held[0].shape[0]
    pieces = [held[d] for d in HOPS[call]]
    shapes = ([(n, n)], [(n // 2, n)] * 2, [(n // 2, n + BS)])[call]
    fixed = in_hbm(own, got, other)
    pieces = pieces if call == 2 else in_hbm(*pieces)
    return pl.pallas_call(
        functools.partial(beta_kernel, call),
        out_shape=[jax.ShapeDtypeStruct(shape, jnp.float32) for shape in shapes],
        in_specs=[SMEM] * 2 + [ANY] * (len(pieces) + 3 + len(before)),
        out_specs=[VMEM] * len(shapes),
        scratch_shapes=[
            pltpu.VMEM((len(pieces), n, BS), jnp.float32),
            pltpu.VMEM((len(pieces), BS, BS), jnp.float32),
            pltpu.SemaphoreType.DMA((len(pieces),)),
            pltpu.SemaphoreType.DMA((len(pieces),)),
            pltpu.SemaphoreType.DMA,
        ],
        compiler_params=pltpu.CompilerParams(vmem_limit_bytes=12 * MIB),
        cost_estimate=LARGE,
        name=f"beta{call}",
    )(where, plan, *pieces, *fixed, *before)


def last_kernel(where, sends, joined, top, rest, out, top_here, rest_here, sems):
    half, n = top.shape
    copies = [
        pltpu.make_async_copy(source, target, sems.at[i])
        for i, (source, target) in enumerate(((joined, out), (top, top_here), (rest, rest_here)))
    ]
    for copy in copies:
        copy.start()
    block = sends[(where[1] + 4) & 7] >> 3
    for copy in copies:
        copy.wait()
    out[:half] += top_here[...]
    out[half:] += rest_here[:, :n]
    out[:half, pl.ds(pl.multiple_of(block * BS, BS), BS)] += rest_here[:, n:]


def per_device(
    coeffs,
    diag_alpha,
    diag_beta,
    alpha_tiles,
    beta_tiles,
    alpha_source,
    alpha_live,
    beta_source,
    beta_live,
):
    n = coeffs.shape[0]
    where = jnp.stack([lax.axis_index(ALPHA), lax.axis_index(BETA)]).astype(jnp.int32)
    f1, b1 = step(coeffs, "z"), step(coeffs, "z", -1)
    uf, ub = step(coeffs, "x"), step(coeffs, "x", -1)
    v = swap(coeffs, "yhi")
    alpha_plan, beta_plan, picks, sends = pl.pallas_call(
        plan_kernel,
        out_shape=[
            jax.ShapeDtypeStruct((1, 32), jnp.int32),
            jax.ShapeDtypeStruct((3, 32), jnp.int32),
            jax.ShapeDtypeStruct((8,), jnp.int32),
            jax.ShapeDtypeStruct((SLOTS,), jnp.int32),
        ],
        in_specs=[SMEM] * 5,
        out_specs=[SMEM] * 4,
        name="plan",
    )(where, alpha_source, alpha_live, beta_source, beta_live)
    tiles = send_call(where, sends, beta_tiles)
    f1, b1, tiles = lax.optimization_barrier((f1, b1, tiles))
    f2, b2 = step(f1, "z"), step(b1, "z", -1)
    uf, ub, v = lax.optimization_barrier((uf, ub, v, f1))[:3]
    vf, vb = step(v, "x"), step(v, "x", -1)
    got = swap(after(tiles, v), "ylo")
    f2, b2 = lax.optimization_barrier((f2, b2))
    f3, b3 = step(f2, "z"), step(b2, "z", -1)
    vf, vb, got, uf = lax.optimization_barrier((vf, vb, got, uf, f2))[:4]
    u2, v2 = step(uf, "x"), step(vf, "x")
    other = swap(got, "core")
    picked = pick_call(picks, [coeffs, uf, ub, v, vf, vb])
    f3, b3, picked = lax.optimization_barrier((f3, b3, picked))
    picked = swap(picked, "core")
    held = [coeffs, f1, f2, f3, step(f3, "z"), b3, b2, b1]
    top, bottom = beta_call(1, where, beta_plan, held, beta_tiles, got, other)
    top_other = swap(top, "ylo")
    pieces = [coeffs, uf, u2, ub, v, vf, v2, vb]
    us2, vs2 = swap(after(u2, top), "core"), swap(after(v2, top), "core")
    (rest,) = beta_call(2, where, beta_plan, held, beta_tiles, got, other, [bottom])
    rest_other = swap(rest, "ylo")
    alpha = alpha_call(alpha_plan, pieces, us2, vs2, picked, after(alpha_tiles, rest))
    (beta_own,) = beta_call(0, where, beta_plan, held, after(beta_tiles, rest), got, other)
    joined = (diag_alpha[:, None] + diag_beta[None, :]) * coeffs + alpha + beta_own
    return pl.pallas_call(
        last_kernel,
        out_shape=jax.ShapeDtypeStruct((n, n), jnp.float32),
        in_specs=[SMEM] * 2 + [ANY] * 3,
        out_specs=VMEM,
        scratch_shapes=[
            pltpu.VMEM(top_other.shape, jnp.float32),
            pltpu.VMEM(rest_other.shape, jnp.float32),
            pltpu.SemaphoreType.DMA((3,)),
        ],
        compiler_params=pltpu.CompilerParams(vmem_limit_bytes=8 * MIB),
        cost_estimate=SMALL,
        name="last",
    )(where, sends, lax.optimization_barrier(joined), top_other, rest_other)


def solution(mesh):
    parts = Mesh(mesh.devices.reshape(SIZES), AXES)
    return jax.shard_map(
        per_device,
        mesh=parts,
        in_specs=(
            P(ALPHA, BETA),
            P(ALPHA),
            P(BETA),
            P(ALPHA, None, None, None),
            P(BETA, None, None, None),
            P(),
            P(),
            P(),
            P(),
        ),
        out_specs=P(ALPHA, BETA),
        check_vma=False,
    )
```

```python
import functools

import jax
import jax.numpy as jnp
from jax import lax
from jax.experimental import pallas as pl
from jax.experimental.pallas import tpu as pltpu
from jax.sharding import Mesh
from jax.sharding import PartitionSpec as P

AXES = ("yhi", "x", "core", "ylo", "z")
SIZES = (2, 4, 2, 2, 8)
ALPHA = ("yhi", "x", "core")
BETA = ("ylo", "z")
BS = 256
SLOTS = 8
MIB = 1 << 20
LARGE = pl.CostEstimate(flops=1 << 34, bytes_accessed=1 << 25, transcendentals=0)
SMALL = pl.CostEstimate(flops=1 << 20, bytes_accessed=1 << 18, transcendentals=0)

SMEM = pl.BlockSpec(memory_space=pltpu.SMEM)
HBM = pl.BlockSpec(memory_space=pltpu.HBM)
ANY = pl.BlockSpec(memory_space=pl.ANY)
VMEM = pl.BlockSpec(memory_space=pltpu.VMEM)


def swap(value, axis):
    return lax.ppermute(value, axis, [(0, 1), (1, 0)])


def step(value, axis, way=1):
    n = lax.axis_size(axis)
    if axis == "z":
        pairs = [(i, (i + way) % n) for i in range(n)]
        pairs += [(n + i, n + (i - way) % n) for i in range(n)]
        return lax.ppermute(value, ("core", axis), pairs)
    pairs = [(2 * i, 2 * ((i + way) % n)) for i in range(n)]
    pairs += [(2 * i + 1, 2 * ((i - way) % n) + 1) for i in range(n)]
    return lax.ppermute(value, (axis, "core"), pairs)


def in_hbm(*values):
    return [pltpu.with_memory_space_constraint(value, pltpu.HBM) for value in values]


def after(value, *earlier):
    return lax.optimization_barrier((value, *earlier))[0]


def dot3(a, b):
    a_hi = a.astype(jnp.bfloat16)
    b_hi = b.astype(jnp.bfloat16)
    a_lo = (a - a_hi.astype(jnp.float32)).astype(jnp.bfloat16)
    b_lo = (b - b_hi.astype(jnp.float32)).astype(jnp.bfloat16)
    dot = functools.partial(jnp.dot, preferred_element_type=jnp.float32)
    return dot(a_hi, b_hi) + (dot(a_hi, b_lo) + dot(a_lo, b_hi))


def plan_kernel(
    where, alpha_source, alpha_live, beta_source, beta_live, alpha_plan, beta_plan, picks, sends
):
    me, mb = where[0], where[1]
    up = (me & 1) == 0
    alpha_plan[0, 0] = 0
    for row in range(3):
        beta_plan[row, 0] = 0

    def put(plan, row, word):
        count = plan[row, 0] + 1
        plan[row, 0] = count
        plan[row, count] = word

    def alpha(slot, _):
        row, c = 2 * me + (slot >> 3), slot & 7

        @pl.when(alpha_live[row, c] > 0)
        def _():
            src = alpha_source[row, c]
            owner = src >> 1
            ahead = (me >> 1) - (owner >> 1)
            hops = jnp.where((owner & 1) == 0, ahead, -ahead) & 3
            piece = hops + 4 * ((owner >> 3) ^ (me >> 3)) + 8 * ((owner ^ me) & 1)
            put(alpha_plan, 0, piece * 64 + (src & 1) * 32 + slot)

        src = alpha_source[2 * (me ^ 1) + (slot >> 3), c]
        owner = src >> 1

        @pl.when(((owner ^ me) & 1) == 0)
        def _():
            ahead = (me >> 1) - (owner >> 1)
            picks[4 * ((owner >> 3) ^ (me >> 3)) + (jnp.where(up, ahead, -ahead) & 3)] = src & 1

        return 0

    def beta(target, slot, _):
        row, c = 2 * (mb ^ (8 * target)) + (slot >> 3), slot & 7
        src = beta_source[row, c]
        owner = src >> 1
        near = (owner >> 3) == (mb >> 3)
        place = owner & 7

        @pl.when(near & (beta_live[row, c] > 0))
        def _():
            ahead = mb - owner
            d = jnp.where(up, ahead, -ahead) & 7
            call = jnp.where(d == 4, 2, 1) if target else 0
            tile = place if target else c
            word = d * 64 + (src & 1) * 32 + (slot >> 3) * 16 + tile
            put(beta_plan, call, word)

        if not target:

            @pl.when(jnp.logical_not(near))
            def _():
                sends[place] = slot

        return 0

    lax.fori_loop(0, 2 * SLOTS, alpha, 0)
    for target in range(2):
        lax.fori_loop(0, 2 * SLOTS, functools.partial(beta, target), 0)


def start_one_of(pieces, piece, make):
    for i, ref in enumerate(pieces):
        pl.when(piece == i)(lambda ref=ref: make(ref).start())


SOON = (0, 1, 3, 4, 5, 7)


def pick_kernel(picks, *refs):
    pieces, (out, sem) = refs[:6], refs[6:]
    copies = [
        pltpu.make_async_copy(
            piece.at[pl.ds(pl.multiple_of(picks[d] * BS, BS), BS)], out.at[i], sem.at[i]
        )
        for i, (d, piece) in enumerate(zip(SOON, pieces))
    ]
    for copy in copies:
        copy.start()
    for copy in copies:
        copy.wait()


def pick_call(picks, pieces):
    n = pieces[0].shape[1]
    return pl.pallas_call(
        pick_kernel,
        out_shape=jax.ShapeDtypeStruct((6, BS, n), jnp.float32),
        in_specs=[SMEM] + [ANY] * 6,
        out_specs=VMEM,
        scratch_shapes=[pltpu.SemaphoreType.DMA((6,))],
        compiler_params=pltpu.CompilerParams(vmem_limit_bytes=12 * MIB),
        cost_estimate=SMALL,
        name="pick",
    )(picks, *pieces)


def alpha_kernel(plan, *refs):
    pieces, (us2, vs2, picked, own), refs = refs[:8], refs[8:12], refs[12:]
    out, data, tiles, data_sem, tile_sem = refs
    count = plan[0, 0]

    def tile_of(k, slot):
        return pltpu.make_async_copy(own.at[slot >> 3, slot & 7], tiles.at[k], tile_sem.at[k])

    def rows_of(k, ref):
        return pltpu.make_async_copy(ref, data.at[k], data_sem.at[k])

    def fetch(k, _):
        word = plan[0, k + 1]
        piece = word >> 6
        tile_of(k, word & 31).start()
        rows = pl.ds(pl.multiple_of(((word >> 5) & 1) * BS, BS), BS)
        start_one_of(pieces, piece, lambda ref: rows_of(k, ref.at[rows]))
        pl.when(piece == 10)(lambda: rows_of(k, us2.at[rows]).start())
        pl.when(piece == 14)(lambda: rows_of(k, vs2.at[rows]).start())
        place = (piece & 7) - (piece > 10).astype(jnp.int32) - (piece > 14).astype(jnp.int32)
        pl.when((piece >= 8) & (piece != 10) & (piece != 14))(
            lambda: rows_of(k, picked.at[place]).start()
        )
        return 0

    lax.fori_loop(0, count, fetch, 0)
    out[...] = jnp.zeros_like(out)

    def product(k, _):
        slot = plan[0, k + 1] & 31
        tile_of(k, slot).wait()
        rows_of(k, picked.at[0]).wait()
        rows = pl.multiple_of((slot >> 3) * BS, BS)
        out[pl.ds(rows, BS), :] += dot3(tiles[k], data[k])
        return 0

    lax.fori_loop(0, count, product, 0)


def alpha_call(plan, pieces, us2, vs2, picked, own):
    n = own.shape[0] * BS
    return pl.pallas_call(
        alpha_kernel,
        out_shape=jax.ShapeDtypeStruct((n, n), jnp.float32),
        in_specs=[SMEM] + [HBM] * 12,
        out_specs=VMEM,
        scratch_shapes=[
            pltpu.VMEM((2 * SLOTS, BS, n), jnp.float32),
            pltpu.VMEM((2 * SLOTS, BS, BS), jnp.float32),
            pltpu.SemaphoreType.DMA((2 * SLOTS,)),
            pltpu.SemaphoreType.DMA((2 * SLOTS,)),
        ],
        compiler_params=pltpu.CompilerParams(vmem_limit_bytes=18 * MIB),
        cost_estimate=SMALL,
        name="alpha",
    )(plan, *in_hbm(*pieces, us2, vs2, picked, own))


def send_kernel(where, sends, own, out, sem):
    copies = []
    for i in range(SLOTS // 2):
        slot = sends[(where[0] & 1) * (SLOTS // 2) + i]
        copies.append(
            pltpu.make_async_copy(own.at[slot >> 3, slot & 7], out.at[i], sem.at[i])
        )
    for copy in copies:
        copy.start()
    for copy in copies:
        copy.wait()


def send_call(where, sends, own):
    return pl.pallas_call(
        send_kernel,
        out_shape=jax.ShapeDtypeStruct((SLOTS // 2, BS, BS), jnp.float32),
        in_specs=[SMEM] * 2 + [HBM],
        out_specs=VMEM,
        scratch_shapes=[pltpu.SemaphoreType.DMA((SLOTS // 2,))],
        cost_estimate=SMALL,
        name="send",
    )(where, sends, *in_hbm(own))


NEAR = (0, 1, 2, 3, 5, 6, 7)
HOPS = (tuple(range(8)), NEAR, NEAR, (4,))


def beta_kernel(call, where, plan, *refs):
    numbers = HOPS[call]
    pieces, refs = refs[: len(numbers)], refs[len(numbers) :]
    own, got, other, refs = refs[0], refs[1], refs[2], refs[3:]
    before, refs = (refs[0], refs[1:]) if call == 3 else (None, refs)
    out, data, tiles, data_sem, tile_sem, out_sem = refs
    rows, half = data.shape[1], BS
    n = 2 * half
    if call == 3:
        first = pltpu.make_async_copy(before, out.at[:, pl.ds(0, n)], out_sem)
        first.start()
    at = half if call == 2 else 0
    row = min(call, 1) if call < 3 else 2
    core = where[0] & 1
    count = plan[row, 0]

    def columns_of(k, ref, block):
        block = ref.at[pl.ds(at, rows), pl.ds(pl.multiple_of(block * BS, BS), BS)]
        return pltpu.make_async_copy(block, data.at[k], data_sem.at[k])

    def tile_from(k, ref):
        return pltpu.make_async_copy(ref, tiles.at[k], tile_sem.at[k])

    def fetch(k, _):
        word = plan[row, k + 1]
        tile = word & 15
        for number, ref in zip(numbers, pieces):
            pl.when((word >> 6) == number)(
                lambda ref=ref: columns_of(k, ref, (word >> 5) & 1).start()
            )
        if call == 0:
            tile_from(k, own.at[(word >> 4) & 1, tile]).start()
        else:
            start_one_of(
                (got, other), core ^ (tile >> 2), lambda ref: tile_from(k, ref.at[tile & 3])
            )
        return 0

    lax.fori_loop(0, count, fetch, 0)
    if call == 3:
        out[:, n:] = jnp.zeros((half, BS), jnp.float32)
        first.wait()
    else:
        out[...] = jnp.zeros_like(out)

    def product(k, _):
        block = (plan[row, k + 1] >> 4) & 1
        columns_of(k, pieces[0], 0).wait()
        tile_from(k, own.at[0, 0]).wait()
        columns = pl.ds(pl.multiple_of(block * BS, BS), BS)
        if call == 3:
            out[:, n:] += dot3(data[k, :half], tiles[k])
            out[:, columns] += dot3(data[k, half:], tiles[k])
        else:
            out[:, columns] += dot3(data[k], tiles[k])
        return 0

    lax.fori_loop(0, count, product, 0)


def beta_call(call, where, plan, held, own, got, other, before=()):
    n = held[0].shape[0]
    half = n // 2
    rows = half if call in (1, 2) else n
    shape = ((n, n), (half, n), (half, n), (half, n + BS))[call]
    fresh = {1: (3, 5), 3: (4,)}.get(call, ())
    pieces = [held[d] if d in fresh else in_hbm(held[d])[0] for d in HOPS[call]]
    fixed = [*in_hbm(own, got), other] if call == 1 else in_hbm(own, got, other)
    return pl.pallas_call(
        functools.partial(beta_kernel, call),
        out_shape=jax.ShapeDtypeStruct(shape, jnp.float32),
        in_specs=[SMEM] * 2 + [ANY] * (len(pieces) + 3 + len(before)),
        out_specs=VMEM,
        scratch_shapes=[
            pltpu.VMEM((len(pieces), rows, BS), jnp.float32),
            pltpu.VMEM((len(pieces), BS, BS), jnp.float32),
            pltpu.SemaphoreType.DMA((len(pieces),)),
            pltpu.SemaphoreType.DMA((len(pieces),)),
            pltpu.SemaphoreType.DMA,
        ],
        compiler_params=pltpu.CompilerParams(vmem_limit_bytes=12 * MIB),
        cost_estimate=LARGE,
        name=f"beta{call}",
    )(where, plan, *pieces, *fixed, *before)


def last_kernel(where, sends, joined, top, rest, out, top_here, rest_here, sems):
    half, n = top.shape
    copies = [
        pltpu.make_async_copy(source, target, sems.at[i])
        for i, (source, target) in enumerate(((joined, out), (top, top_here), (rest, rest_here)))
    ]
    for copy in copies:
        copy.start()
    block = sends[(where[1] + 4) & 7] >> 3
    for copy in copies:
        copy.wait()
    out[:half] += top_here[...]
    out[half:] += rest_here[:, :n]
    out[:half, pl.ds(pl.multiple_of(block * BS, BS), BS)] += rest_here[:, n:]


def per_device(
    coeffs,
    diag_alpha,
    diag_beta,
    alpha_tiles,
    beta_tiles,
    alpha_source,
    alpha_live,
    beta_source,
    beta_live,
):
    n = coeffs.shape[0]
    where = jnp.stack([lax.axis_index(ALPHA), lax.axis_index(BETA)]).astype(jnp.int32)
    f1, b1 = step(coeffs, "z"), step(coeffs, "z", -1)
    uf, ub = step(coeffs, "x"), step(coeffs, "x", -1)
    v = swap(coeffs, "yhi")
    alpha_plan, beta_plan, picks, sends = pl.pallas_call(
        plan_kernel,
        out_shape=[
            jax.ShapeDtypeStruct((1, 32), jnp.int32),
            jax.ShapeDtypeStruct((3, 32), jnp.int32),
            jax.ShapeDtypeStruct((8,), jnp.int32),
            jax.ShapeDtypeStruct((SLOTS,), jnp.int32),
        ],
        in_specs=[SMEM] * 5,
        out_specs=[SMEM] * 4,
        name="plan",
    )(where, alpha_source, alpha_live, beta_source, beta_live)
    tiles = send_call(where, sends, beta_tiles)
    f1, b1, tiles = lax.optimization_barrier((f1, b1, tiles))
    f2, b2 = step(f1, "z"), step(b1, "z", -1)
    uf, ub, v = lax.optimization_barrier((uf, ub, v, f1))[:3]
    vf, vb = step(v, "x"), step(v, "x", -1)
    got = swap(after(tiles, v), "ylo")
    f2, b2 = lax.optimization_barrier((f2, b2))
    f3, b3 = step(f2, "z"), step(b2, "z", -1)
    vf, vb, got, uf = lax.optimization_barrier((vf, vb, got, uf, f2))[:4]
    u2, v2 = step(uf, "x"), step(vf, "x")
    other = swap(got, "core")
    picked = pick_call(picks, [coeffs, uf, ub, v, vf, vb])
    f3, b3, picked = lax.optimization_barrier((f3, b3, picked))
    picked = swap(picked, "core")
    held = [coeffs, f1, f2, f3, step(f3, "z"), b3, b2, b1]
    top = beta_call(1, where, beta_plan, held, beta_tiles, got, other)
    top_other = swap(top, "ylo")
    bottom = beta_call(2, where, beta_plan, held, after(beta_tiles, top), got, other)
    pieces = [coeffs, uf, u2, ub, v, vf, v2, vb]
    us2, vs2 = swap(after(u2, top), "core"), swap(after(v2, top), "core")
    rest = beta_call(3, where, beta_plan, held, beta_tiles, got, other, [bottom])
    rest_other = swap(rest, "ylo")
    alpha = alpha_call(alpha_plan, pieces, us2, vs2, picked, after(alpha_tiles, rest))
    beta_own = beta_call(0, where, beta_plan, held, after(beta_tiles, rest), got, other)
    joined = (diag_alpha[:, None] + diag_beta[None, :]) * coeffs + alpha + beta_own
    return pl.pallas_call(
        last_kernel,
        out_shape=jax.ShapeDtypeStruct((n, n), jnp.float32),
        in_specs=[SMEM] * 2 + [ANY] * 3,
        out_specs=VMEM,
        scratch_shapes=[
            pltpu.VMEM(top_other.shape, jnp.float32),
            pltpu.VMEM(rest_other.shape, jnp.float32),
            pltpu.SemaphoreType.DMA((3,)),
        ],
        compiler_params=pltpu.CompilerParams(vmem_limit_bytes=8 * MIB),
        cost_estimate=SMALL,
        name="last",
    )(where, sends, lax.optimization_barrier(joined), top_other, rest_other)


def solution(mesh):
    parts = Mesh(mesh.devices.reshape(SIZES), AXES)
    return jax.shard_map(
        per_device,
        mesh=parts,
        in_specs=(
            P(ALPHA, BETA),
            P(ALPHA),
            P(BETA),
            P(ALPHA, None, None, None),
            P(BETA, None, None, None),
            P(),
            P(),
            P(),
            P(),
        ),
        out_specs=P(ALPHA, BETA),
        check_vma=False,
    )
```

```python
import functools

import jax
import jax.numpy as jnp
from jax import lax
from jax.experimental import pallas as pl
from jax.experimental.pallas import tpu as pltpu
from jax.sharding import Mesh
from jax.sharding import PartitionSpec as P

AXES = ("yhi", "x", "core", "ylo", "z")
SIZES = (2, 4, 2, 2, 8)
ALPHA = ("yhi", "x", "core")
BETA = ("ylo", "z")
BS = 256
SLOTS = 8
MIB = 1 << 20
LARGE = pl.CostEstimate(flops=1 << 34, bytes_accessed=1 << 25, transcendentals=0)
SMALL = pl.CostEstimate(flops=1 << 20, bytes_accessed=1 << 18, transcendentals=0)

SMEM = pl.BlockSpec(memory_space=pltpu.SMEM)
HBM = pl.BlockSpec(memory_space=pltpu.HBM)
ANY = pl.BlockSpec(memory_space=pl.ANY)
VMEM = pl.BlockSpec(memory_space=pltpu.VMEM)


def swap(value, axis):
    return lax.ppermute(value, axis, [(0, 1), (1, 0)])


def step(value, axis, way=1):
    n = lax.axis_size(axis)
    if axis == "z":
        pairs = [(i, (i + way) % n) for i in range(n)]
        pairs += [(n + i, n + (i - way) % n) for i in range(n)]
        return lax.ppermute(value, ("core", axis), pairs)
    pairs = [(2 * i, 2 * ((i + way) % n)) for i in range(n)]
    pairs += [(2 * i + 1, 2 * ((i - way) % n) + 1) for i in range(n)]
    return lax.ppermute(value, (axis, "core"), pairs)


def in_hbm(*values):
    return [pltpu.with_memory_space_constraint(value, pltpu.HBM) for value in values]


def after(value, *earlier):
    return lax.optimization_barrier((value, *earlier))[0]


def dot3(a, b):
    a_hi = a.astype(jnp.bfloat16)
    b_hi = b.astype(jnp.bfloat16)
    a_lo = (a - a_hi.astype(jnp.float32)).astype(jnp.bfloat16)
    b_lo = (b - b_hi.astype(jnp.float32)).astype(jnp.bfloat16)
    dot = functools.partial(jnp.dot, preferred_element_type=jnp.float32)
    return dot(a_hi, b_hi) + (dot(a_hi, b_lo) + dot(a_lo, b_hi))


def plan_kernel(
    where, alpha_source, alpha_live, beta_source, beta_live, alpha_plan, beta_plan, picks, sends
):
    me, mb = where[0], where[1]
    up = (me & 1) == 0
    alpha_plan[0, 0] = 0
    for row in range(3):
        beta_plan[row, 0] = 0

    def put(plan, row, word):
        count = plan[row, 0] + 1
        plan[row, 0] = count
        plan[row, count] = word

    def alpha(slot, _):
        row, c = 2 * me + (slot >> 3), slot & 7

        @pl.when(alpha_live[row, c] > 0)
        def _():
            src = alpha_source[row, c]
            owner = src >> 1
            ahead = (me >> 1) - (owner >> 1)
            hops = jnp.where((owner & 1) == 0, ahead, -ahead) & 3
            piece = hops + 4 * ((owner >> 3) ^ (me >> 3)) + 8 * ((owner ^ me) & 1)
            put(alpha_plan, 0, piece * 64 + (src & 1) * 32 + slot)

        src = alpha_source[2 * (me ^ 1) + (slot >> 3), c]
        owner = src >> 1

        @pl.when(((owner ^ me) & 1) == 0)
        def _():
            ahead = (me >> 1) - (owner >> 1)
            picks[4 * ((owner >> 3) ^ (me >> 3)) + (jnp.where(up, ahead, -ahead) & 3)] = src & 1

        return 0

    def beta(target, slot, _):
        row, c = 2 * (mb ^ (8 * target)) + (slot >> 3), slot & 7
        src = beta_source[row, c]
        owner = src >> 1
        near = (owner >> 3) == (mb >> 3)
        place = owner & 7

        @pl.when(near & (beta_live[row, c] > 0))
        def _():
            ahead = mb - owner
            d = jnp.where(up, ahead, -ahead) & 7
            call = jnp.where(d == 4, 2, 1) if target else 0
            tile = place if target else c
            word = d * 64 + (src & 1) * 32 + (slot >> 3) * 16 + tile
            put(beta_plan, call, word)

        if not target:

            @pl.when(jnp.logical_not(near))
            def _():
                sends[place] = slot

        return 0

    lax.fori_loop(0, 2 * SLOTS, alpha, 0)
    for target in range(2):
        lax.fori_loop(0, 2 * SLOTS, functools.partial(beta, target), 0)


def start_one_of(pieces, piece, make):
    for i, ref in enumerate(pieces):
        pl.when(piece == i)(lambda ref=ref: make(ref).start())


SOON = (0, 1, 3, 4, 5, 7)


def pick_kernel(picks, *refs):
    pieces, (out, sem) = refs[:6], refs[6:]
    copies = [
        pltpu.make_async_copy(
            piece.at[pl.ds(pl.multiple_of(picks[d] * BS, BS), BS)], out.at[i], sem.at[i]
        )
        for i, (d, piece) in enumerate(zip(SOON, pieces))
    ]
    for copy in copies:
        copy.start()
    for copy in copies:
        copy.wait()


def pick_call(picks, pieces):
    n = pieces[0].shape[1]
    return pl.pallas_call(
        pick_kernel,
        out_shape=jax.ShapeDtypeStruct((6, BS, n), jnp.float32),
        in_specs=[SMEM] + [ANY] * 6,
        out_specs=VMEM,
        scratch_shapes=[pltpu.SemaphoreType.DMA((6,))],
        compiler_params=pltpu.CompilerParams(vmem_limit_bytes=12 * MIB),
        cost_estimate=SMALL,
        name="pick",
    )(picks, *pieces)


def alpha_kernel(plan, *refs):
    pieces, (us2, vs2, picked, own), refs = refs[:8], refs[8:12], refs[12:]
    out, data, tiles, data_sem, tile_sem = refs
    count = plan[0, 0]

    def tile_of(k, slot):
        return pltpu.make_async_copy(own.at[slot >> 3, slot & 7], tiles.at[k], tile_sem.at[k])

    def rows_of(k, ref):
        return pltpu.make_async_copy(ref, data.at[k], data_sem.at[k])

    def fetch(k, _):
        word = plan[0, k + 1]
        piece = word >> 6
        tile_of(k, word & 31).start()
        rows = pl.ds(pl.multiple_of(((word >> 5) & 1) * BS, BS), BS)
        start_one_of(pieces, piece, lambda ref: rows_of(k, ref.at[rows]))
        pl.when(piece == 10)(lambda: rows_of(k, us2.at[rows]).start())
        pl.when(piece == 14)(lambda: rows_of(k, vs2.at[rows]).start())
        place = (piece & 7) - (piece > 10).astype(jnp.int32) - (piece > 14).astype(jnp.int32)
        pl.when((piece >= 8) & (piece != 10) & (piece != 14))(
            lambda: rows_of(k, picked.at[place]).start()
        )
        return 0

    lax.fori_loop(0, count, fetch, 0)
    out[...] = jnp.zeros_like(out)

    def product(k, _):
        slot = plan[0, k + 1] & 31
        tile_of(k, slot).wait()
        rows_of(k, picked.at[0]).wait()
        rows = pl.multiple_of((slot >> 3) * BS, BS)
        out[pl.ds(rows, BS), :] += dot3(tiles[k], data[k])
        return 0

    lax.fori_loop(0, count, product, 0)


def alpha_call(plan, pieces, us2, vs2, picked, own):
    n = own.shape[0] * BS
    return pl.pallas_call(
        alpha_kernel,
        out_shape=jax.ShapeDtypeStruct((n, n), jnp.float32),
        in_specs=[SMEM] + [HBM] * 12,
        out_specs=VMEM,
        scratch_shapes=[
            pltpu.VMEM((2 * SLOTS, BS, n), jnp.float32),
            pltpu.VMEM((2 * SLOTS, BS, BS), jnp.float32),
            pltpu.SemaphoreType.DMA((2 * SLOTS,)),
            pltpu.SemaphoreType.DMA((2 * SLOTS,)),
        ],
        compiler_params=pltpu.CompilerParams(vmem_limit_bytes=18 * MIB),
        cost_estimate=SMALL,
        name="alpha",
    )(plan, *in_hbm(*pieces, us2, vs2, picked, own))


def send_kernel(where, sends, own, out, sem):
    copies = []
    for i in range(SLOTS // 2):
        slot = sends[(where[0] & 1) * (SLOTS // 2) + i]
        copies.append(
            pltpu.make_async_copy(own.at[slot >> 3, slot & 7], out.at[i], sem.at[i])
        )
    for copy in copies:
        copy.start()
    for copy in copies:
        copy.wait()


def send_call(where, sends, own):
    return pl.pallas_call(
        send_kernel,
        out_shape=jax.ShapeDtypeStruct((SLOTS // 2, BS, BS), jnp.float32),
        in_specs=[SMEM] * 2 + [HBM],
        out_specs=VMEM,
        scratch_shapes=[pltpu.SemaphoreType.DMA((SLOTS // 2,))],
        cost_estimate=SMALL,
        name="send",
    )(where, sends, *in_hbm(own))


NEAR = (0, 1, 2, 3, 5, 6, 7)
HOPS = (tuple(range(8)), NEAR, NEAR, (4,))


def beta_kernel(call, where, plan, *refs):
    numbers = HOPS[call]
    pieces, refs = refs[: len(numbers)], refs[len(numbers) :]
    own, got, other, refs = refs[0], refs[1], refs[2], refs[3:]
    before, refs = (refs[0], refs[1:]) if call == 3 else (None, refs)
    out, data, tiles, data_sem, tile_sem, out_sem = refs
    rows, half = data.shape[1], BS
    n = 2 * half
    if call == 3:
        first = pltpu.make_async_copy(before, out.at[:, pl.ds(0, n)], out_sem)
        first.start()
    at = half if call == 2 else 0
    row = min(call, 1) if call < 3 else 2
    core = where[0] & 1
    count = plan[row, 0]

    def columns_of(k, ref, block):
        block = ref.at[pl.ds(at, rows), pl.ds(pl.multiple_of(block * BS, BS), BS)]
        return pltpu.make_async_copy(block, data.at[k], data_sem.at[k])

    def tile_from(k, ref):
        return pltpu.make_async_copy(ref, tiles.at[k], tile_sem.at[k])

    def fetch(k, _):
        word = plan[row, k + 1]
        tile = word & 15
        for number, ref in zip(numbers, pieces):
            pl.when((word >> 6) == number)(
                lambda ref=ref: columns_of(k, ref, (word >> 5) & 1).start()
            )
        if call == 0:
            tile_from(k, own.at[(word >> 4) & 1, tile]).start()
        else:
            start_one_of(
                (got, other), core ^ (tile >> 2), lambda ref: tile_from(k, ref.at[tile & 3])
            )
        return 0

    lax.fori_loop(0, count, fetch, 0)
    if call == 3:
        out[:, n:] = jnp.zeros((half, BS), jnp.float32)
        first.wait()
    else:
        out[...] = jnp.zeros_like(out)

    def product(k, _):
        block = (plan[row, k + 1] >> 4) & 1
        columns_of(k, pieces[0], 0).wait()
        tile_from(k, own.at[0, 0]).wait()
        columns = pl.ds(pl.multiple_of(block * BS, BS), BS)
        if call == 3:
            out[:, n:] += dot3(data[k, :half], tiles[k])
            out[:, columns] += dot3(data[k, half:], tiles[k])
        else:
            out[:, columns] += dot3(data[k], tiles[k])
        return 0

    lax.fori_loop(0, count, product, 0)


def beta_call(call, where, plan, held, own, got, other, before=()):
    n = held[0].shape[0]
    half = n // 2
    rows = half if call in (1, 2) else n
    shape = ((n, n), (half, n), (half, n), (half, n + BS))[call]
    fresh = {1: (3, 5), 3: (4,)}.get(call, ())
    pieces = [held[d] if d in fresh else in_hbm(held[d])[0] for d in HOPS[call]]
    fixed = [*in_hbm(own, got), other] if call == 1 else in_hbm(own, got, other)
    return pl.pallas_call(
        functools.partial(beta_kernel, call),
        out_shape=jax.ShapeDtypeStruct(shape, jnp.float32),
        in_specs=[SMEM] * 2 + [ANY] * (len(pieces) + 3 + len(before)),
        out_specs=VMEM,
        scratch_shapes=[
            pltpu.VMEM((len(pieces), rows, BS), jnp.float32),
            pltpu.VMEM((len(pieces), BS, BS), jnp.float32),
            pltpu.SemaphoreType.DMA((len(pieces),)),
            pltpu.SemaphoreType.DMA((len(pieces),)),
            pltpu.SemaphoreType.DMA,
        ],
        compiler_params=pltpu.CompilerParams(vmem_limit_bytes=12 * MIB),
        cost_estimate=LARGE,
        name=f"beta{call}",
    )(where, plan, *pieces, *fixed, *before)


def last_kernel(where, sends, joined, top, rest, out, top_here, rest_here, sems):
    half, n = top.shape
    copies = [
        pltpu.make_async_copy(source, target, sems.at[i])
        for i, (source, target) in enumerate(((joined, out), (top, top_here), (rest, rest_here)))
    ]
    for copy in copies:
        copy.start()
    block = sends[(where[1] + 4) & 7] >> 3
    for copy in copies:
        copy.wait()
    out[:half] += top_here[...]
    out[half:] += rest_here[:, :n]
    out[:half, pl.ds(pl.multiple_of(block * BS, BS), BS)] += rest_here[:, n:]


def per_device(
    coeffs,
    diag_alpha,
    diag_beta,
    alpha_tiles,
    beta_tiles,
    alpha_source,
    alpha_live,
    beta_source,
    beta_live,
):
    n = coeffs.shape[0]
    where = jnp.stack([lax.axis_index(ALPHA), lax.axis_index(BETA)]).astype(jnp.int32)
    f1, b1 = step(coeffs, "z"), step(coeffs, "z", -1)
    uf, ub = step(coeffs, "x"), step(coeffs, "x", -1)
    v = swap(coeffs, "yhi")
    alpha_plan, beta_plan, picks, sends = pl.pallas_call(
        plan_kernel,
        out_shape=[
            jax.ShapeDtypeStruct((1, 32), jnp.int32),
            jax.ShapeDtypeStruct((3, 32), jnp.int32),
            jax.ShapeDtypeStruct((8,), jnp.int32),
            jax.ShapeDtypeStruct((SLOTS,), jnp.int32),
        ],
        in_specs=[SMEM] * 5,
        out_specs=[SMEM] * 4,
        name="plan",
    )(where, alpha_source, alpha_live, beta_source, beta_live)
    tiles = send_call(where, sends, beta_tiles)
    f1, tiles = lax.optimization_barrier((f1, tiles))
    f2, b2 = step(f1, "z"), step(b1, "z", -1)
    uf, ub, v = lax.optimization_barrier((uf, ub, v, f1, b1))[:3]
    vf, vb = step(v, "x"), step(v, "x", -1)
    got = swap(after(tiles, v), "ylo")
    f2, b2 = lax.optimization_barrier((f2, b2))
    f3, b3 = step(f2, "z"), step(b2, "z", -1)
    vf, vb, got, uf = lax.optimization_barrier((vf, vb, got, uf, f2))[:4]
    u2, v2 = step(uf, "x"), step(vf, "x")
    other = swap(got, "core")
    picked = pick_call(picks, [coeffs, uf, ub, v, vf, vb])
    f3, b3, picked = lax.optimization_barrier((f3, b3, picked))
    picked = swap(picked, "core")
    held = [coeffs, f1, f2, f3, step(f3, "z"), b3, b2, b1]
    top = beta_call(1, where, beta_plan, held, beta_tiles, got, other)
    top_other = swap(top, "ylo")
    bottom = beta_call(2, where, beta_plan, held, after(beta_tiles, top), got, other)
    pieces = [coeffs, uf, u2, ub, v, vf, v2, vb]
    us2, vs2 = swap(after(u2, top), "core"), swap(after(v2, top), "core")
    rest = beta_call(3, where, beta_plan, held, beta_tiles, got, other, [bottom])
    rest_other = swap(rest, "ylo")
    alpha = alpha_call(alpha_plan, pieces, us2, vs2, picked, after(alpha_tiles, rest))
    beta_own = beta_call(0, where, beta_plan, held, after(beta_tiles, rest), got, other)
    joined = (diag_alpha[:, None] + diag_beta[None, :]) * coeffs + alpha + beta_own
    return pl.pallas_call(
        last_kernel,
        out_shape=jax.ShapeDtypeStruct((n, n), jnp.float32),
        in_specs=[SMEM] * 2 + [ANY] * 3,
        out_specs=VMEM,
        scratch_shapes=[
            pltpu.VMEM(top_other.shape, jnp.float32),
            pltpu.VMEM(rest_other.shape, jnp.float32),
            pltpu.SemaphoreType.DMA((3,)),
        ],
        compiler_params=pltpu.CompilerParams(vmem_limit_bytes=8 * MIB),
        cost_estimate=SMALL,
        name="last",
    )(where, sends, lax.optimization_barrier(joined), top_other, rest_other)


def solution(mesh):
    parts = Mesh(mesh.devices.reshape(SIZES), AXES)
    return jax.shard_map(
        per_device,
        mesh=parts,
        in_specs=(
            P(ALPHA, BETA),
            P(ALPHA),
            P(BETA),
            P(ALPHA, None, None, None),
            P(BETA, None, None, None),
            P(),
            P(),
            P(),
            P(),
        ),
        out_specs=P(ALPHA, BETA),
        check_vma=False,
    )
```

```python
import functools

import jax
import jax.numpy as jnp
from jax import lax
from jax.experimental import pallas as pl
from jax.experimental.pallas import tpu as pltpu
from jax.sharding import Mesh
from jax.sharding import PartitionSpec as P

AXES = ("yhi", "x", "core", "ylo", "z")
SIZES = (2, 4, 2, 2, 8)
ALPHA = ("yhi", "x", "core")
BETA = ("ylo", "z")
BS = 256
SLOTS = 8
MIB = 1 << 20
LARGE = pl.CostEstimate(flops=1 << 34, bytes_accessed=1 << 25, transcendentals=0)
SMALL = pl.CostEstimate(flops=1 << 20, bytes_accessed=1 << 18, transcendentals=0)

SMEM = pl.BlockSpec(memory_space=pltpu.SMEM)
HBM = pl.BlockSpec(memory_space=pltpu.HBM)
ANY = pl.BlockSpec(memory_space=pl.ANY)
VMEM = pl.BlockSpec(memory_space=pltpu.VMEM)


def swap(value, axis):
    return lax.ppermute(value, axis, [(0, 1), (1, 0)])


def step(value, axis, way=1):
    n = lax.axis_size(axis)
    if axis == "z":
        pairs = [(i, (i + way) % n) for i in range(n)]
        pairs += [(n + i, n + (i - way) % n) for i in range(n)]
        return lax.ppermute(value, ("core", axis), pairs)
    pairs = [(2 * i, 2 * ((i + way) % n)) for i in range(n)]
    pairs += [(2 * i + 1, 2 * ((i - way) % n) + 1) for i in range(n)]
    return lax.ppermute(value, (axis, "core"), pairs)


def in_hbm(*values):
    return [pltpu.with_memory_space_constraint(value, pltpu.HBM) for value in values]


def after(value, *earlier):
    return lax.optimization_barrier((value, *earlier))[0]


def dot3(a, b):
    a_hi = a.astype(jnp.bfloat16)
    b_hi = b.astype(jnp.bfloat16)
    a_lo = (a - a_hi.astype(jnp.float32)).astype(jnp.bfloat16)
    b_lo = (b - b_hi.astype(jnp.float32)).astype(jnp.bfloat16)
    dot = functools.partial(jnp.dot, preferred_element_type=jnp.float32)
    return dot(a_hi, b_hi) + (dot(a_hi, b_lo) + dot(a_lo, b_hi))


def plan_kernel(
    where, alpha_source, alpha_live, beta_source, beta_live, alpha_plan, beta_plan, picks, sends
):
    me, mb = where[0], where[1]
    up = (me & 1) == 0
    alpha_plan[0, 0] = 0
    for row in range(3):
        beta_plan[row, 0] = 0

    def put(plan, row, word):
        count = plan[row, 0] + 1
        plan[row, 0] = count
        plan[row, count] = word

    def alpha(slot, _):
        row, c = 2 * me + (slot >> 3), slot & 7

        @pl.when(alpha_live[row, c] > 0)
        def _():
            src = alpha_source[row, c]
            owner = src >> 1
            ahead = (me >> 1) - (owner >> 1)
            hops = jnp.where((owner & 1) == 0, ahead, -ahead) & 3
            piece = hops + 4 * ((owner >> 3) ^ (me >> 3)) + 8 * ((owner ^ me) & 1)
            put(alpha_plan, 0, piece * 64 + (src & 1) * 32 + slot)

        src = alpha_source[2 * (me ^ 1) + (slot >> 3), c]
        owner = src >> 1

        @pl.when(((owner ^ me) & 1) == 0)
        def _():
            ahead = (me >> 1) - (owner >> 1)
            picks[4 * ((owner >> 3) ^ (me >> 3)) + (jnp.where(up, ahead, -ahead) & 3)] = src & 1

        return 0

    def beta(target, slot, _):
        row, c = 2 * (mb ^ (8 * target)) + (slot >> 3), slot & 7
        src = beta_source[row, c]
        owner = src >> 1
        near = (owner >> 3) == (mb >> 3)
        place = owner & 7

        @pl.when(near & (beta_live[row, c] > 0))
        def _():
            ahead = mb - owner
            d = jnp.where(up, ahead, -ahead) & 7
            call = jnp.where(d == 4, 2, 1) if target else 0
            tile = place if target else c
            word = d * 64 + (src & 1) * 32 + (slot >> 3) * 16 + tile
            put(beta_plan, call, word)

        if not target:

            @pl.when(jnp.logical_not(near))
            def _():
                sends[place] = slot

        return 0

    lax.fori_loop(0, 2 * SLOTS, alpha, 0)
    for target in range(2):
        lax.fori_loop(0, 2 * SLOTS, functools.partial(beta, target), 0)


def start_one_of(pieces, piece, make):
    for i, ref in enumerate(pieces):
        pl.when(piece == i)(lambda ref=ref: make(ref).start())


SOON = (0, 1, 3, 4, 5, 7)


def pick_kernel(picks, *refs):
    pieces, (out, sem) = refs[:6], refs[6:]
    copies = [
        pltpu.make_async_copy(
            piece.at[pl.ds(pl.multiple_of(picks[d] * BS, BS), BS)], out.at[i], sem.at[i]
        )
        for i, (d, piece) in enumerate(zip(SOON, pieces))
    ]
    for copy in copies:
        copy.start()
    for copy in copies:
        copy.wait()


def pick_call(picks, pieces):
    n = pieces[0].shape[1]
    return pl.pallas_call(
        pick_kernel,
        out_shape=jax.ShapeDtypeStruct((6, BS, n), jnp.float32),
        in_specs=[SMEM] + [ANY] * 6,
        out_specs=VMEM,
        scratch_shapes=[pltpu.SemaphoreType.DMA((6,))],
        compiler_params=pltpu.CompilerParams(vmem_limit_bytes=12 * MIB),
        cost_estimate=SMALL,
        name="pick",
    )(picks, *pieces)


def alpha_kernel(plan, *refs):
    pieces, (us2, vs2, picked, own), refs = refs[:8], refs[8:12], refs[12:]
    out, data, tiles, data_sem, tile_sem = refs
    count = plan[0, 0]

    def tile_of(k, slot):
        return pltpu.make_async_copy(own.at[slot >> 3, slot & 7], tiles.at[k], tile_sem.at[k])

    def rows_of(k, ref):
        return pltpu.make_async_copy(ref, data.at[k], data_sem.at[k])

    def fetch(k, _):
        word = plan[0, k + 1]
        piece = word >> 6
        tile_of(k, word & 31).start()
        rows = pl.ds(pl.multiple_of(((word >> 5) & 1) * BS, BS), BS)
        start_one_of(pieces, piece, lambda ref: rows_of(k, ref.at[rows]))
        pl.when(piece == 10)(lambda: rows_of(k, us2.at[rows]).start())
        pl.when(piece == 14)(lambda: rows_of(k, vs2.at[rows]).start())
        place = (piece & 7) - (piece > 10).astype(jnp.int32) - (piece > 14).astype(jnp.int32)
        pl.when((piece >= 8) & (piece != 10) & (piece != 14))(
            lambda: rows_of(k, picked.at[place]).start()
        )
        return 0

    lax.fori_loop(0, count, fetch, 0)
    out[...] = jnp.zeros_like(out)

    def product(k, _):
        slot = plan[0, k + 1] & 31
        tile_of(k, slot).wait()
        rows_of(k, picked.at[0]).wait()
        rows = pl.multiple_of((slot >> 3) * BS, BS)
        out[pl.ds(rows, BS), :] += dot3(tiles[k], data[k])
        return 0

    lax.fori_loop(0, count, product, 0)


def alpha_call(plan, pieces, us2, vs2, picked, own):
    n = own.shape[0] * BS
    return pl.pallas_call(
        alpha_kernel,
        out_shape=jax.ShapeDtypeStruct((n, n), jnp.float32),
        in_specs=[SMEM] + [HBM] * 12,
        out_specs=VMEM,
        scratch_shapes=[
            pltpu.VMEM((2 * SLOTS, BS, n), jnp.float32),
            pltpu.VMEM((2 * SLOTS, BS, BS), jnp.float32),
            pltpu.SemaphoreType.DMA((2 * SLOTS,)),
            pltpu.SemaphoreType.DMA((2 * SLOTS,)),
        ],
        compiler_params=pltpu.CompilerParams(vmem_limit_bytes=18 * MIB),
        cost_estimate=SMALL,
        name="alpha",
    )(plan, *in_hbm(*pieces, us2, vs2, picked, own))


def send_kernel(where, sends, own, out, sem):
    copies = []
    for i in range(SLOTS // 2):
        slot = sends[(where[0] & 1) * (SLOTS // 2) + i]
        copies.append(
            pltpu.make_async_copy(own.at[slot >> 3, slot & 7], out.at[i], sem.at[i])
        )
    for copy in copies:
        copy.start()
    for copy in copies:
        copy.wait()


def send_call(where, sends, own):
    return pl.pallas_call(
        send_kernel,
        out_shape=jax.ShapeDtypeStruct((SLOTS // 2, BS, BS), jnp.float32),
        in_specs=[SMEM] * 2 + [HBM],
        out_specs=VMEM,
        scratch_shapes=[pltpu.SemaphoreType.DMA((SLOTS // 2,))],
        cost_estimate=SMALL,
        name="send",
    )(where, sends, *in_hbm(own))


NEAR = (0, 1, 2, 3, 5, 6, 7)
HOPS = (tuple(range(8)), NEAR, NEAR, (4,))


def beta_kernel(call, where, plan, *refs):
    numbers = HOPS[call]
    pieces, refs = refs[: len(numbers)], refs[len(numbers) :]
    own, got, other, refs = refs[0], refs[1], refs[2], refs[3:]
    before, refs = (refs[0], refs[1:]) if call == 3 else (None, refs)
    out, data, tiles, data_sem, tile_sem, out_sem = refs
    rows, half = data.shape[1], BS
    n = 2 * half
    if call == 3:
        first = pltpu.make_async_copy(before, out.at[:, pl.ds(0, n)], out_sem)
        first.start()
    at = half if call == 2 else 0
    row = min(call, 1) if call < 3 else 2
    core = where[0] & 1
    count = plan[row, 0]

    def columns_of(k, ref, block):
        block = ref.at[pl.ds(at, rows), pl.ds(pl.multiple_of(block * BS, BS), BS)]
        return pltpu.make_async_copy(block, data.at[k], data_sem.at[k])

    def tile_from(k, ref):
        return pltpu.make_async_copy(ref, tiles.at[k], tile_sem.at[k])

    def fetch(k, _):
        word = plan[row, k + 1]
        tile = word & 15
        for number, ref in zip(numbers, pieces):
            pl.when((word >> 6) == number)(
                lambda ref=ref: columns_of(k, ref, (word >> 5) & 1).start()
            )
        if call == 0:
            tile_from(k, own.at[(word >> 4) & 1, tile]).start()
        else:
            start_one_of(
                (got, other), core ^ (tile >> 2), lambda ref: tile_from(k, ref.at[tile & 3])
            )
        return 0

    lax.fori_loop(0, count, fetch, 0)
    if call == 3:
        out[:, n:] = jnp.zeros((half, BS), jnp.float32)
        first.wait()
    else:
        out[...] = jnp.zeros_like(out)

    def product(k, _):
        block = (plan[row, k + 1] >> 4) & 1
        columns_of(k, pieces[0], 0).wait()
        tile_from(k, own.at[0, 0]).wait()
        columns = pl.ds(pl.multiple_of(block * BS, BS), BS)
        if call == 3:
            out[:, n:] += dot3(data[k, :half], tiles[k])
            out[:, columns] += dot3(data[k, half:], tiles[k])
        else:
            out[:, columns] += dot3(data[k], tiles[k])
        return 0

    lax.fori_loop(0, count, product, 0)


def beta_call(call, where, plan, held, own, got, other, before=()):
    n = held[0].shape[0]
    half = n // 2
    rows = half if call in (1, 2) else n
    shape = ((n, n), (half, n), (half, n), (half, n + BS))[call]
    fresh = {1: (3, 5), 3: (4,)}.get(call, ())
    pieces = [held[d] if d in fresh else in_hbm(held[d])[0] for d in HOPS[call]]
    fixed = [*in_hbm(own, got), other] if call == 1 else in_hbm(own, got, other)
    return pl.pallas_call(
        functools.partial(beta_kernel, call),
        out_shape=jax.ShapeDtypeStruct(shape, jnp.float32),
        in_specs=[SMEM] * 2 + [ANY] * (len(pieces) + 3 + len(before)),
        out_specs=VMEM,
        scratch_shapes=[
            pltpu.VMEM((len(pieces), rows, BS), jnp.float32),
            pltpu.VMEM((len(pieces), BS, BS), jnp.float32),
            pltpu.SemaphoreType.DMA((len(pieces),)),
            pltpu.SemaphoreType.DMA((len(pieces),)),
            pltpu.SemaphoreType.DMA,
        ],
        compiler_params=pltpu.CompilerParams(vmem_limit_bytes=12 * MIB),
        cost_estimate=LARGE,
        name=f"beta{call}",
    )(where, plan, *pieces, *fixed, *before)


def last_kernel(where, sends, joined, top, rest, out):
    half, n = top.shape
    block = sends[(where[1] + 4) & 7] >> 3
    out[half:] = joined[half:] + rest[:, :n]
    out[:half] = joined[:half] + top[...]
    out[:half, pl.ds(pl.multiple_of(block * BS, BS), BS)] += rest[:, n:]


def per_device(
    coeffs,
    diag_alpha,
    diag_beta,
    alpha_tiles,
    beta_tiles,
    alpha_source,
    alpha_live,
    beta_source,
    beta_live,
):
    n = coeffs.shape[0]
    where = jnp.stack([lax.axis_index(ALPHA), lax.axis_index(BETA)]).astype(jnp.int32)
    f1, b1 = step(coeffs, "z"), step(coeffs, "z", -1)
    uf, ub = step(coeffs, "x"), step(coeffs, "x", -1)
    v = swap(coeffs, "yhi")
    alpha_plan, beta_plan, picks, sends = pl.pallas_call(
        plan_kernel,
        out_shape=[
            jax.ShapeDtypeStruct((1, 32), jnp.int32),
            jax.ShapeDtypeStruct((3, 32), jnp.int32),
            jax.ShapeDtypeStruct((8,), jnp.int32),
            jax.ShapeDtypeStruct((SLOTS,), jnp.int32),
        ],
        in_specs=[SMEM] * 5,
        out_specs=[SMEM] * 4,
        name="plan",
    )(where, alpha_source, alpha_live, beta_source, beta_live)
    tiles = send_call(where, sends, beta_tiles)
    f1, tiles = lax.optimization_barrier((f1, tiles))
    f2, b2 = step(f1, "z"), step(b1, "z", -1)
    uf, ub, v = lax.optimization_barrier((uf, ub, v, f1, b1))[:3]
    vf, vb = step(v, "x"), step(v, "x", -1)
    got = swap(after(tiles, v), "ylo")
    f2, b2 = lax.optimization_barrier((f2, b2))
    f3, b3 = step(f2, "z"), step(b2, "z", -1)
    vf, vb, got, uf = lax.optimization_barrier((vf, vb, got, uf, f2))[:4]
    u2, v2 = step(uf, "x"), step(vf, "x")
    other = swap(got, "core")
    picked = pick_call(picks, [coeffs, uf, ub, v, vf, vb])
    f3, b3, picked = lax.optimization_barrier((f3, b3, picked))
    picked = swap(picked, "core")
    held = [coeffs, f1, f2, f3, step(f3, "z"), b3, b2, b1]
    top = beta_call(1, where, beta_plan, held, beta_tiles, got, other)
    top_other = swap(top, "ylo")
    bottom = beta_call(2, where, beta_plan, held, after(beta_tiles, top), got, other)
    pieces = [coeffs, uf, u2, ub, v, vf, v2, vb]
    us2, vs2 = swap(after(u2, top), "core"), swap(after(v2, top), "core")
    rest = beta_call(3, where, beta_plan, held, beta_tiles, got, other, [bottom])
    rest_other = swap(rest, "ylo")
    alpha = alpha_call(alpha_plan, pieces, us2, vs2, picked, after(alpha_tiles, rest))
    beta_own = beta_call(0, where, beta_plan, held, after(beta_tiles, rest), got, other)
    joined = (diag_alpha[:, None] + diag_beta[None, :]) * coeffs + alpha + beta_own
    parts = [
        pltpu.with_memory_space_constraint(part, pltpu.VMEM)
        for part in (lax.optimization_barrier(joined), top_other, rest_other)
    ]
    return pl.pallas_call(
        last_kernel,
        out_shape=jax.ShapeDtypeStruct((n, n), jnp.float32),
        in_specs=[SMEM] * 2 + [VMEM] * 3,
        out_specs=VMEM,
        compiler_params=pltpu.CompilerParams(vmem_limit_bytes=8 * MIB),
        cost_estimate=SMALL,
        name="last",
    )(where, sends, *parts)


def solution(mesh):
    parts = Mesh(mesh.devices.reshape(SIZES), AXES)
    return jax.shard_map(
        per_device,
        mesh=parts,
        in_specs=(
            P(ALPHA, BETA),
            P(ALPHA),
            P(BETA),
            P(ALPHA, None, None, None),
            P(BETA, None, None, None),
            P(),
            P(),
            P(),
            P(),
        ),
        out_specs=P(ALPHA, BETA),
        check_vma=False,
    )
```

```python
import functools

import jax
import jax.numpy as jnp
from jax import lax
from jax.experimental import pallas as pl
from jax.experimental.pallas import tpu as pltpu
from jax.sharding import Mesh
from jax.sharding import PartitionSpec as P

AXES = ("yhi", "x", "core", "ylo", "z")
SIZES = (2, 4, 2, 2, 8)
ALPHA = ("yhi", "x", "core")
BETA = ("ylo", "z")
BS = 256
SLOTS = 8
MIB = 1 << 20
LARGE = pl.CostEstimate(flops=1 << 34, bytes_accessed=1 << 25, transcendentals=0)
SMALL = pl.CostEstimate(flops=1 << 20, bytes_accessed=1 << 18, transcendentals=0)

SMEM = pl.BlockSpec(memory_space=pltpu.SMEM)
HBM = pl.BlockSpec(memory_space=pltpu.HBM)
ANY = pl.BlockSpec(memory_space=pl.ANY)
VMEM = pl.BlockSpec(memory_space=pltpu.VMEM)


def swap(value, axis):
    return lax.ppermute(value, axis, [(0, 1), (1, 0)])


def step(value, axis, way=1):
    n = lax.axis_size(axis)
    if axis == "z":
        pairs = [(i, (i + way) % n) for i in range(n)]
        pairs += [(n + i, n + (i - way) % n) for i in range(n)]
        return lax.ppermute(value, ("core", axis), pairs)
    pairs = [(2 * i, 2 * ((i + way) % n)) for i in range(n)]
    pairs += [(2 * i + 1, 2 * ((i - way) % n) + 1) for i in range(n)]
    return lax.ppermute(value, (axis, "core"), pairs)


def in_hbm(*values):
    return [pltpu.with_memory_space_constraint(value, pltpu.HBM) for value in values]


def after(value, *earlier):
    return lax.optimization_barrier((value, *earlier))[0]


def dot3(a, b):
    a_hi = a.astype(jnp.bfloat16)
    b_hi = b.astype(jnp.bfloat16)
    a_lo = (a - a_hi.astype(jnp.float32)).astype(jnp.bfloat16)
    b_lo = (b - b_hi.astype(jnp.float32)).astype(jnp.bfloat16)
    dot = functools.partial(jnp.dot, preferred_element_type=jnp.float32)
    return dot(a_hi, b_hi) + (dot(a_hi, b_lo) + dot(a_lo, b_hi))


def plan_kernel(
    where, alpha_source, alpha_live, beta_source, beta_live, alpha_plan, beta_plan, picks, sends
):
    me, mb = where[0], where[1]
    up = (me & 1) == 0
    alpha_plan[0, 0] = 0
    for row in range(3):
        beta_plan[row, 0] = 0

    def put(plan, row, word):
        count = plan[row, 0] + 1
        plan[row, 0] = count
        plan[row, count] = word

    def alpha(slot, _):
        row, c = 2 * me + (slot >> 3), slot & 7

        @pl.when(alpha_live[row, c] > 0)
        def _():
            src = alpha_source[row, c]
            owner = src >> 1
            ahead = (me >> 1) - (owner >> 1)
            hops = jnp.where((owner & 1) == 0, ahead, -ahead) & 3
            piece = hops + 4 * ((owner >> 3) ^ (me >> 3)) + 8 * ((owner ^ me) & 1)
            put(alpha_plan, 0, piece * 64 + (src & 1) * 32 + slot)

        src = alpha_source[2 * (me ^ 1) + (slot >> 3), c]
        owner = src >> 1

        @pl.when(((owner ^ me) & 1) == 0)
        def _():
            ahead = (me >> 1) - (owner >> 1)
            picks[4 * ((owner >> 3) ^ (me >> 3)) + (jnp.where(up, ahead, -ahead) & 3)] = src & 1

        return 0

    def beta(target, slot, _):
        row, c = 2 * (mb ^ (8 * target)) + (slot >> 3), slot & 7
        src = beta_source[row, c]
        owner = src >> 1
        near = (owner >> 3) == (mb >> 3)
        place = owner & 7

        @pl.when(near & (beta_live[row, c] > 0))
        def _():
            ahead = mb - owner
            d = jnp.where(up, ahead, -ahead) & 7
            call = jnp.where(d == 4, 2, 1) if target else 0
            tile = place if target else c
            word = d * 64 + (src & 1) * 32 + (slot >> 3) * 16 + tile
            put(beta_plan, call, word)

        if not target:

            @pl.when(jnp.logical_not(near))
            def _():
                sends[place] = slot

        return 0

    lax.fori_loop(0, 2 * SLOTS, alpha, 0)
    for target in range(2):
        lax.fori_loop(0, 2 * SLOTS, functools.partial(beta, target), 0)


def start_one_of(pieces, piece, make):
    for i, ref in enumerate(pieces):
        pl.when(piece == i)(lambda ref=ref: make(ref).start())


SOON = (0, 1, 3, 4, 5, 7)


def pick_kernel(picks, *refs):
    pieces, (out, sem) = refs[:6], refs[6:]
    copies = [
        pltpu.make_async_copy(
            piece.at[pl.ds(pl.multiple_of(picks[d] * BS, BS), BS)], out.at[i], sem.at[i]
        )
        for i, (d, piece) in enumerate(zip(SOON, pieces))
    ]
    for copy in copies:
        copy.start()
    for copy in copies:
        copy.wait()


def pick_call(picks, pieces):
    n = pieces[0].shape[1]
    return pl.pallas_call(
        pick_kernel,
        out_shape=jax.ShapeDtypeStruct((6, BS, n), jnp.float32),
        in_specs=[SMEM] + [ANY] * 6,
        out_specs=VMEM,
        scratch_shapes=[pltpu.SemaphoreType.DMA((6,))],
        compiler_params=pltpu.CompilerParams(vmem_limit_bytes=12 * MIB),
        cost_estimate=SMALL,
        name="pick",
    )(picks, *pieces)


def alpha_kernel(plan, *refs):
    pieces, (us2, vs2, picked, own), refs = refs[:8], refs[8:12], refs[12:]
    out, data, tiles, data_sem, tile_sem = refs
    count = plan[0, 0]

    def tile_of(k, slot):
        return pltpu.make_async_copy(own.at[slot >> 3, slot & 7], tiles.at[k], tile_sem.at[k])

    def rows_of(k, ref):
        return pltpu.make_async_copy(ref, data.at[k], data_sem.at[k])

    def fetch(k, _):
        word = plan[0, k + 1]
        piece = word >> 6
        tile_of(k, word & 31).start()
        rows = pl.ds(pl.multiple_of(((word >> 5) & 1) * BS, BS), BS)
        start_one_of(pieces, piece, lambda ref: rows_of(k, ref.at[rows]))
        pl.when(piece == 10)(lambda: rows_of(k, us2.at[rows]).start())
        pl.when(piece == 14)(lambda: rows_of(k, vs2.at[rows]).start())
        place = (piece & 7) - (piece > 10).astype(jnp.int32) - (piece > 14).astype(jnp.int32)
        pl.when((piece >= 8) & (piece != 10) & (piece != 14))(
            lambda: rows_of(k, picked.at[place]).start()
        )
        return 0

    lax.fori_loop(0, count, fetch, 0)
    out[...] = jnp.zeros_like(out)

    def product(k, _):
        slot = plan[0, k + 1] & 31
        tile_of(k, slot).wait()
        rows_of(k, picked.at[0]).wait()
        rows = pl.multiple_of((slot >> 3) * BS, BS)
        out[pl.ds(rows, BS), :] += dot3(tiles[k], data[k])
        return 0

    lax.fori_loop(0, count, product, 0)


def alpha_call(plan, pieces, us2, vs2, picked, own):
    n = own.shape[0] * BS
    return pl.pallas_call(
        alpha_kernel,
        out_shape=jax.ShapeDtypeStruct((n, n), jnp.float32),
        in_specs=[SMEM] + [HBM] * 12,
        out_specs=VMEM,
        scratch_shapes=[
            pltpu.VMEM((2 * SLOTS, BS, n), jnp.float32),
            pltpu.VMEM((2 * SLOTS, BS, BS), jnp.float32),
            pltpu.SemaphoreType.DMA((2 * SLOTS,)),
            pltpu.SemaphoreType.DMA((2 * SLOTS,)),
        ],
        compiler_params=pltpu.CompilerParams(vmem_limit_bytes=18 * MIB),
        cost_estimate=SMALL,
        name="alpha",
    )(plan, *in_hbm(*pieces, us2, vs2, picked, own))


def send_kernel(where, sends, own, out, sem):
    copies = []
    for i in range(SLOTS // 2):
        slot = sends[(where[0] & 1) * (SLOTS // 2) + i]
        copies.append(
            pltpu.make_async_copy(own.at[slot >> 3, slot & 7], out.at[i], sem.at[i])
        )
    for copy in copies:
        copy.start()
    for copy in copies:
        copy.wait()


def send_call(where, sends, own):
    return pl.pallas_call(
        send_kernel,
        out_shape=jax.ShapeDtypeStruct((SLOTS // 2, BS, BS), jnp.float32),
        in_specs=[SMEM] * 2 + [HBM],
        out_specs=VMEM,
        scratch_shapes=[pltpu.SemaphoreType.DMA((SLOTS // 2,))],
        cost_estimate=SMALL,
        name="send",
    )(where, sends, *in_hbm(own))


NEAR = (0, 1, 2, 3, 5, 6, 7)
HOPS = (tuple(range(8)), NEAR, NEAR, (4,))


def beta_kernel(call, where, plan, *refs):
    numbers = HOPS[call]
    pieces, refs = refs[: len(numbers)], refs[len(numbers) :]
    own, got, other, refs = refs[0], refs[1], refs[2], refs[3:]
    before, refs = (refs[0], refs[1:]) if call == 3 else (None, refs)
    out, data, tiles, data_sem, tile_sem, out_sem = refs
    rows, half = data.shape[1], BS
    n = 2 * half
    if call == 3:
        first = pltpu.make_async_copy(before, out.at[:, pl.ds(0, n)], out_sem)
        first.start()
    at = half if call == 2 else 0
    row = min(call, 1) if call < 3 else 2
    core = where[0] & 1
    count = plan[row, 0]

    def columns_of(k, ref, block):
        block = ref.at[pl.ds(at, rows), pl.ds(pl.multiple_of(block * BS, BS), BS)]
        return pltpu.make_async_copy(block, data.at[k], data_sem.at[k])

    def tile_from(k, ref):
        return pltpu.make_async_copy(ref, tiles.at[k], tile_sem.at[k])

    def fetch(k, _):
        word = plan[row, k + 1]
        tile = word & 15
        for number, ref in zip(numbers, pieces):
            pl.when((word >> 6) == number)(
                lambda ref=ref: columns_of(k, ref, (word >> 5) & 1).start()
            )
        if call == 0:
            tile_from(k, own.at[(word >> 4) & 1, tile]).start()
        else:
            start_one_of(
                (got, other), core ^ (tile >> 2), lambda ref: tile_from(k, ref.at[tile & 3])
            )
        return 0

    lax.fori_loop(0, count, fetch, 0)
    if call == 3:
        out[:, n:] = jnp.zeros((half, BS), jnp.float32)
        first.wait()
    else:
        out[...] = jnp.zeros_like(out)

    def product(k, _):
        block = (plan[row, k + 1] >> 4) & 1
        columns_of(k, pieces[0], 0).wait()
        tile_from(k, own.at[0, 0]).wait()
        columns = pl.ds(pl.multiple_of(block * BS, BS), BS)
        if call == 3:
            out[:, n:] += dot3(data[k, :half], tiles[k])
            out[:, columns] += dot3(data[k, half:], tiles[k])
        else:
            out[:, columns] += dot3(data[k], tiles[k])
        return 0

    lax.fori_loop(0, count, product, 0)


def beta_call(call, where, plan, held, own, got, other, before=()):
    n = held[0].shape[0]
    half = n // 2
    rows = half if call in (1, 2) else n
    shape = ((n, n), (half, n), (half, n), (half, n + BS))[call]
    fresh = {1: (3, 5), 3: (4,)}.get(call, ())
    pieces = [held[d] if d in fresh else in_hbm(held[d])[0] for d in HOPS[call]]
    fixed = [*in_hbm(own, got), other] if call == 1 else in_hbm(own, got, other)
    return pl.pallas_call(
        functools.partial(beta_kernel, call),
        out_shape=jax.ShapeDtypeStruct(shape, jnp.float32),
        in_specs=[SMEM] * 2 + [ANY] * (len(pieces) + 3 + len(before)),
        out_specs=VMEM,
        scratch_shapes=[
            pltpu.VMEM((len(pieces), rows, BS), jnp.float32),
            pltpu.VMEM((len(pieces), BS, BS), jnp.float32),
            pltpu.SemaphoreType.DMA((len(pieces),)),
            pltpu.SemaphoreType.DMA((len(pieces),)),
            pltpu.SemaphoreType.DMA,
        ],
        compiler_params=pltpu.CompilerParams(vmem_limit_bytes=12 * MIB),
        cost_estimate=LARGE,
        name=f"beta{call}",
    )(where, plan, *pieces, *fixed, *before)


def last_kernel(where, sends, joined, top, rest, out, top_here, rest_here, sems):
    half, n = top.shape
    copies = [
        pltpu.make_async_copy(source, target, sems.at[i])
        for i, (source, target) in enumerate(((joined, out), (top, top_here), (rest, rest_here)))
    ]
    for copy in copies:
        copy.start()
    block = sends[(where[1] + 4) & 7] >> 3
    for copy in copies:
        copy.wait()
    out[:half] += top_here[...]
    out[half:] += rest_here[:, :n]
    out[:half, pl.ds(pl.multiple_of(block * BS, BS), BS)] += rest_here[:, n:]


def per_device(
    coeffs,
    diag_alpha,
    diag_beta,
    alpha_tiles,
    beta_tiles,
    alpha_source,
    alpha_live,
    beta_source,
    beta_live,
):
    n = coeffs.shape[0]
    where = jnp.stack([lax.axis_index(ALPHA), lax.axis_index(BETA)]).astype(jnp.int32)
    f1, b1 = step(coeffs, "z"), step(coeffs, "z", -1)
    uf, ub = step(coeffs, "x"), step(coeffs, "x", -1)
    v = swap(coeffs, "yhi")
    alpha_plan, beta_plan, picks, sends = pl.pallas_call(
        plan_kernel,
        out_shape=[
            jax.ShapeDtypeStruct((1, 32), jnp.int32),
            jax.ShapeDtypeStruct((3, 32), jnp.int32),
            jax.ShapeDtypeStruct((8,), jnp.int32),
            jax.ShapeDtypeStruct((SLOTS,), jnp.int32),
        ],
        in_specs=[SMEM] * 5,
        out_specs=[SMEM] * 4,
        name="plan",
    )(where, alpha_source, alpha_live, beta_source, beta_live)
    tiles = send_call(where, sends, beta_tiles)
    f1, tiles = lax.optimization_barrier((f1, tiles))
    f2, b2 = step(f1, "z"), step(b1, "z", -1)
    uf, ub, v = lax.optimization_barrier((uf, ub, v, f1, b1))[:3]
    vf, vb = step(v, "x"), step(v, "x", -1)
    got = swap(after(tiles, v), "ylo")
    f3, b3 = step(f2, "z"), step(b2, "z", -1)
    vf, vb, got, uf = lax.optimization_barrier((vf, vb, got, uf, b2))[:4]
    u2, v2 = step(uf, "x"), step(vf, "x")
    other = swap(got, "core")
    picked = pick_call(picks, [coeffs, uf, ub, v, vf, vb])
    f3, b3, picked = lax.optimization_barrier((f3, b3, picked))
    picked = swap(picked, "core")
    held = [coeffs, f1, f2, f3, step(f3, "z"), b3, b2, b1]
    top = beta_call(1, where, beta_plan, held, beta_tiles, got, other)
    top_other = swap(top, "ylo")
    bottom = beta_call(2, where, beta_plan, held, after(beta_tiles, top), got, other)
    pieces = [coeffs, uf, u2, ub, v, vf, v2, vb]
    us2, vs2 = swap(after(u2, top), "core"), swap(after(v2, top), "core")
    rest = beta_call(3, where, beta_plan, held, beta_tiles, got, other, [bottom])
    rest_other = swap(rest, "ylo")
    alpha = alpha_call(alpha_plan, pieces, us2, vs2, picked, after(alpha_tiles, rest))
    beta_own = beta_call(0, where, beta_plan, held, after(beta_tiles, rest), got, other)
    joined = (diag_alpha[:, None] + diag_beta[None, :]) * coeffs + alpha + beta_own
    return pl.pallas_call(
        last_kernel,
        out_shape=jax.ShapeDtypeStruct((n, n), jnp.float32),
        in_specs=[SMEM] * 2 + [ANY] * 3,
        out_specs=VMEM,
        scratch_shapes=[
            pltpu.VMEM(top_other.shape, jnp.float32),
            pltpu.VMEM(rest_other.shape, jnp.float32),
            pltpu.SemaphoreType.DMA((3,)),
        ],
        compiler_params=pltpu.CompilerParams(vmem_limit_bytes=8 * MIB),
        cost_estimate=SMALL,
        name="last",
    )(where, sends, lax.optimization_barrier(joined), top_other, rest_other)


def solution(mesh):
    parts = Mesh(mesh.devices.reshape(SIZES), AXES)
    return jax.shard_map(
        per_device,
        mesh=parts,
        in_specs=(
            P(ALPHA, BETA),
            P(ALPHA),
            P(BETA),
            P(ALPHA, None, None, None),
            P(BETA, None, None, None),
            P(),
            P(),
            P(),
            P(),
        ),
        out_specs=P(ALPHA, BETA),
        check_vma=False,
    )
```
